32 devices in a mesh: dp: 16 (over z, y, core), rank: 2 (over x).
Axes of the slice: x: 2, y: 2, z: 4, core: 2. Of those that a mesh axis runs over, the one named last changes fastest.
Arguments:
- tokens: bfloat16 [2, 32, 256, 768], P(None, ('dp', 'rank')), may hold values from -6 to 6
- cotangent: bfloat16 [2, 32, 256, 768], P(None, ('dp', 'rank')), may hold values from -6 to 6
- seg_lengths: int32 [2, 32, 4], P(None, ('dp', 'rank')), may hold values from 1 to 128, 256 in all within a row
- attn_weights: bfloat16 [3, 768, 768], P(None, ('dp', 'rank')), may hold values from -0.21875 to 0.21875
- out_weight: bfloat16 [768, 768], P(('dp', 'rank')), may hold values from -1.75 to 1.75
- ffn_in: bfloat16 [768, 3072], P(None, ('dp', 'rank')), may hold values from -0.21875 to 0.21875
- ffn_out: bfloat16 [3072, 768], P(('dp', 'rank')), may hold values from -0.109375 to 0.109375
- lin_biases: bfloat16 [4, 768], replicated, may hold values from -1.796875 to 1.796875
- ffn_bias: bfloat16 [3072], replicated, may hold values from -1.796875 to 1.796875
- norm_gains: bfloat16 [2, 768], replicated, may hold values from 0.5 to 1.5
- norm_biases: bfloat16 [2, 768], replicated, may hold values from -1.796875 to 1.796875
- shared_down: bfloat16 [1024, 768], P('rank', 'dp'), may hold values from -0.21875 to 0.21875
- shared_up: bfloat16 [768, 1024], P('dp', 'rank'), may hold values from -0.1875 to 0.1875
- scale_d: bfloat16 [2, 1024], P(None, 'rank'), may hold values from -4 to 4
- scale_b: bfloat16 [2, 768], replicated, may hold values from -3 to 3
Outputs:
- output: bfloat16 [2, 32, 256, 768], P(None, ('dp', 'rank'))
- input_grad: bfloat16 [2, 32, 256, 768], P(None, ('dp', 'rank'))
- d_grad: float32 [2, 1024], P(None, 'rank')
- b_grad: float32 [2, 768], replicated
The draws below stay inside these ranges and needn't reach their ends.
Inputs may be any that keep to these rules, and one draw needn't show every extreme that they name: `seg_lengths`: the 4 lengths of each packed row sum to 256, and the longest in each row is exactly 128.
All inputs are finite; a program needn't handle non-finite values.
Results may differ from the reference program's by a relative error of at most 0.02.
Values may be sent and summed in bfloat16 or wider, within the bound.
A program may use at most 128 MiB of HBM per device.

```python
import math
import jax
import jax.numpy as jnp
import numpy as np
from jax import lax

D = 768
HEADS = 12
HEAD = 64
FF = 3072
RANK = 1024
L = 256
SEGS = 4
MICRO = 2
SEQS = 32
ALLTOK = 16384


def shard_levels(key, shape, cuts, low, largest):
    gain = 1.0
    for dim, parts in cuts:
        steps = jax.random.uniform(jax.random.fold_in(jax.random.fold_in(key, 6), dim), (parts,), jnp.float32, low / len(cuts), largest / len(cuts))
        gain = gain * jnp.repeat(jnp.exp(steps), shape[dim] // parts).reshape((-1,) + (1,) * (len(shape) - 1 - dim))
    return gain


def length_profile(count, total, most, lean):
    loads = [(1 << 20) // math.isqrt(standing ** lean) + 1 for standing in range(2, count + 1)]
    spare, holding = total - most - (count - 1), [1] * (count - 1)
    while spare > 0:
        free = [i for i in range(count - 1) if holding[i] < most]
        whole, budget = sum([loads[i] for i in free]), spare
        for i in free:
            addition = min(most - holding[i], max(1, budget * loads[i] // whole), spare)
            holding[i] = holding[i] + addition
            spare = spare - addition
    return np.array([most] + holding)


def uneven_parts(own_key, amount, total, reach, lean):
    if amount == 2:
        one = jax.random.randint(own_key, (), max(1, total - reach), min(reach, total - 1) + 1)
        return jnp.stack([one, total - one])
    sizes = jnp.asarray(length_profile(amount, total, reach, lean), jnp.int32)
    couples = (amount - 1) // 2
    giver, receiver = sizes[1:1 + 2 * couples:2], sizes[2:2 + 2 * couples:2]
    room = jnp.minimum(giver - 1, reach - receiver)
    passed = jax.random.randint(jax.random.fold_in(own_key, 1), (couples,), 0, 1 << 20) % (room + 1)
    sizes = sizes.at[1:1 + 2 * couples:2].set(giver - passed).at[2:2 + 2 * couples:2].set(receiver + passed)
    return sizes[jax.random.permutation(jax.random.fold_in(own_key, 2), amount)]


def gaussian(key, extent, scale, limit, shards=(), held_as=jnp.bfloat16):
    entries = jax.random.normal(key, extent, jnp.float32) * scale
    if len(shards) > 0:
        entries = shard_levels(key, extent, shards, -0.22, 0.18) * entries
    return jnp.clip(entries, min=-limit, max=limit).astype(held_as)


def setup_inputs(seed: int = 0) -> dict:
    key_of = jax.random.split(jax.random.key(seed), 16)
    tokens = gaussian(key_of[0], (MICRO, SEQS, L, D), 1.0, 6.0, ((1, 32),))
    cotangent = gaussian(key_of[1], (MICRO, SEQS, L, D), 1.0, 6.0, ((1, 32),))
    seg_lengths = jax.vmap(lambda own: uneven_parts(own, SEGS, L, L // 2, 2))(jax.random.split(key_of[2], MICRO * SEQS)).reshape((MICRO, SEQS, SEGS)).astype(jnp.int32)
    attn_weights = gaussian(key_of[3], (3, D, D), D ** -0.5, 0.21875, ((1, 32),))
    out_weight = gaussian(key_of[4], (D, D), (D // 64) ** -0.5, 1.75, ((0, 32),))
    ffn_in = gaussian(key_of[5], (D, FF), D ** -0.5, 0.21875, ((1, 32),))
    ffn_out = gaussian(key_of[6], (FF, D), FF ** -0.5, 0.109375, ((0, 32),))
    lin_biases = gaussian(key_of[7], (4, D), 0.3, 1.796875)
    ffn_bias = gaussian(key_of[8], (FF,), 0.3, 1.796875)
    norm_gains = jnp.clip(1.0 + 0.1 * jax.random.normal(key_of[9], (2, D), jnp.float32), 0.5, 1.5).astype(jnp.bfloat16)
    norm_biases = gaussian(key_of[10], (2, D), 0.3, 1.796875)
    shared_down = gaussian(key_of[11], (RANK, D), D ** -0.5, 0.21875, ((0, 2), (1, 16)))
    shared_up = gaussian(key_of[12], (D, RANK), RANK ** -0.5, 0.1875, ((0, 16), (1, 2)))
    scale_d = gaussian(key_of[13], (2, RANK), 1.0, 4.0, ((1, 2),))
    scale_b = gaussian(key_of[14], (2, D), 0.5, 3.0)
    return dict(tokens=tokens, cotangent=cotangent, seg_lengths=seg_lengths, attn_weights=attn_weights, out_weight=out_weight, ffn_in=ffn_in, ffn_out=ffn_out, lin_biases=lin_biases, ffn_bias=ffn_bias, norm_gains=norm_gains, norm_biases=norm_biases, shared_down=shared_down, shared_up=shared_up, scale_d=scale_d, scale_b=scale_b)


@jax.custom_vjp
def low(v):
    return lax.optimization_barrier(v.astype(jnp.bfloat16)).astype(jnp.float32)

@jax.custom_vjp
def low_back(v):
    return v

def low_keep(v):
    return (low(v), None)

def low_pass(kept, grad):
    return (grad,)

def back_keep(v):
    return (v, None)

def back_low(kept, grad):
    return (low(grad),)
low.defvjp(low_keep, low_pass)
low_back.defvjp(back_keep, back_low)
eps_norm = 1e-05
neg_big = -1000000000.0
group_seqs = 8
exact = lax.Precision.HIGHEST

def layer_norm(resid, norm_gain, norm_shift):
    row_mean = lax.optimization_barrier(jnp.mean(resid, axis=-1, keepdims=True))
    centred = resid - row_mean
    variance = lax.optimization_barrier(jnp.mean(centred * centred, axis=-1, keepdims=True))
    return centred * lax.rsqrt(variance + eps_norm) * norm_gain + norm_shift

def segment_match(lengths, length_rows):
    cumulative = jnp.cumsum(lengths, axis=-1)
    places = jnp.arange(length_rows, dtype=jnp.int32)
    labels = lax.optimization_barrier(jnp.sum((places[None, :, None] >= cumulative[:, None, :]).astype(jnp.int32), axis=-1))
    return labels[:, :, None] == labels[:, None, :]

def block_forward(token_rows, scales_d, scales_b, same_segment, frozen):
    w_query, w_key, w_value, w_output, w_inner, w_branch, biases, inner_shift, gain_pair, shift_pair, down_matrix, up_matrix = frozen
    row_count = token_rows.shape[0]
    seq_here = same_segment.shape[0]
    head_shape = (seq_here, L, HEADS, HEAD)
    lowrank = low_back(jnp.dot(token_rows, down_matrix.T, precision=exact))
    scaled_query = low(scales_d[0] * lowrank)
    scaled_value = low(scales_d[1] * lowrank)
    extra_query = low_back(jnp.dot(scaled_query, up_matrix.T, precision=exact))
    extra_value = low_back(jnp.dot(scaled_value, up_matrix.T, precision=exact))
    query_rows = low_back(low(jnp.dot(token_rows, w_query, precision=exact) + biases[0] + scales_b[0] * extra_query))
    key_rows = low_back(low(jnp.dot(token_rows, w_key, precision=exact)))
    value_rows = low_back(low(jnp.dot(token_rows, w_value, precision=exact) + biases[1] + scales_b[1] * extra_value))
    scores = jnp.einsum('sqhe,skhe->shqk', query_rows.reshape(head_shape), key_rows.reshape(head_shape), precision=exact) * HEAD ** (-0.5)
    scores = low_back(jnp.where(same_segment[:, None], scores, neg_big))
    row_peak = lax.optimization_barrier(jnp.max(scores, axis=-1, keepdims=True))
    exponent = jnp.exp(scores - row_peak)
    weights_soft = low(exponent / lax.optimization_barrier(jnp.sum(exponent, axis=-1, keepdims=True)))
    context = jnp.einsum('shqk,skhe->sqhe', weights_soft, value_rows.reshape(head_shape), precision=exact)
    context = low_back(low(context.reshape(row_count, D)))
    attended = low_back(jnp.dot(context, w_output, precision=exact) + biases[2])
    normed_one = layer_norm(token_rows + attended, gain_pair[0], shift_pair[0])
    inner_pre = low_back(jnp.dot(low(normed_one), w_inner, precision=exact) + inner_shift)
    hidden = low_back(low(jax.nn.gelu(inner_pre, approximate=False)))
    branch = low_back(jnp.dot(hidden, w_branch, precision=exact) + biases[3])
    return layer_norm(normed_one + branch, gain_pair[1], shift_pair[1])

def reference(tokens, cotangent, seg_lengths, attn_weights, out_weight, ffn_in, ffn_out, lin_biases, ffn_bias, norm_gains, norm_biases, shared_down, shared_up, scale_d, scale_b):
    float_wide = jnp.float32
    frozen = (attn_weights[0].astype(float_wide), attn_weights[1].astype(float_wide), attn_weights[2].astype(float_wide), out_weight.astype(float_wide), ffn_in.astype(float_wide), ffn_out.astype(float_wide), lin_biases.astype(float_wide), ffn_bias.astype(float_wide), norm_gains.astype(float_wide), norm_biases.astype(float_wide), shared_down.astype(float_wide), shared_up.astype(float_wide))
    groups = MICRO * SEQS // group_seqs
    token_groups = tokens.reshape(groups, group_seqs * L, D)
    cot_groups = cotangent.reshape(groups, group_seqs * L, D)
    length_groups = seg_lengths.reshape(groups, group_seqs, SEGS)
    scales_d = scale_d.astype(float_wide)
    scales_b = scale_b.astype(float_wide)

    def one_group(running, group_item):
        token_rows, cot_rows, lengths = group_item
        same_segment = segment_match(lengths, L)

        def forward(token_in, d_in, b_in):
            return block_forward(token_in, d_in, b_in, same_segment, frozen)
        result, pullback = jax.vjp(forward, token_rows.astype(float_wide), scales_d, scales_b)
        grad_token, grad_d, grad_b = pullback(cot_rows.astype(float_wide))
        return ((running[0] + grad_d, running[1] + grad_b), (result.astype(jnp.bfloat16), grad_token.astype(jnp.bfloat16)))
    initial = (jnp.zeros((2, RANK), float_wide), jnp.zeros((2, D), float_wide))
    (sum_d, sum_b), (outputs, input_grads) = lax.scan(one_group, initial, (token_groups, cot_groups, length_groups))
    factor = 1.0 / math.sqrt(ALLTOK)
    return (outputs.reshape(MICRO, SEQS, L, D), input_grads.reshape(MICRO, SEQS, L, D), sum_d * factor, sum_b * factor)
```

```python
import functools
import math

import jax
import jax.numpy as jnp
from jax import lax
from jax.experimental import pallas as pl
from jax.experimental.pallas import tpu as pltpu
from jax.sharding import PartitionSpec as P

HEAD = 64


eps_norm = 1e-05
neg_big = -1000000000.0


def layer_norm(resid, norm_gain, norm_shift):
    row_mean = jnp.mean(resid, axis=-1, keepdims=True)
    centred = resid - row_mean
    variance = jnp.mean(centred * centred, axis=-1, keepdims=True)
    return centred * lax.rsqrt(variance + eps_norm) * norm_gain + norm_shift


def norm_back(resid, norm_gain, norm_shift, grad_normed):

    def forward_norm(values_in):
        return layer_norm(values_in, norm_gain, norm_shift)

    pullback = jax.vjp(forward_norm, resid)[1]
    return pullback(grad_normed)[0]


def gelu_exact(values_in):
    return jax.nn.gelu(values_in, approximate=False)


def gelu_back(inner_pre, grad_hidden):
    pullback = jax.vjp(gelu_exact, inner_pre)[1]
    return pullback(grad_hidden)[0]


def segment_match(lengths, length_rows):
    cumulative = jnp.cumsum(lengths, axis=-1)
    places = jnp.arange(length_rows, dtype=jnp.int32)
    labels = jnp.sum((places[None, :, None] >= cumulative[:, None, :]).astype(jnp.int32), axis=-1)
    return labels[:, :, None] == labels[:, None, :]


def masked_scores(query_heads, key_heads, same_segment):
    scores = jnp.einsum(
        "sqhe,skhe->shqk", query_heads, key_heads, preferred_element_type=jnp.float32
    ) * HEAD ** (-0.5)
    return jnp.where(same_segment[:, None], scores, neg_big)


def attend(query_heads, key_heads, value_heads, same_segment):
    scores = masked_scores(query_heads, key_heads, same_segment)
    row_peak = jnp.max(scores, axis=-1, keepdims=True)
    exponent = jnp.exp(scores - row_peak)
    row_total = jnp.sum(exponent, axis=-1, keepdims=True)
    weights_soft = (exponent / row_total).astype(jnp.bfloat16)
    context = jnp.einsum(
        "shqk,skhe->sqhe", weights_soft, value_heads, preferred_element_type=jnp.float32
    )
    return (context.astype(jnp.bfloat16), row_peak + jnp.log(row_total))


def attend_back(query_heads, key_heads, value_heads, same_segment, log_total, grad_context):
    scores = masked_scores(query_heads, key_heads, same_segment)
    weights_soft = jnp.exp(scores - log_total)
    grad_values = jnp.einsum(
        "shqk,sqhe->skhe",
        weights_soft.astype(jnp.bfloat16),
        grad_context,
        preferred_element_type=jnp.float32,
    )
    grad_weights = jnp.einsum(
        "sqhe,skhe->shqk", grad_context, value_heads, preferred_element_type=jnp.float32
    )
    inner_sum = jnp.sum(grad_weights * weights_soft, axis=-1, keepdims=True)
    grad_scores = (weights_soft * (grad_weights - inner_sum)).astype(jnp.bfloat16)
    grad_query = jnp.einsum(
        "shqk,skhe->sqhe", grad_scores, key_heads, preferred_element_type=jnp.float32
    ) * HEAD ** (-0.5)
    grad_keys = jnp.einsum(
        "shqk,sqhe->skhe", grad_scores, query_heads, preferred_element_type=jnp.float32
    ) * HEAD ** (-0.5)
    return (grad_query, grad_keys, grad_values)


ALL = slice(None)
MESH_IDS = pl.DeviceIdType.MESH
GROUPS = (((4, 24), 768, 512), ((2, 48), 512, 384), ((96,), 768, 512), ((96,), 768, 512))
SEND_SLOTS = 40
RECV_SLOTS = 25


class Relay:
    def __init__(self, buffers, send_sems, recv_sems):
        self.buffers, self.send_sems, self.recv_sems = buffers, send_sems, recv_sems
        place = lax.axis_index("dp")
        self.x = lax.axis_index("rank")
        self.z, self.y, self.c = place // 4, (place // 2) % 2, place % 2

    def device(self, z, y, c, x):
        return {"dp": z * 4 + y * 2 + c, "rank": x}

    def neighbour(self, c, which):
        z, y, x = self.z, self.y, self.x
        if which == "s":
            return self.device(z, y, 1 - c, x)
        if which == "u":
            return self.device(z + 1, y, c, x)
        if which == "d":
            return self.device(z - 1, y, c, x)
        if (which == "p") == (c == 0):
            return self.device(z, y, c, 1 - x)
        return self.device(z, 1 - y, c, x)

    def view(self, g, c, plane, p, q, part):
        lead, cols, split = GROUPS[g]
        window = {"A": pl.ds(0, split), "B": pl.ds(split, cols - split), "F": pl.ds(0, cols)}[part]
        place = (plane, q, c, p) if c == 0 else (plane, p, c, q)
        return self.buffers[g].at[place + (ALL,) * len(lead) + (window,)]

    def copy(self, g, c, plane, p, q, part, to, send, recv):
        block = self.view(g, c, plane, p, q, part)
        return pltpu.make_async_remote_copy(
            block,
            block,
            self.send_sems.at[g, send],
            self.recv_sems.at[g, recv],
            device_id=self.neighbour(c, to),
            device_id_type=MESH_IDS,
        )


class Steps:
    def __init__(self, relay, g, c):
        self.relay, self.g, self.c = relay, g, c
        self.z = relay.z
        self.p, self.q = (relay.x, relay.y) if c == 0 else (relay.y, relay.x)
        self.sent = []

    def send(self, cond, *where):
        copy = functools.partial(self.relay.copy, self.g, self.c)
        if cond is None:
            copy(*where).start()
        else:

            @pl.when(cond)
            def _():
                copy(*where).start()

        self.sent.append((cond, where))

    def finish(self):
        copy = functools.partial(self.relay.copy, self.g, self.c)
        for cond, where in self.sent:
            if cond is None:
                copy(*where).wait_send()
            else:

                @pl.when(cond)
                def _(where=where):
                    copy(*where).wait_send()

    def got(self, *where):
        self.relay.copy(self.g, self.c, *where).wait_recv()

    def own(self):
        z, p, q = self.z, self.p, self.q
        self.send(None, z, p, q, "A", "p", 0, 0)
        self.send(z < 3, z, p, q, "B", "u", 1, 9 + z)
        self.send(z > 0, z, p, q, "B", "d", 2, 9 + z)
        self.send(None, z, p, q, "B", "p", 3, 13 + z)

    def pair(self):
        z, p, q = self.z, self.p, self.q
        self.got(z, 1 - p, q, "A", "p", 0, 0)
        self.send(z < 3, z, ALL, q, "A", "u", 4, 1 + z)
        self.send(z > 0, z, ALL, q, "A", "d", 5, 1 + z)
        self.send(None, z, ALL, q, "A", "q", 6, 5 + z)

    def line(self, far):
        z, p, q = self.z, self.p, self.q
        for side in (0, 1):
            plane = z - far if side == 0 else z + far
            cond = plane >= 0 if side == 0 else plane <= 3
            more = z < 3 if side == 0 else z > 0
            to = "u" if side == 0 else "d"
            slot = 6 * far + 1 + 3 * side

            @pl.when(cond)
            def _():
                self.got(plane, ALL, q, "A", to, 0, 1 + plane)

            if far < 3:
                self.send(jnp.logical_and(cond, more), plane, ALL, q, "A", to, slot, 1 + plane)
            self.send(cond, plane, ALL, q, "A", "q", slot + 1, 5 + plane)

            @pl.when(cond)
            def _():
                self.got(plane, p, q, "B", to, 0, 9 + plane)

            if far < 3:
                self.send(jnp.logical_and(cond, more), plane, p, q, "B", to, slot + 2, 9 + plane)
            self.send(cond, plane, p, q, "B", "p", 23 + 2 * far + side, 13 + plane)

    def cross(self, turn):
        plane = lax.rem(self.z + turn, 4)
        self.got(plane, 1 - self.p, self.q, "B", "p", 0, 13 + plane)
        self.send(None, plane, ALL, self.q, "B", "q", 31 + turn, 17 + plane)

    def hand_on(self, turn):
        plane = lax.rem(self.z + turn, 4)
        self.got(plane, ALL, 1 - self.q, "A", "q", 0, 5 + plane)
        self.got(plane, ALL, 1 - self.q, "B", "q", 0, 17 + plane)
        self.send(None, plane, ALL, ALL, "F", "s", 35 + turn, 21 + plane)

    def take(self, turn):
        plane = lax.rem(self.z + turn, 4)
        self.relay.copy(self.g, 1 - self.c, plane, ALL, ALL, "F", "s", 0, 21 + plane).wait_recv()


def relay_order(relay, c):
    steps = [Steps(relay, g, c) for g in range(len(GROUPS))]
    order = [steps[0].own, steps[0].pair]
    late = []
    for g, now in enumerate(steps):
        following = steps[g + 1] if g + 1 < len(steps) else None
        if following is not None:
            order.append(following.own)
        order += [functools.partial(now.line, 1), functools.partial(now.cross, 0)] + late[:2]
        order += [functools.partial(now.line, 2)] + late[2:]
        if following is not None:
            order.append(following.pair)
        order += [functools.partial(now.line, 3)]
        order += [functools.partial(now.cross, turn) for turn in (1, 2, 3)]
        late = [functools.partial(now.hand_on, turn) for turn in range(4)]
    order += late
    for now in steps:
        order += [functools.partial(now.take, turn) for turn in range(4)]
    order += [now.finish for now in steps]
    return order


def gather_kernel(*refs):
    count = len(GROUPS)
    pieces, outs, buffers = refs[:count], refs[count : 2 * count], refs[2 * count : 3 * count]
    send_sems, recv_sems, local_sems = refs[3 * count :]
    relay = Relay(buffers, send_sems, recv_sems)
    z, y, c, x = relay.z, relay.y, relay.c, relay.x
    mine = [
        pltpu.make_async_copy(pieces[g], buffers[g].at[z, y, c, x], local_sems.at[g])
        for g in range(count)
    ]
    for copy in mine:
        copy.start()
    barrier = pltpu.get_barrier_semaphore()

    def greet(device):
        pl.semaphore_signal(barrier, 1, device_id=device, device_id_type=MESH_IDS)

    greet(relay.device(z, y, 1 - c, x))
    greet(relay.device(z, y, c, 1 - x))
    greet(relay.device(z, 1 - y, c, x))

    @pl.when(z < 3)
    def _():
        greet(relay.device(z + 1, y, c, x))

    @pl.when(z > 0)
    def _():
        greet(relay.device(z - 1, y, c, x))

    pl.semaphore_wait(barrier, 3 + jnp.where(z < 3, 1, 0) + jnp.where(z > 0, 1, 0))
    for copy in mine:
        copy.wait()
    for core in (0, 1):

        @pl.when(c == core)
        def _():
            for step in relay_order(relay, core):
                step()

    back = [pltpu.make_async_copy(buffers[g], outs[g], local_sems.at[g]) for g in range(count)]
    for copy in back:
        copy.start()
    for copy in back:
        copy.wait()


def gather_all(pieces):
    shapes = [(4, 2, 2, 2) + lead + (cols,) for lead, cols, _ in GROUPS]
    count = len(GROUPS)
    return pl.pallas_call(
        gather_kernel,
        out_shape=[jax.ShapeDtypeStruct(shape, jnp.bfloat16) for shape in shapes],
        in_specs=[pl.BlockSpec(memory_space=pl.ANY)] * count,
        out_specs=[pl.BlockSpec(memory_space=pl.ANY)] * count,
        scratch_shapes=[pltpu.VMEM(shape, jnp.bfloat16) for shape in shapes]
        + [
            pltpu.SemaphoreType.DMA((count, SEND_SLOTS)),
            pltpu.SemaphoreType.DMA((count, RECV_SLOTS)),
            pltpu.SemaphoreType.DMA((count,)),
        ],
        compiler_params=pltpu.CompilerParams(
            collective_id=0, has_side_effects=True, vmem_limit_bytes=48 << 20
        ),
    )(*pieces)


def gather_weights(attn_weights, out_weight, ffn_in, ffn_out, shared_down, shared_up):
    if lax.axis_size("dp") == 16 and lax.axis_size("rank") == 2:
        pieces = (
            jnp.concatenate([attn_weights, out_weight[None]]),
            jnp.stack([shared_down.T, shared_up]),
            ffn_in.T,
            ffn_out,
        )
        square, vera, inner_t, branch = gather_all(pieces)
        square = square.reshape(32, 4, 24, 768).transpose(1, 0, 2, 3).reshape(4, 768, 768)
        vera = vera.reshape(16, 2, 2, 48, 512).transpose(2, 0, 3, 1, 4).reshape(2, 768, 1024)
        return (square[:3], square[3], inner_t.reshape(3072, 768).T, branch.reshape(3072, 768), vera[0].T, vera[1])
    down_local = lax.all_gather(shared_down, "dp", axis=1, tiled=True)
    up_local = lax.all_gather(shared_up, "dp", axis=0, tiled=True)
    return (
        lax.all_gather(attn_weights, ("dp", "rank"), axis=1, tiled=True),
        lax.all_gather(out_weight, ("dp", "rank"), axis=0, tiled=True),
        lax.all_gather(ffn_in, ("dp", "rank"), axis=1, tiled=True),
        lax.all_gather(ffn_out, ("dp", "rank"), axis=0, tiled=True),
        lax.all_gather(down_local, "rank", axis=0, tiled=True),
        lax.all_gather(up_local, "rank", axis=1, tiled=True),
    )


def per_device(
    tokens,
    cotangent,
    seg_lengths,
    attn_weights,
    out_weight,
    ffn_in,
    ffn_out,
    lin_biases,
    ffn_bias,
    norm_gains,
    norm_biases,
    shared_down,
    shared_up,
    scale_d,
    scale_b,
):
    micro_count, seq_count, length_rows, model_width = tokens.shape
    head_count = model_width // HEAD
    out_shape = tokens.shape
    seq_count = micro_count * seq_count
    row_count = seq_count * length_rows
    head_shape = (seq_count, length_rows, head_count, HEAD)
    float_wide = jnp.float32
    narrow = jnp.bfloat16
    attn_full, output_full, inner_full, branch_full, down_use, up_use = gather_weights(
        attn_weights, out_weight, ffn_in, ffn_out, shared_down, shared_up
    )
    scales_use = lax.all_gather(scale_d, "rank", axis=1, tiled=True)
    rank_cols = scales_use.shape[1]
    sum_d = jnp.zeros((2, rank_cols), float_wide)
    sum_b = jnp.zeros((2, model_width), float_wide)
    outputs = []
    input_grads = []
    for micro_step in range(1):
        token_rows = tokens.reshape(row_count, model_width)
        same_segment = segment_match(seg_lengths.reshape(seq_count, -1), length_rows)
        lowrank = jnp.einsum("rd,kd->rk", token_rows, down_use, preferred_element_type=float_wide)
        scaled = (scales_use[:, None, :] * lowrank[None]).astype(narrow)
        adapted = jnp.concatenate(
            [
                jnp.einsum("rk,dk->rd", scaled[0], up_use, preferred_element_type=float_wide),
                jnp.einsum("rk,dk->rd", scaled[1], up_use, preferred_element_type=float_wide),
            ],
            axis=1,
        )
        extra_query = adapted[:, :model_width]
        extra_value = adapted[:, model_width:]
        query_rows = (
            jnp.dot(token_rows, attn_full[0], preferred_element_type=float_wide)
            + lin_biases[0]
            + scale_b[0] * extra_query
        ).astype(narrow)
        key_rows = jnp.dot(token_rows, attn_full[1], preferred_element_type=float_wide).astype(
            narrow
        )
        value_rows = (
            jnp.dot(token_rows, attn_full[2], preferred_element_type=float_wide)
            + lin_biases[1]
            + scale_b[1] * extra_value
        ).astype(narrow)
        query_heads = query_rows.reshape(head_shape)
        key_heads = key_rows.reshape(head_shape)
        value_heads = value_rows.reshape(head_shape)
        context, log_total = attend(query_heads, key_heads, value_heads, same_segment)
        attended = (
            jnp.dot(
                context.reshape(row_count, model_width),
                output_full,
                preferred_element_type=float_wide,
            )
            + lin_biases[2]
        )
        resid_one = token_rows.astype(float_wide) + attended
        normed_one = layer_norm(resid_one, norm_gains[0], norm_biases[0])
        inner_pre = (
            jnp.dot(normed_one.astype(narrow), inner_full, preferred_element_type=float_wide)
            + ffn_bias
        )
        hidden = gelu_exact(inner_pre).astype(narrow)
        branch = jnp.dot(hidden, branch_full, preferred_element_type=float_wide) + lin_biases[3]
        resid_two = normed_one + branch
        outputs.append(
            layer_norm(resid_two, norm_gains[1], norm_biases[1])
            .astype(narrow)
            .reshape(out_shape)
        )
        grad_out = cotangent.reshape(row_count, model_width).astype(float_wide)
        grad_two = norm_back(resid_two, norm_gains[1], norm_biases[1], grad_out)
        grad_hidden = jnp.einsum(
            "rd,fd->rf", grad_two.astype(narrow), branch_full, preferred_element_type=float_wide
        ).astype(narrow)
        grad_inner = gelu_back(inner_pre, grad_hidden.astype(float_wide)).astype(narrow)
        grad_normed = grad_two + jnp.einsum(
            "rf,df->rd", grad_inner, inner_full, preferred_element_type=float_wide
        )
        grad_one = norm_back(resid_one, norm_gains[0], norm_biases[0], grad_normed)
        grad_attended = grad_one.astype(narrow)
        grad_context = jnp.einsum(
            "ro,io->ri", grad_attended, output_full, preferred_element_type=float_wide
        ).astype(narrow)
        grad_query, grad_keys, grad_values = attend_back(
            query_heads,
            key_heads,
            value_heads,
            same_segment,
            log_total,
            grad_context.reshape(head_shape),
        )
        query_grad = grad_query.reshape(row_count, model_width).astype(narrow)
        key_grad = grad_keys.reshape(row_count, model_width).astype(narrow)
        value_grad = grad_values.reshape(row_count, model_width).astype(narrow)
        grad_input = grad_one + jnp.einsum(
            "ro,io->ri", query_grad, attn_full[0], preferred_element_type=float_wide
        )
        grad_input = grad_input + jnp.einsum(
            "ro,io->ri", key_grad, attn_full[1], preferred_element_type=float_wide
        )
        grad_input = grad_input + jnp.einsum(
            "ro,io->ri", value_grad, attn_full[2], preferred_element_type=float_wide
        )
        query_grad_wide = query_grad.astype(float_wide)
        value_grad_wide = value_grad.astype(float_wide)
        sum_b = sum_b + jnp.stack(
            [
                jnp.sum(extra_query * query_grad_wide, axis=0),
                jnp.sum(extra_value * value_grad_wide, axis=0),
            ]
        )
        grad_extra = jnp.concatenate(
            [
                (scale_b[0] * query_grad_wide).astype(narrow),
                (scale_b[1] * value_grad_wide).astype(narrow),
            ],
            axis=1,
        )
        grad_scaled = jnp.concatenate(
            [
                jnp.dot(grad_extra[:, :model_width], up_use, preferred_element_type=float_wide),
                jnp.dot(grad_extra[:, model_width:], up_use, preferred_element_type=float_wide),
            ],
            axis=1,
        )
        grad_scaled_query = grad_scaled[:, :rank_cols]
        grad_scaled_value = grad_scaled[:, rank_cols:]
        sum_d = sum_d + jnp.stack(
            [
                jnp.sum(lowrank * grad_scaled_query, axis=0),
                jnp.sum(lowrank * grad_scaled_value, axis=0),
            ]
        )
        grad_lowrank = (
            scales_use[0] * grad_scaled_query + scales_use[1] * grad_scaled_value
        ).astype(narrow)
        grad_from_adapter = jnp.dot(grad_lowrank, down_use, preferred_element_type=float_wide)
        input_grads.append(
            (grad_input + grad_from_adapter)
            .astype(narrow)
            .reshape(out_shape)
        )
    grad_scale = 1.0 / math.sqrt(
        row_count * lax.axis_size("dp") * lax.axis_size("rank")
    )
    total_d, total_b = lax.psum((sum_d, sum_b), ("dp", "rank"))
    local_cols = scale_d.shape[1]
    total_d = lax.dynamic_slice_in_dim(total_d, lax.axis_index("rank") * local_cols, local_cols, 1)
    return (outputs[0], input_grads[0], total_d * grad_scale, total_b * grad_scale)


def solution(mesh):
    return jax.shard_map(
        per_device,
        mesh=mesh,
        in_specs=(
            P(None, ("dp", "rank"), None, None),
            P(None, ("dp", "rank"), None, None),
            P(None, ("dp", "rank"), None),
            P(None, ("dp", "rank"), None),
            P(("dp", "rank"), None),
            P(None, ("dp", "rank")),
            P(("dp", "rank"), None),
            P(),
            P(),
            P(),
            P(),
            P("rank", "dp"),
            P("dp", "rank"),
            P(None, "rank"),
            P(),
        ),
        out_specs=(
            P(None, ("dp", "rank"), None, None),
            P(None, ("dp", "rank"), None, None),
            P(None, "rank"),
            P(),
        ),
        check_vma=False,
    )
```

```python
import functools
import math

import jax
import jax.numpy as jnp
from jax import lax
from jax.experimental import pallas as pl
from jax.experimental.pallas import tpu as pltpu
from jax.sharding import PartitionSpec as P

HEAD = 64


eps_norm = 1e-05
neg_big = -1000000000.0


def layer_norm(resid, norm_gain, norm_shift):
    row_mean = jnp.mean(resid, axis=-1, keepdims=True)
    centred = resid - row_mean
    variance = jnp.mean(centred * centred, axis=-1, keepdims=True)
    return centred * lax.rsqrt(variance + eps_norm) * norm_gain + norm_shift


def norm_back(resid, norm_gain, norm_shift, grad_normed):

    def forward_norm(values_in):
        return layer_norm(values_in, norm_gain, norm_shift)

    pullback = jax.vjp(forward_norm, resid)[1]
    return pullback(grad_normed)[0]


def gelu_exact(values_in):
    return jax.nn.gelu(values_in, approximate=False)


def gelu_back(inner_pre, grad_hidden):
    pullback = jax.vjp(gelu_exact, inner_pre)[1]
    return pullback(grad_hidden)[0]


def segment_match(lengths, length_rows):
    cumulative = jnp.cumsum(lengths, axis=-1)
    places = jnp.arange(length_rows, dtype=jnp.int32)
    labels = jnp.sum((places[None, :, None] >= cumulative[:, None, :]).astype(jnp.int32), axis=-1)
    return labels[:, :, None] == labels[:, None, :]


def masked_scores(query_heads, key_heads, same_segment):
    scores = jnp.einsum(
        "sqhe,skhe->shqk", query_heads, key_heads, preferred_element_type=jnp.float32
    ) * HEAD ** (-0.5)
    return jnp.where(same_segment[:, None], scores, neg_big)


def attend(query_heads, key_heads, value_heads, same_segment):
    scores = masked_scores(query_heads, key_heads, same_segment)
    row_peak = jnp.max(scores, axis=-1, keepdims=True)
    exponent = jnp.exp(scores - row_peak)
    row_total = jnp.sum(exponent, axis=-1, keepdims=True)
    weights_soft = (exponent / row_total).astype(jnp.bfloat16)
    context = jnp.einsum(
        "shqk,skhe->sqhe", weights_soft, value_heads, preferred_element_type=jnp.float32
    )
    return (context.astype(jnp.bfloat16), row_peak + jnp.log(row_total))


def attend_back(query_heads, key_heads, value_heads, same_segment, log_total, grad_context):
    scores = masked_scores(query_heads, key_heads, same_segment)
    weights_soft = jnp.exp(scores - log_total)
    grad_values = jnp.einsum(
        "shqk,sqhe->skhe",
        weights_soft.astype(jnp.bfloat16),
        grad_context,
        preferred_element_type=jnp.float32,
    )
    grad_weights = jnp.einsum(
        "sqhe,skhe->shqk", grad_context, value_heads, preferred_element_type=jnp.float32
    )
    inner_sum = jnp.sum(grad_weights * weights_soft, axis=-1, keepdims=True)
    grad_scores = (weights_soft * (grad_weights - inner_sum)).astype(jnp.bfloat16)
    grad_query = jnp.einsum(
        "shqk,skhe->sqhe", grad_scores, key_heads, preferred_element_type=jnp.float32
    ) * HEAD ** (-0.5)
    grad_keys = jnp.einsum(
        "shqk,sqhe->skhe", grad_scores, query_heads, preferred_element_type=jnp.float32
    ) * HEAD ** (-0.5)
    return (grad_query, grad_keys, grad_values)


ALL = slice(None)
MESH_IDS = pl.DeviceIdType.MESH
WIDE = jnp.float32
NARROW = jnp.bfloat16
GROUPS = (((2, 48), 512, 384), ((4, 24), 768, 512), ((96,), 768, 512), ((96,), 768, 512))
VERA, SQUARE, INNER, BRANCH = range(4)
SEND_SLOTS = 39
RECV_SLOTS = 25
LINE = 4
PLANE = 8


class Relay:
    def __init__(self, buffers, send_sems, recv_sems):
        self.buffers, self.send_sems, self.recv_sems = buffers, send_sems, recv_sems
        place = lax.axis_index("dp")
        self.x = lax.axis_index("rank")
        self.z, self.y, self.c = place // 4, (place // 2) % 2, place % 2

    def device(self, z, y, c, x):
        return {"dp": z * 4 + y * 2 + c, "rank": x}

    def neighbour(self, c, which):
        z, y, x = self.z, self.y, self.x
        if which == "s":
            return self.device(z, y, 1 - c, x)
        if which == "u":
            return self.device(z + 1, y, c, x)
        if which == "d":
            return self.device(z - 1, y, c, x)
        if (which == "p") == (c == 0):
            return self.device(z, y, c, 1 - x)
        return self.device(z, 1 - y, c, x)

    def view(self, g, c, plane, p, q, part):
        lead, cols, split = GROUPS[g]
        window = {"A": pl.ds(0, split), "B": pl.ds(split, cols - split), "F": pl.ds(0, cols)}[part]
        place = (plane, q, c, p) if c == 0 else (plane, p, c, q)
        return self.buffers[g].at[place + (ALL,) * len(lead) + (window,)]

    def copy(self, g, c, plane, p, q, part, to, send, recv):
        block = self.view(g, c, plane, p, q, part)
        return pltpu.make_async_remote_copy(
            block,
            block,
            self.send_sems.at[g, send],
            self.recv_sems.at[g, recv],
            device_id=self.neighbour(c, to),
            device_id_type=MESH_IDS,
        )


class Steps:
    def __init__(self, relay, g, c):
        self.relay, self.g, self.c = relay, g, c
        self.z = relay.z
        self.p, self.q = (relay.x, relay.y) if c == 0 else (relay.y, relay.x)
        self.closing = False

    def send(self, cond, *where):
        def act():
            copy = self.relay.copy(self.g, self.c, *where)
            if self.closing:
                copy.wait_send()
            else:
                copy.start()

        if cond is None:
            act()
        else:
            pl.when(cond)(act)

    def finish(self):
        self.closing = True
        self.own()
        self.pair()
        for far in (1, 2, 3):
            self.line(far)
        for turn in range(4):
            self.cross(turn)
            self.hand_on(turn)

    def got(self, *where):
        if not self.closing:
            self.relay.copy(self.g, self.c, *where).wait_recv()

    def own(self):
        z, p, q = self.z, self.p, self.q
        self.send(None, z, p, q, "A", "p", 0, 0)
        self.send(z < 3, z, p, q, "B", "u", 1, 9 + z)
        self.send(z > 0, z, p, q, "B", "d", 2, 9 + z)
        self.send(None, z, p, q, "B", "p", 3, 13 + z)

    def pair(self):
        z, p, q = self.z, self.p, self.q
        self.got(z, 1 - p, q, "A", "p", 0, 0)
        self.send(z < 3, z, ALL, q, "A", "u", 4, 1 + z)
        self.send(z > 0, z, ALL, q, "A", "d", 5, 1 + z)
        self.send(None, z, ALL, q, "A", "q", 6, 5 + z)

    def line(self, far):
        z, p, q = self.z, self.p, self.q
        for side in (0, 1):
            plane = z - far if side == 0 else z + far
            cond = plane >= 0 if side == 0 else plane <= 3
            more = z < 3 if side == 0 else z > 0
            to = "u" if side == 0 else "d"
            slot = 6 * far + 1 + 3 * side

            @pl.when(cond)
            def _():
                self.got(plane, ALL, q, "A", to, 0, 1 + plane)

            if far < 3:
                self.send(jnp.logical_and(cond, more), plane, ALL, q, "A", to, slot, 1 + plane)
            self.send(cond, plane, ALL, q, "A", "q", slot + 1, 5 + plane)

            @pl.when(cond)
            def _():
                self.got(plane, p, q, "B", to, 0, 9 + plane)

            if far < 3:
                self.send(jnp.logical_and(cond, more), plane, p, q, "B", to, slot + 2, 9 + plane)
            self.send(cond, plane, p, q, "B", "p", 23 + 2 * far + side, 13 + plane)

    def cross(self, turn):
        plane = lax.rem(self.z + turn, 4)
        self.got(plane, 1 - self.p, self.q, "B", "p", 0, 13 + plane)
        self.send(None, plane, ALL, self.q, "B", "q", 31 + turn, 17 + plane)

    def hand_on(self, turn):
        plane = lax.rem(self.z + turn, 4)
        self.got(plane, ALL, 1 - self.q, "A", "q", 0, 5 + plane)
        self.got(plane, ALL, 1 - self.q, "B", "q", 0, 17 + plane)
        self.send(None, plane, ALL, ALL, "F", "s", 35 + turn, 21 + plane)

    def take(self, turn):
        plane = lax.rem(self.z + turn, 4)
        self.relay.copy(self.g, 1 - self.c, plane, ALL, ALL, "F", "s", 0, 21 + plane).wait_recv()


class Gather:
    def __init__(self, relay):
        self.relay = relay
        self.steps = [[Steps(relay, g, c) for g in range(len(GROUPS))] for c in (0, 1)]

    def __call__(self, name, g, *where):
        for core in (0, 1):

            @pl.when(self.relay.c == core)
            def _():
                getattr(self.steps[core][g], name)(*where)


def dot_nn(left, right):
    return jnp.dot(left, right, preferred_element_type=WIDE)


def dot_nt(left, right):
    return lax.dot_general(left, right, (((1,), (1,)), ((), ())), preferred_element_type=WIDE)


def dot_tn(left, right):
    return lax.dot_general(left, right, (((0,), (0,)), ((), ())), preferred_element_type=WIDE)


def standardise(resid):
    centred = resid - jnp.mean(resid, axis=-1, keepdims=True)
    inverse = lax.rsqrt(jnp.mean(centred * centred, axis=-1, keepdims=True) + eps_norm)
    return centred * inverse, inverse


def standardise_back(normed, inverse, grad):
    along = jnp.mean(grad * normed, axis=-1, keepdims=True)
    return inverse * (grad - jnp.mean(grad, axis=-1, keepdims=True) - normed * along)


def layer_kernel(grad_scale, *refs):
    (
        tokens,
        cotangent,
        seg_lengths,
        attn_piece,
        out_piece,
        inner_piece,
        branch_piece,
        lin_biases,
        ffn_bias,
        norm_gains,
        norm_biases,
        down_piece,
        up_piece,
        scale_d,
        scale_b,
        output,
        input_grad,
        d_grad,
        b_grad,
        vera,
        square,
        inner_t,
        branch_w,
        scales,
        same,
        low,
        extra_q,
        extra_v,
        query,
        key,
        value,
        probs,
        context,
        normed_one,
        inverse_one,
        resid,
        narrow_one,
        hidden,
        slope,
        out_stage,
        grad_stage,
        plane_sums,
        line_sums,
        bias_row,
        send_sems,
        recv_sems,
        local_sems,
        sum_sems,
    ) = refs
    relay = Relay((vera, square, inner_t, branch_w), send_sems, recv_sems)
    gather = Gather(relay)
    z, y, c, x = relay.z, relay.y, relay.c, relay.x
    spot = c * 4 + y * 2 + x

    def in_plane(turn):
        other = lax.rem(spot + turn, PLANE)
        return other, relay.device(z, (other // 2) % 2, other // 4, other % 2)

    def in_line(turn):
        other = lax.rem(z + turn, LINE)
        return other, relay.device(other, y, c, x)

    mine = [
        pltpu.make_async_copy(up_piece, vera.at[z, y, c, x, 1], local_sems.at[0]),
        pltpu.make_async_copy(attn_piece, square.at[z, y, c, x, pl.ds(0, 3)], local_sems.at[1]),
        pltpu.make_async_copy(out_piece, square.at[z, y, c, x, 3], local_sems.at[2]),
        pltpu.make_async_copy(branch_piece, branch_w.at[z, y, c, x], local_sems.at[3]),
        pltpu.make_async_copy(scale_d, scales.at[x], local_sems.at[4]),
        pltpu.make_async_copy(inner_piece, inner_t.at[z, y, c, x], local_sems.at[5]),
        pltpu.make_async_copy(down_piece, vera.at[z, y, c, x, 0], local_sems.at[6]),
    ]
    for copy in mine:
        copy.start()
    barrier = pltpu.get_barrier_semaphore()
    for turn in range(1, PLANE):
        pl.semaphore_signal(barrier, 1, device_id=in_plane(turn)[1], device_id_type=MESH_IDS)
    for turn in range(1, LINE):
        pl.semaphore_signal(barrier, 1, device_id=in_line(turn)[1], device_id_type=MESH_IDS)
    for copy in mine:
        copy.wait()
    pl.semaphore_wait(barrier, PLANE - 1 + LINE - 1)

    scale_copy = pltpu.make_async_remote_copy(
        scales.at[x],
        scales.at[x],
        sum_sems.at[0],
        sum_sems.at[1],
        device_id=relay.device(z, y, c, 1 - x),
        device_id_type=MESH_IDS,
    )
    gather("own", VERA)
    scale_copy.start()
    for seq in range(2):
        row_place = lax.broadcasted_iota(jnp.int32, (256, 256), 0)
        col_place = lax.broadcasted_iota(jnp.int32, (256, 256), 1)
        row_label = jnp.zeros((256, 256), jnp.int32)
        col_label = jnp.zeros((256, 256), jnp.int32)
        end = jnp.int32(0)
        for k in range(seg_lengths.shape[1]):
            end = end + seg_lengths[seq, k]
            row_label = row_label + (row_place >= end).astype(jnp.int32)
            col_label = col_label + (col_place >= end).astype(jnp.int32)
        same[seq] = jnp.where(row_label == col_label, 0.0, neg_big)

    bias_row[...] = ffn_bias[...].astype(WIDE).reshape(1, -1)

    def row(ref, k):
        return ref[k : k + 1, :].astype(WIDE)

    def rows_of(i):
        return pl.ds(pl.multiple_of(i * 256, 256), 256)

    def down_t(h):
        return vera[:, :, :, h, 0].reshape(768, 512)

    def up(h):
        return vera[:, :, :, h, 1].reshape(768, 512)

    def weight(k):
        return square[:, :, :, :, k].reshape(768, 768)

    def steps_at(i, relays):
        for k, steps in relays.items():

            @pl.when(i == k)
            def _():
                for step in steps:
                    gather(*step)

    def adapters(i):
        rows = rows_of(i)
        token_rows = tokens[rows, :]
        parts_q, parts_v = [], []
        for h in range(2):
            lowrank = dot_nn(token_rows, down_t(h))
            low[rows, h * 512 : (h + 1) * 512] = lowrank
            parts_q.append(dot_nt((scales[h, 0:1, :].astype(WIDE) * lowrank).astype(NARROW), up(h)))
            parts_v.append(dot_nt((scales[h, 1:2, :].astype(WIDE) * lowrank).astype(NARROW), up(h)))
        extra_q[rows, :] = parts_q[0] + parts_q[1]
        extra_v[rows, :] = parts_v[0] + parts_v[1]

    def project_key():
        key[...] = dot_nn(tokens[...], weight(1)).astype(NARROW)

    def project_query():
        total = dot_nn(tokens[...], weight(0)) + row(lin_biases, 0) + row(scale_b, 0) * extra_q[...]
        query[...] = (total * HEAD ** (-0.5)).astype(NARROW)

    def project_value():
        total = dot_nn(tokens[...], weight(2)) + row(lin_biases, 1) + row(scale_b, 1) * extra_v[...]
        value[...] = total.astype(NARROW)

    def head_cols(j):
        return pl.ds(pl.multiple_of(j * 128, 128), 128)

    first_half = lax.broadcasted_iota(jnp.int32, (256, 128), 1) < HEAD

    def attend_pair(it):
        seq, j = it // 6, lax.rem(it, 6)
        rows, cols = rows_of(seq), head_cols(j)
        q_pair, k_pair, v_pair = query[rows, cols], key[rows, cols], value[rows, cols]
        zero = jnp.zeros_like(q_pair)
        parts = []
        for half in range(2):
            mine_here = first_half if half == 0 else jnp.logical_not(first_half)
            scores = dot_nt(jnp.where(mine_here, q_pair, zero), k_pair) + same[seq]
            peak = jnp.max(scores, axis=-1, keepdims=True)
            exponent = jnp.exp(scores - peak)
            total = jnp.sum(exponent, axis=-1, keepdims=True)
            soft = (exponent * (1.0 / total)).astype(NARROW)
            probs[it * 2 + half] = soft
            parts.append(dot_nn(soft, v_pair))
        context[rows, cols] = jnp.where(first_half, parts[0], parts[1]).astype(NARROW)

    def close_attention(i):
        rows = rows_of(i)
        attended = dot_nn(context[rows, :], weight(3)) + row(lin_biases, 2)
        normed, inverse = standardise(tokens[rows, :].astype(WIDE) + attended)
        normed_one[rows, :] = normed
        inverse_one[rows, :] = inverse
        scaled = normed * row(norm_gains, 0) + row(norm_biases, 0)
        narrow_one[rows, :] = scaled.astype(NARROW)
        resid[rows, :] = scaled + row(lin_biases, 3)

    def hidden_cols(plane):
        return pl.ds(pl.multiple_of(plane * 768, 768), 768)

    def inner_block(it):
        turn, i = it // 2, lax.rem(it, 2)
        plane = lax.rem(z + turn, 4)
        rows, cols = rows_of(i), hidden_cols(plane)
        block = dot_nt(narrow_one[rows, :], inner_t[plane].reshape(768, 768))
        block = block + bias_row[0:1, cols]
        below = 0.5 + 0.5 * lax.erf(block * 0.7071067811865476)
        hidden[rows, cols] = (block * below).astype(NARROW)
        slope[rows, cols] = (below + block * jnp.exp(-0.5 * block * block) * 0.3989422804014327).astype(NARROW)

    def branch_block(turn):
        plane = lax.rem(z + turn, 4)
        resid[...] += dot_nn(hidden[:, hidden_cols(plane)], branch_w[plane].reshape(768, 768))

    gather("pair", VERA)
    gather("own", SQUARE)
    gather("line", VERA, 1)
    gather("cross", VERA, 0)
    gather("line", VERA, 2)
    gather("pair", SQUARE)
    gather("line", VERA, 3)
    for turn in (1, 2, 3):
        gather("cross", VERA, turn)
    gather("own", INNER)
    gather("line", SQUARE, 1)
    gather("cross", SQUARE, 0)
    gather("hand_on", VERA, 0)
    gather("hand_on", VERA, 1)
    gather("line", SQUARE, 2)
    gather("hand_on", VERA, 2)
    gather("hand_on", VERA, 3)
    gather("pair", INNER)
    gather("line", SQUARE, 3)
    for turn in range(4):
        gather("take", VERA, turn)
    scale_copy.wait()

    @pl.loop(0, 2)
    def _(i):
        steps_at(i, {1: [("cross", SQUARE, 1), ("cross", SQUARE, 2)]})
        adapters(i)

    gather("cross", SQUARE, 3)
    gather("own", BRANCH)
    gather("line", INNER, 1)
    gather("cross", INNER, 0)
    gather("hand_on", SQUARE, 0)
    gather("hand_on", SQUARE, 1)
    gather("line", INNER, 2)
    gather("hand_on", SQUARE, 2)
    gather("hand_on", SQUARE, 3)
    gather("pair", BRANCH)
    gather("line", INNER, 3)
    for turn in range(4):
        gather("take", SQUARE, turn)
    project_key()
    gather("cross", INNER, 1)
    project_query()
    gather("cross", INNER, 2)
    project_value()
    gather("cross", INNER, 3)

    @pl.loop(0, 12)
    def _(it):
        steps_at(
            it,
            {
                0: [("line", BRANCH, 1)],
                2: [("cross", BRANCH, 0)],
                4: [("hand_on", INNER, 0)],
                6: [("hand_on", INNER, 1)],
                8: [("line", BRANCH, 2)],
                10: [("hand_on", INNER, 2)],
            },
        )
        attend_pair(it)

    gather("hand_on", INNER, 3)

    @pl.loop(0, 2)
    def _(i):
        steps_at(i, {1: [("line", BRANCH, 3)]})
        close_attention(i)

    for turn in (1, 2, 3):
        gather("cross", BRANCH, turn)

    @pl.loop(0, 8)
    def _(it):
        steps_at(
            it,
            {
                0: [("take", INNER, 0)],
                2: [("take", INNER, 1), ("hand_on", BRANCH, 0)],
                4: [("take", INNER, 2), ("hand_on", BRANCH, 1)],
                6: [("take", INNER, 3), ("hand_on", BRANCH, 2)],
            },
        )
        inner_block(it)

    gather("hand_on", BRANCH, 3)

    @pl.loop(0, 4)
    def _(turn):
        steps_at(turn, {k: [("take", BRANCH, k)] for k in range(4)})
        branch_block(turn)

    @pl.loop(0, 2)
    def _(i):
        rows = rows_of(i)
        normed, inverse = standardise(resid[rows, :])
        gain = row(norm_gains, 1)
        out_stage[rows, :] = (normed * gain + row(norm_biases, 1)).astype(NARROW)
        grad = standardise_back(normed, inverse, cotangent[rows, :].astype(WIDE) * gain)
        resid[rows, :] = grad
        narrow_one[rows, :] = grad.astype(NARROW)

    out_copy = pltpu.make_async_copy(out_stage, output, local_sems.at[0])
    out_copy.start()

    @pl.loop(0, 4)
    def _(plane):
        cols = hidden_cols(plane)
        for i in range(2):
            rows = pl.ds(i * 256, 256)
            grad = dot_nt(narrow_one[rows, :], branch_w[plane].reshape(768, 768)).astype(NARROW)
            grad = (slope[rows, cols].astype(WIDE) * grad.astype(WIDE)).astype(NARROW)
            resid[rows, :] += dot_nn(grad, inner_t[plane].reshape(768, 768))

    @pl.loop(0, 2)
    def _(i):
        rows = rows_of(i)
        grad = standardise_back(normed_one[rows, :], inverse_one[rows, :], resid[rows, :] * row(norm_gains, 0))
        resid[rows, :] = grad
        narrow_one[rows, :] = dot_nt(grad.astype(NARROW), weight(3)).astype(NARROW)

    @pl.loop(0, 12)
    def _(it):
        seq, j = it // 6, lax.rem(it, 6)
        rows, cols = rows_of(seq), head_cols(j)
        q_pair, k_pair, v_pair, grad = query[rows, cols], key[rows, cols], value[rows, cols], narrow_one[rows, cols]
        zero = jnp.zeros_like(grad)
        parts_q, parts_k, parts_v = [], [], []
        for half in range(2):
            mine_here = first_half if half == 0 else jnp.logical_not(first_half)
            soft = probs[it * 2 + half]
            wide = soft.astype(WIDE)
            grad_soft = dot_nt(jnp.where(mine_here, grad, zero), v_pair)
            inner_sum = jnp.sum(grad_soft * wide, axis=-1, keepdims=True)
            grad_scores = (wide * (grad_soft - inner_sum)).astype(NARROW)
            parts_v.append(dot_tn(soft, grad))
            parts_q.append(dot_nn(grad_scores, k_pair))
            parts_k.append(dot_tn(grad_scores, q_pair))
        query[rows, cols] = (jnp.where(first_half, parts_q[0], parts_q[1]) * HEAD ** (-0.5)).astype(NARROW)
        key[rows, cols] = jnp.where(first_half, parts_k[0], parts_k[1]).astype(NARROW)
        value[rows, cols] = jnp.where(first_half, parts_v[0], parts_v[1]).astype(NARROW)

    plane_sums[spot] = jnp.zeros((4, 1024), WIDE)
    low_grad = hidden

    @pl.loop(0, 2)
    def _(i):
        rows = rows_of(i)
        grad_q, grad_v = query[rows, :].astype(WIDE), value[rows, :].astype(WIDE)
        plane_sums[spot, 2:3, 0:768] += jnp.sum(extra_q[rows, :] * grad_q, axis=0, keepdims=True)
        plane_sums[spot, 3:4, 0:768] += jnp.sum(extra_v[rows, :] * grad_v, axis=0, keepdims=True)
        grad_q = (row(scale_b, 0) * grad_q).astype(NARROW)
        grad_v = (row(scale_b, 1) * grad_v).astype(NARROW)
        for h in range(2):
            half = slice(h * 512, (h + 1) * 512)
            scaled_q, scaled_v = dot_nn(grad_q, up(h)), dot_nn(grad_v, up(h))
            plane_sums[spot, 0:1, half] += jnp.sum(low[rows, half] * scaled_q, axis=0, keepdims=True)
            plane_sums[spot, 1:2, half] += jnp.sum(low[rows, half] * scaled_v, axis=0, keepdims=True)
            total = scales[h, 0:1, :].astype(WIDE) * scaled_q + scales[h, 1:2, :].astype(WIDE) * scaled_v
            low_grad[rows, half] = total.astype(NARROW)

    def plane_copy(turn, slot):
        return pltpu.make_async_remote_copy(
            plane_sums.at[slot],
            plane_sums.at[slot],
            sum_sems.at[1 + turn],
            sum_sems.at[9 + slot],
            device_id=in_plane(turn)[1],
            device_id_type=MESH_IDS,
        )

    def line_copy(turn, slot):
        return pltpu.make_async_remote_copy(
            line_sums.at[slot],
            line_sums.at[slot],
            sum_sems.at[16 + turn],
            sum_sems.at[20 + slot],
            device_id=in_line(turn)[1],
            device_id_type=MESH_IDS,
        )

    def input_rows(i):
        rows = slice(i * 256, (i + 1) * 256)
        total = resid[rows, :] + dot_nt(query[rows, :], weight(0))
        total = total + dot_nt(key[rows, :], weight(1))
        total = total + dot_nt(value[rows, :], weight(2))
        for h in range(2):
            total = total + dot_nt(low_grad[rows, h * 512 : (h + 1) * 512], down_t(h))
        grad_stage[rows, :] = total.astype(NARROW)
        return pltpu.make_async_copy(grad_stage.at[rows, :], input_grad.at[rows, :], local_sems.at[1 + i])

    for turn in range(1, PLANE):
        plane_copy(turn, spot).start()
    grad_copies = [input_rows(0)]
    grad_copies[0].start()
    for turn in range(1, PLANE):
        plane_copy(turn, in_plane(turn)[0]).wait_recv()
    total = plane_sums[0]
    for other in range(1, PLANE):
        total = total + plane_sums[other]
    line_sums[z] = total
    for turn in range(1, LINE):
        line_copy(turn, z).start()
    grad_copies.append(input_rows(1))
    grad_copies[1].start()
    for turn in range(1, LINE):
        line_copy(turn, in_line(turn)[0]).wait_recv()
    cols = pl.ds(pl.multiple_of(x * 512, 512), 512)
    total_d, total_b = line_sums[0, 0:2, cols], line_sums[0, 2:4, 0:768]
    for other in range(1, LINE):
        total_d = total_d + line_sums[other, 0:2, cols]
        total_b = total_b + line_sums[other, 2:4, 0:768]
    d_grad[...] = total_d * grad_scale
    b_grad[...] = total_b * grad_scale

    for turn in range(1, PLANE):
        plane_copy(turn, spot).wait_send()
    for turn in range(1, LINE):
        line_copy(turn, z).wait_send()
    for g in range(len(GROUPS)):
        gather("finish", g)
    out_copy.wait()
    for copy in grad_copies:
        copy.wait()


def fused_layer(
    tokens,
    cotangent,
    seg_lengths,
    attn_weights,
    out_weight,
    ffn_in,
    ffn_out,
    lin_biases,
    ffn_bias,
    norm_gains,
    norm_biases,
    shared_down,
    shared_up,
    scale_d,
    scale_b,
):
    rows, width = tokens.shape[0] * tokens.shape[1] * tokens.shape[2], tokens.shape[3]
    devices = lax.axis_size("dp") * lax.axis_size("rank")
    in_vmem, anywhere = pl.BlockSpec(memory_space=pltpu.VMEM), pl.BlockSpec(memory_space=pl.ANY)
    in_smem = pl.BlockSpec(memory_space=pltpu.SMEM)
    shapes = [(4, 2, 2, 2) + lead + (cols,) for lead, cols, _ in GROUPS]
    flat = (rows, width)
    scratch = [pltpu.VMEM(shape, NARROW) for shape in shapes] + [
        pltpu.VMEM((2, 2, 512), NARROW),
        pltpu.VMEM((2, 256, 256), WIDE),
        pltpu.VMEM((rows, 1024), WIDE),
        pltpu.VMEM(flat, WIDE),
        pltpu.VMEM(flat, WIDE),
        pltpu.VMEM(flat, NARROW),
        pltpu.VMEM(flat, NARROW),
        pltpu.VMEM(flat, NARROW),
        pltpu.VMEM((24, 256, 256), NARROW),
        pltpu.VMEM(flat, NARROW),
        pltpu.VMEM(flat, WIDE),
        pltpu.VMEM((rows, 1), WIDE),
        pltpu.VMEM(flat, WIDE),
        pltpu.VMEM(flat, NARROW),
        pltpu.VMEM((rows, 3072), NARROW),
        pltpu.VMEM((rows, 3072), NARROW),
        pltpu.VMEM(flat, NARROW),
        pltpu.VMEM(flat, NARROW),
        pltpu.VMEM((PLANE, 4, 1024), WIDE),
        pltpu.VMEM((LINE, 4, 1024), WIDE),
        pltpu.VMEM((1, 3072), WIDE),
        pltpu.SemaphoreType.DMA((len(GROUPS), SEND_SLOTS)),
        pltpu.SemaphoreType.DMA((len(GROUPS), RECV_SLOTS)),
        pltpu.SemaphoreType.DMA((7,)),
        pltpu.SemaphoreType.DMA((24,)),
    ]
    output, input_grad, d_grad, b_grad = pl.pallas_call(
        functools.partial(layer_kernel, 1.0 / math.sqrt(rows * devices)),
        out_shape=(
            jax.ShapeDtypeStruct(flat, NARROW),
            jax.ShapeDtypeStruct(flat, NARROW),
            jax.ShapeDtypeStruct((2, 512), WIDE),
            jax.ShapeDtypeStruct((2, 768), WIDE),
        ),
        in_specs=[in_vmem, in_vmem, in_smem]
        + [anywhere] * 4
        + [in_vmem] * 4
        + [anywhere] * 3
        + [in_vmem],
        out_specs=(anywhere, anywhere, in_vmem, in_vmem),
        scratch_shapes=scratch,
        compiler_params=pltpu.CompilerParams(
            collective_id=0, has_side_effects=True, vmem_limit_bytes=61 << 20
        ),
    )(
        tokens.reshape(flat),
        cotangent.reshape(flat),
        seg_lengths.reshape(-1, seg_lengths.shape[-1]),
        attn_weights,
        out_weight,
        ffn_in.T,
        ffn_out,
        lin_biases,
        ffn_bias,
        norm_gains,
        norm_biases,
        shared_down.T,
        shared_up,
        scale_d,
        scale_b,
    )
    return output.reshape(tokens.shape), input_grad.reshape(tokens.shape), d_grad, b_grad


def gather_weights(attn_weights, out_weight, ffn_in, ffn_out, shared_down, shared_up):
    down_local = lax.all_gather(shared_down, "dp", axis=1, tiled=True)
    up_local = lax.all_gather(shared_up, "dp", axis=0, tiled=True)
    return (
        lax.all_gather(attn_weights, ("dp", "rank"), axis=1, tiled=True),
        lax.all_gather(out_weight, ("dp", "rank"), axis=0, tiled=True),
        lax.all_gather(ffn_in, ("dp", "rank"), axis=1, tiled=True),
        lax.all_gather(ffn_out, ("dp", "rank"), axis=0, tiled=True),
        lax.all_gather(down_local, "rank", axis=0, tiled=True),
        lax.all_gather(up_local, "rank", axis=1, tiled=True),
    )


def per_device(
    tokens,
    cotangent,
    seg_lengths,
    attn_weights,
    out_weight,
    ffn_in,
    ffn_out,
    lin_biases,
    ffn_bias,
    norm_gains,
    norm_biases,
    shared_down,
    shared_up,
    scale_d,
    scale_b,
):
    micro_count, seq_count, length_rows, model_width = tokens.shape
    head_count = model_width // HEAD
    out_shape = tokens.shape
    seq_count = micro_count * seq_count
    row_count = seq_count * length_rows
    head_shape = (seq_count, length_rows, head_count, HEAD)
    float_wide = jnp.float32
    narrow = jnp.bfloat16
    attn_full, output_full, inner_full, branch_full, down_use, up_use = gather_weights(
        attn_weights, out_weight, ffn_in, ffn_out, shared_down, shared_up
    )
    scales_use = lax.all_gather(scale_d, "rank", axis=1, tiled=True)
    rank_cols = scales_use.shape[1]
    sum_d = jnp.zeros((2, rank_cols), float_wide)
    sum_b = jnp.zeros((2, model_width), float_wide)
    outputs = []
    input_grads = []
    for micro_step in range(1):
        token_rows = tokens.reshape(row_count, model_width)
        same_segment = segment_match(seg_lengths.reshape(seq_count, -1), length_rows)
        lowrank = jnp.einsum("rd,kd->rk", token_rows, down_use, preferred_element_type=float_wide)
        scaled = (scales_use[:, None, :] * lowrank[None]).astype(narrow)
        adapted = jnp.concatenate(
            [
                jnp.einsum("rk,dk->rd", scaled[0], up_use, preferred_element_type=float_wide),
                jnp.einsum("rk,dk->rd", scaled[1], up_use, preferred_element_type=float_wide),
            ],
            axis=1,
        )
        extra_query = adapted[:, :model_width]
        extra_value = adapted[:, model_width:]
        query_rows = (
            jnp.dot(token_rows, attn_full[0], preferred_element_type=float_wide)
            + lin_biases[0]
            + scale_b[0] * extra_query
        ).astype(narrow)
        key_rows = jnp.dot(token_rows, attn_full[1], preferred_element_type=float_wide).astype(
            narrow
        )
        value_rows = (
            jnp.dot(token_rows, attn_full[2], preferred_element_type=float_wide)
            + lin_biases[1]
            + scale_b[1] * extra_value
        ).astype(narrow)
        query_heads = query_rows.reshape(head_shape)
        key_heads = key_rows.reshape(head_shape)
        value_heads = value_rows.reshape(head_shape)
        context, log_total = attend(query_heads, key_heads, value_heads, same_segment)
        attended = (
            jnp.dot(
                context.reshape(row_count, model_width),
                output_full,
                preferred_element_type=float_wide,
            )
            + lin_biases[2]
        )
        resid_one = token_rows.astype(float_wide) + attended
        normed_one = layer_norm(resid_one, norm_gains[0], norm_biases[0])
        inner_pre = (
            jnp.dot(normed_one.astype(narrow), inner_full, preferred_element_type=float_wide)
            + ffn_bias
        )
        hidden = gelu_exact(inner_pre).astype(narrow)
        branch = jnp.dot(hidden, branch_full, preferred_element_type=float_wide) + lin_biases[3]
        resid_two = normed_one + branch
        outputs.append(
            layer_norm(resid_two, norm_gains[1], norm_biases[1])
            .astype(narrow)
            .reshape(out_shape)
        )
        grad_out = cotangent.reshape(row_count, model_width).astype(float_wide)
        grad_two = norm_back(resid_two, norm_gains[1], norm_biases[1], grad_out)
        grad_hidden = jnp.einsum(
            "rd,fd->rf", grad_two.astype(narrow), branch_full, preferred_element_type=float_wide
        ).astype(narrow)
        grad_inner = gelu_back(inner_pre, grad_hidden.astype(float_wide)).astype(narrow)
        grad_normed = grad_two + jnp.einsum(
            "rf,df->rd", grad_inner, inner_full, preferred_element_type=float_wide
        )
        grad_one = norm_back(resid_one, norm_gains[0], norm_biases[0], grad_normed)
        grad_attended = grad_one.astype(narrow)
        grad_context = jnp.einsum(
            "ro,io->ri", grad_attended, output_full, preferred_element_type=float_wide
        ).astype(narrow)
        grad_query, grad_keys, grad_values = attend_back(
            query_heads,
            key_heads,
            value_heads,
            same_segment,
            log_total,
            grad_context.reshape(head_shape),
        )
        query_grad = grad_query.reshape(row_count, model_width).astype(narrow)
        key_grad = grad_keys.reshape(row_count, model_width).astype(narrow)
        value_grad = grad_values.reshape(row_count, model_width).astype(narrow)
        grad_input = grad_one + jnp.einsum(
            "ro,io->ri", query_grad, attn_full[0], preferred_element_type=float_wide
        )
        grad_input = grad_input + jnp.einsum(
            "ro,io->ri", key_grad, attn_full[1], preferred_element_type=float_wide
        )
        grad_input = grad_input + jnp.einsum(
            "ro,io->ri", value_grad, attn_full[2], preferred_element_type=float_wide
        )
        query_grad_wide = query_grad.astype(float_wide)
        value_grad_wide = value_grad.astype(float_wide)
        sum_b = sum_b + jnp.stack(
            [
                jnp.sum(extra_query * query_grad_wide, axis=0),
                jnp.sum(extra_value * value_grad_wide, axis=0),
            ]
        )
        grad_extra = jnp.concatenate(
            [
                (scale_b[0] * query_grad_wide).astype(narrow),
                (scale_b[1] * value_grad_wide).astype(narrow),
            ],
            axis=1,
        )
        grad_scaled = jnp.concatenate(
            [
                jnp.dot(grad_extra[:, :model_width], up_use, preferred_element_type=float_wide),
                jnp.dot(grad_extra[:, model_width:], up_use, preferred_element_type=float_wide),
            ],
            axis=1,
        )
        grad_scaled_query = grad_scaled[:, :rank_cols]
        grad_scaled_value = grad_scaled[:, rank_cols:]
        sum_d = sum_d + jnp.stack(
            [
                jnp.sum(lowrank * grad_scaled_query, axis=0),
                jnp.sum(lowrank * grad_scaled_value, axis=0),
            ]
        )
        grad_lowrank = (
            scales_use[0] * grad_scaled_query + scales_use[1] * grad_scaled_value
        ).astype(narrow)
        grad_from_adapter = jnp.dot(grad_lowrank, down_use, preferred_element_type=float_wide)
        input_grads.append(
            (grad_input + grad_from_adapter)
            .astype(narrow)
            .reshape(out_shape)
        )
    grad_scale = 1.0 / math.sqrt(
        row_count * lax.axis_size("dp") * lax.axis_size("rank")
    )
    total_d, total_b = lax.psum((sum_d, sum_b), ("dp", "rank"))
    local_cols = scale_d.shape[1]
    total_d = lax.dynamic_slice_in_dim(total_d, lax.axis_index("rank") * local_cols, local_cols, 1)
    return (outputs[0], input_grads[0], total_d * grad_scale, total_b * grad_scale)


def solution(mesh):
    return jax.shard_map(
        fused_layer if (mesh.shape["dp"], mesh.shape["rank"]) == (16, 2) else per_device,
        mesh=mesh,
        in_specs=(
            P(None, ("dp", "rank"), None, None),
            P(None, ("dp", "rank"), None, None),
            P(None, ("dp", "rank"), None),
            P(None, ("dp", "rank"), None),
            P(("dp", "rank"), None),
            P(None, ("dp", "rank")),
            P(("dp", "rank"), None),
            P(),
            P(),
            P(),
            P(),
            P("rank", "dp"),
            P("dp", "rank"),
            P(None, "rank"),
            P(),
        ),
        out_specs=(
            P(None, ("dp", "rank"), None, None),
            P(None, ("dp", "rank"), None, None),
            P(None, "rank"),
            P(),
        ),
        check_vma=False,
    )
```

```python
import functools
import math

import jax
import jax.numpy as jnp
from jax import lax
from jax.experimental import pallas as pl
from jax.experimental.pallas import tpu as pltpu
from jax.sharding import PartitionSpec as P

HEAD = 64


eps_norm = 1e-05
neg_big = -1000000000.0


def layer_norm(resid, norm_gain, norm_shift):
    row_mean = jnp.mean(resid, axis=-1, keepdims=True)
    centred = resid - row_mean
    variance = jnp.mean(centred * centred, axis=-1, keepdims=True)
    return centred * lax.rsqrt(variance + eps_norm) * norm_gain + norm_shift


def norm_back(resid, norm_gain, norm_shift, grad_normed):

    def forward_norm(values_in):
        return layer_norm(values_in, norm_gain, norm_shift)

    pullback = jax.vjp(forward_norm, resid)[1]
    return pullback(grad_normed)[0]


def gelu_exact(values_in):
    return jax.nn.gelu(values_in, approximate=False)


def gelu_back(inner_pre, grad_hidden):
    pullback = jax.vjp(gelu_exact, inner_pre)[1]
    return pullback(grad_hidden)[0]


def segment_match(lengths, length_rows):
    cumulative = jnp.cumsum(lengths, axis=-1)
    places = jnp.arange(length_rows, dtype=jnp.int32)
    labels = jnp.sum((places[None, :, None] >= cumulative[:, None, :]).astype(jnp.int32), axis=-1)
    return labels[:, :, None] == labels[:, None, :]


def masked_scores(query_heads, key_heads, same_segment):
    scores = jnp.einsum(
        "sqhe,skhe->shqk", query_heads, key_heads, preferred_element_type=jnp.float32
    ) * HEAD ** (-0.5)
    return jnp.where(same_segment[:, None], scores, neg_big)


def attend(query_heads, key_heads, value_heads, same_segment):
    scores = masked_scores(query_heads, key_heads, same_segment)
    row_peak = jnp.max(scores, axis=-1, keepdims=True)
    exponent = jnp.exp(scores - row_peak)
    row_total = jnp.sum(exponent, axis=-1, keepdims=True)
    weights_soft = (exponent / row_total).astype(jnp.bfloat16)
    context = jnp.einsum(
        "shqk,skhe->sqhe", weights_soft, value_heads, preferred_element_type=jnp.float32
    )
    return (context.astype(jnp.bfloat16), row_peak + jnp.log(row_total))


def attend_back(query_heads, key_heads, value_heads, same_segment, log_total, grad_context):
    scores = masked_scores(query_heads, key_heads, same_segment)
    weights_soft = jnp.exp(scores - log_total)
    grad_values = jnp.einsum(
        "shqk,sqhe->skhe",
        weights_soft.astype(jnp.bfloat16),
        grad_context,
        preferred_element_type=jnp.float32,
    )
    grad_weights = jnp.einsum(
        "sqhe,skhe->shqk", grad_context, value_heads, preferred_element_type=jnp.float32
    )
    inner_sum = jnp.sum(grad_weights * weights_soft, axis=-1, keepdims=True)
    grad_scores = (weights_soft * (grad_weights - inner_sum)).astype(jnp.bfloat16)
    grad_query = jnp.einsum(
        "shqk,skhe->sqhe", grad_scores, key_heads, preferred_element_type=jnp.float32
    ) * HEAD ** (-0.5)
    grad_keys = jnp.einsum(
        "shqk,sqhe->skhe", grad_scores, query_heads, preferred_element_type=jnp.float32
    ) * HEAD ** (-0.5)
    return (grad_query, grad_keys, grad_values)


ALL = slice(None)
MESH_IDS = pl.DeviceIdType.MESH
WIDE = jnp.float32
NARROW = jnp.bfloat16
GROUPS = (((2, 48), 512, 256), ((4, 24), 768, 512), ((96,), 768, 384), ((96,), 768, 512))
VERA, SQUARE, INNER, BRANCH = range(4)
SCHEDULE = (
    ("own", VERA),
    ("own", SQUARE),
    ("pair", VERA),
    ("pair", SQUARE),
    ("line_b", VERA, 1),
    ("line_b", SQUARE, 1),
    ("line_a", VERA, 1),
    ("cross", VERA, 1),
    ("cross", SQUARE, 0),
    ("own", INNER),
    ("line_b", VERA, 2),
    ("line_a", SQUARE, 1),
    ("cross", SQUARE, 1),
    ("cross", VERA, 0),
    ("line_b", VERA, 3),
    ("cross", VERA, 2),
    ("line_a", VERA, 2),
    ("line_b", SQUARE, 2),
    ("pair", INNER),
    ("cross", VERA, 3),
    ("cross", SQUARE, 2),
    ("hand_on", VERA, 2),
    ("line_a", SQUARE, 2),
    ("cross", INNER, 0),
    ("line_a", VERA, 3),
    ("hand_on", SQUARE, 0),
    ("hand_on", VERA, 0),
    ("hand_on", SQUARE, 2),
    ("line_b", SQUARE, 3),
    ("own", BRANCH),
    ("hand_on", VERA, 3),
    ("cross", SQUARE, 3),
    ("hand_on", VERA, 1),
    ("hand_on", SQUARE, 1),
    ("line_b", INNER, 1),
    ("line_a", SQUARE, 3),
    ("line_b", BRANCH, 1),
    ("hand_on", INNER, 0),
    ("line_b", INNER, 2),
    ("line_a", INNER, 1),
    ("take", VERA, 0),
    ("take", VERA, 1),
    ("take", SQUARE, 2),
    ("take", VERA, 3),
    ("take", INNER, 0),
    ("take", SQUARE, 1),
    ("take", SQUARE, 0),
    ("take", VERA, 2),
    ("line_b", BRANCH, 2),
    ("scales",),
    ("adapters", 0),
    ("cross", INNER, 2),
    ("hand_on", SQUARE, 3),
    ("adapters", 1),
    ("cross", INNER, 1),
    ("pair", BRANCH),
    ("take", SQUARE, 3),
    ("project_key", 0),
    ("line_a", INNER, 2),
    ("project_query", 0),
    ("project_value", 0),
    ("cross", BRANCH, 0),
    ("attend", 0),
    ("line_b", INNER, 3),
    ("attend", 1),
    ("attend", 2),
    ("line_a", BRANCH, 1),
    ("line_b", BRANCH, 3),
    ("attend", 3),
    ("hand_on", INNER, 1),
    ("attend", 4),
    ("cross", INNER, 3),
    ("hand_on", INNER, 2),
    ("line_a", INNER, 3),
    ("attend", 5),
    ("hand_on", BRANCH, 0),
    ("cross", BRANCH, 1),
    ("cross", BRANCH, 2),
    ("take", INNER, 1),
    ("close", 0),
    ("line_a", BRANCH, 2),
    ("close", 1),
    ("inner", 0),
    ("cross", BRANCH, 3),
    ("inner", 1),
    ("hand_on", INNER, 3),
    ("inner", 2),
    ("take", INNER, 2),
    ("inner", 3),
    ("line_a", BRANCH, 3),
    ("hand_on", BRANCH, 1),
    ("inner", 4),
    ("hand_on", BRANCH, 2),
    ("inner", 5),
    ("take", INNER, 3),
    ("inner", 6),
    ("take", BRANCH, 0),
    ("take", BRANCH, 1),
    ("inner", 7),
    ("branch", 0),
    ("hand_on", BRANCH, 3),
    ("take", BRANCH, 2),
    ("branch", 1),
    ("branch", 2),
    ("take", BRANCH, 3),
    ("branch", 3),
)
SEND_SLOTS = 39
RECV_SLOTS = 25
LINE = 4
PLANE = 8


def nearest(z, turn):
    upper = z // 2
    inner = z * (1 - upper) + (3 - z) * upper
    plane = turn + inner * (1 - 2 * turn) * (1 - turn // 2)
    return plane * (1 - upper) + (3 - plane) * upper


class Relay:
    def __init__(self, buffers, send_sems, recv_sems):
        self.buffers, self.send_sems, self.recv_sems = buffers, send_sems, recv_sems
        place = lax.axis_index("dp")
        self.x = lax.axis_index("rank")
        self.z, self.y, self.c = place // 4, (place // 2) % 2, place % 2

    def device(self, z, y, c, x):
        return {"dp": z * 4 + y * 2 + c, "rank": x}

    def neighbour(self, c, which):
        z, y, x = self.z, self.y, self.x
        if which == "s":
            return self.device(z, y, 1 - c, x)
        if which == "u":
            return self.device(z + 1, y, c, x)
        if which == "d":
            return self.device(z - 1, y, c, x)
        if (which == "p") == (c == 0):
            return self.device(z, y, c, 1 - x)
        return self.device(z, 1 - y, c, x)

    def view(self, g, c, plane, p, q, part):
        lead, cols, split = GROUPS[g]
        window = {"A": pl.ds(0, split), "B": pl.ds(split, cols - split), "F": pl.ds(0, cols)}[part]
        place = (plane, q, c, p) if c == 0 else (plane, p, c, q)
        return self.buffers[g].at[place + (ALL,) * len(lead) + (window,)]

    def copy(self, g, c, plane, p, q, part, to, send, recv):
        block = self.view(g, c, plane, p, q, part)
        return pltpu.make_async_remote_copy(
            block,
            block,
            self.send_sems.at[g, send],
            self.recv_sems.at[g, recv],
            device_id=self.neighbour(c, to),
            device_id_type=MESH_IDS,
        )


class Steps:
    def __init__(self, relay, g, c):
        self.relay, self.g, self.c = relay, g, c
        self.z = relay.z
        self.p, self.q = (relay.x, relay.y) if c == 0 else (relay.y, relay.x)
        self.closing = False

    def send(self, cond, *where):
        def act():
            copy = self.relay.copy(self.g, self.c, *where)
            if self.closing:
                copy.wait_send()
            else:
                copy.start()

        if cond is None:
            act()
        else:
            pl.when(cond)(act)

    def finish(self):
        self.closing = True
        self.own()
        self.pair()
        for far in (1, 2, 3):
            self.line_a(far)
            self.line_b(far)
        for turn in range(4):
            self.cross(turn)
            self.hand_on(turn)

    def got(self, *where):
        if not self.closing:
            self.relay.copy(self.g, self.c, *where).wait_recv()

    def own(self):
        z, p, q = self.z, self.p, self.q
        self.send(None, z, p, q, "A", "p", 0, 0)
        self.send(z < 3, z, p, q, "B", "u", 1, 9 + z)
        self.send(z > 0, z, p, q, "B", "d", 2, 9 + z)
        self.send(None, z, p, q, "B", "p", 3, 13 + z)

    def pair(self):
        z, p, q = self.z, self.p, self.q
        self.got(z, 1 - p, q, "A", "p", 0, 0)
        self.send(z < 3, z, ALL, q, "A", "u", 4, 1 + z)
        self.send(z > 0, z, ALL, q, "A", "d", 5, 1 + z)
        self.send(None, z, ALL, q, "A", "q", 6, 5 + z)

    def line(self, part, far):
        z, p, q = self.z, self.p, self.q
        for side in (0, 1):
            plane = z - far if side == 0 else z + far
            cond = plane >= 0 if side == 0 else plane <= 3
            more = z < 3 if side == 0 else z > 0
            to = "u" if side == 0 else "d"
            slot = 6 * far + 1 + 3 * side
            if part == "A":

                @pl.when(cond)
                def _():
                    self.got(plane, ALL, q, "A", to, 0, 1 + plane)

                if far < 3:
                    self.send(jnp.logical_and(cond, more), plane, ALL, q, "A", to, slot, 1 + plane)
                self.send(cond, plane, ALL, q, "A", "q", slot + 1, 5 + plane)
            else:

                @pl.when(cond)
                def _():
                    self.got(plane, p, q, "B", to, 0, 9 + plane)

                if far < 3:
                    self.send(jnp.logical_and(cond, more), plane, p, q, "B", to, slot + 2, 9 + plane)
                self.send(cond, plane, p, q, "B", "p", 23 + 2 * far + side, 13 + plane)

    def line_a(self, far):
        self.line("A", far)

    def line_b(self, far):
        self.line("B", far)

    def cross(self, turn):
        plane = nearest(self.z, turn)
        self.got(plane, 1 - self.p, self.q, "B", "p", 0, 13 + plane)
        self.send(None, plane, ALL, self.q, "B", "q", 31 + turn, 17 + plane)

    def hand_on(self, turn):
        plane = nearest(self.z, turn)
        self.got(plane, ALL, 1 - self.q, "A", "q", 0, 5 + plane)
        self.got(plane, ALL, 1 - self.q, "B", "q", 0, 17 + plane)
        self.send(None, plane, ALL, ALL, "F", "s", 35 + turn, 21 + plane)

    def take(self, turn):
        plane = nearest(self.z, turn)
        self.relay.copy(self.g, 1 - self.c, plane, ALL, ALL, "F", "s", 0, 21 + plane).wait_recv()


class Gather:
    def __init__(self, relay):
        self.relay = relay
        self.steps = [[Steps(relay, g, c) for g in range(len(GROUPS))] for c in (0, 1)]

    def __call__(self, name, g, *where):
        for core in (0, 1):

            @pl.when(self.relay.c == core)
            def _():
                getattr(self.steps[core][g], name)(*where)


def dot_nn(left, right):
    return jnp.dot(left, right, preferred_element_type=WIDE)


def dot_nt(left, right):
    return lax.dot_general(left, right, (((1,), (1,)), ((), ())), preferred_element_type=WIDE)


def dot_tn(left, right):
    return lax.dot_general(left, right, (((0,), (0,)), ((), ())), preferred_element_type=WIDE)


def standardise(resid):
    centred = resid - jnp.mean(resid, axis=-1, keepdims=True)
    inverse = lax.rsqrt(jnp.mean(centred * centred, axis=-1, keepdims=True) + eps_norm)
    return centred * inverse, inverse


def standardise_back(normed, inverse, grad):
    along = jnp.mean(grad * normed, axis=-1, keepdims=True)
    return inverse * (grad - jnp.mean(grad, axis=-1, keepdims=True) - normed * along)


def layer_kernel(grad_scale, *refs):
    (
        tokens,
        cotangent,
        seg_lengths,
        attn_piece,
        out_piece,
        inner_piece,
        branch_piece,
        lin_biases,
        ffn_bias,
        norm_gains,
        norm_biases,
        down_piece,
        up_piece,
        scale_d,
        scale_b,
        output,
        input_grad,
        d_grad,
        b_grad,
        vera,
        square,
        inner_t,
        branch_w,
        scales,
        same,
        low,
        extra_q,
        extra_v,
        query,
        key,
        value,
        probs,
        context,
        normed_one,
        inverse_one,
        resid,
        narrow_one,
        hidden,
        slope,
        out_stage,
        grad_stage,
        plane_sums,
        line_sums,
        bias_row,
        send_sems,
        recv_sems,
        local_sems,
        sum_sems,
    ) = refs
    relay = Relay((vera, square, inner_t, branch_w), send_sems, recv_sems)
    gather = Gather(relay)
    z, y, c, x = relay.z, relay.y, relay.c, relay.x
    spot = c * 4 + y * 2 + x

    def in_plane(turn):
        other = lax.rem(spot + turn, PLANE)
        return other, relay.device(z, (other // 2) % 2, other // 4, other % 2)

    def in_line(turn):
        other = lax.rem(z + turn, LINE)
        return other, relay.device(other, y, c, x)

    mine = [
        pltpu.make_async_copy(up_piece, vera.at[z, y, c, x, 1], local_sems.at[0]),
        pltpu.make_async_copy(attn_piece, square.at[z, y, c, x, pl.ds(0, 3)], local_sems.at[1]),
        pltpu.make_async_copy(out_piece, square.at[z, y, c, x, 3], local_sems.at[2]),
        pltpu.make_async_copy(branch_piece, branch_w.at[z, y, c, x], local_sems.at[3]),
        pltpu.make_async_copy(scale_d, scales.at[x], local_sems.at[4]),
        pltpu.make_async_copy(inner_piece, inner_t.at[z, y, c, x], local_sems.at[5]),
        pltpu.make_async_copy(down_piece, vera.at[z, y, c, x, 0], local_sems.at[6]),
    ]
    for copy in mine:
        copy.start()
    barrier = pltpu.get_barrier_semaphore()

    def greet(device):
        pl.semaphore_signal(barrier, 1, device_id=device, device_id_type=MESH_IDS)

    greet(relay.device(z, y, 1 - c, x))
    greet(relay.device(z, y, c, 1 - x))
    greet(relay.device(z, 1 - y, c, x))

    @pl.when(z < 3)
    def _():
        greet(relay.device(z + 1, y, c, x))

    @pl.when(z > 0)
    def _():
        greet(relay.device(z - 1, y, c, x))

    for copy in mine:
        copy.wait()
    pl.semaphore_wait(barrier, 3 + jnp.where(z < 3, 1, 0) + jnp.where(z > 0, 1, 0))

    scale_copy = pltpu.make_async_remote_copy(
        scales.at[x],
        scales.at[x],
        sum_sems.at[0],
        sum_sems.at[1],
        device_id=relay.device(z, y, c, 1 - x),
        device_id_type=MESH_IDS,
    )
    scale_copy.start()

    def segments(seq):
        row_place = lax.broadcasted_iota(jnp.int32, (256, 256), 0)
        col_place = lax.broadcasted_iota(jnp.int32, (256, 256), 1)
        row_label = jnp.zeros((256, 256), jnp.int32)
        col_label = jnp.zeros((256, 256), jnp.int32)
        end = jnp.int32(0)
        for k in range(seg_lengths.shape[1]):
            end = end + seg_lengths[seq, k]
            row_label = row_label + (row_place >= end).astype(jnp.int32)
            col_label = col_label + (col_place >= end).astype(jnp.int32)
        same[seq] = jnp.where(row_label == col_label, 0.0, neg_big)

    def row(ref, k):
        return ref[k : k + 1, :].astype(WIDE)

    def rows_of(i):
        return pl.ds(pl.multiple_of(i * 256, 256), 256)

    def down_t(h):
        return vera[:, :, :, h, 0].reshape(768, 512)

    def up(h):
        return vera[:, :, :, h, 1].reshape(768, 512)

    def weight(k):
        return square[:, :, :, :, k].reshape(768, 768)

    def steps_at(i, relays):
        for k, steps in relays.items():

            @pl.when(i == k)
            def _():
                for step in steps:
                    take_step(step)

    def adapters(i):
        rows = rows_of(i)
        token_rows = tokens[rows, :]
        parts_q, parts_v = [], []
        for h in range(2):
            lowrank = dot_nn(token_rows, down_t(h))
            low[rows, h * 512 : (h + 1) * 512] = lowrank
            parts_q.append(dot_nt((scales[h, 0:1, :].astype(WIDE) * lowrank).astype(NARROW), up(h)))
            parts_v.append(dot_nt((scales[h, 1:2, :].astype(WIDE) * lowrank).astype(NARROW), up(h)))
        extra_q[rows, :] = parts_q[0] + parts_q[1]
        extra_v[rows, :] = parts_v[0] + parts_v[1]

    def project_key():
        key[...] = dot_nn(tokens[...], weight(1)).astype(NARROW)

    def project_query():
        total = dot_nn(tokens[...], weight(0)) + row(lin_biases, 0) + row(scale_b, 0) * extra_q[...]
        query[...] = (total * HEAD ** (-0.5)).astype(NARROW)

    def project_value():
        total = dot_nn(tokens[...], weight(2)) + row(lin_biases, 1) + row(scale_b, 1) * extra_v[...]
        value[...] = total.astype(NARROW)

    def head_cols(j):
        return pl.ds(pl.multiple_of(j * 128, 128), 128)

    first_half = lax.broadcasted_iota(jnp.int32, (256, 128), 1) < HEAD

    def attend_pair(it):
        seq, j = it // 6, lax.rem(it, 6)
        rows, cols = rows_of(seq), head_cols(j)
        q_pair, k_pair, v_pair = query[rows, cols], key[rows, cols], value[rows, cols]
        zero = jnp.zeros_like(q_pair)
        parts = []
        for half in range(2):
            mine_here = first_half if half == 0 else jnp.logical_not(first_half)
            scores = dot_nt(jnp.where(mine_here, q_pair, zero), k_pair) + same[seq]
            peak = jnp.max(scores, axis=-1, keepdims=True)
            exponent = jnp.exp(scores - peak)
            total = jnp.sum(exponent, axis=-1, keepdims=True)
            soft = (exponent * (1.0 / total)).astype(NARROW)
            probs[it * 2 + half] = soft
            parts.append(dot_nn(soft, v_pair))
        context[rows, cols] = jnp.where(first_half, parts[0], parts[1]).astype(NARROW)

    def close_attention(i):
        rows = rows_of(i)
        attended = dot_nn(context[rows, :], weight(3)) + row(lin_biases, 2)
        normed, inverse = standardise(tokens[rows, :].astype(WIDE) + attended)
        normed_one[rows, :] = normed
        inverse_one[rows, :] = inverse
        scaled = normed * row(norm_gains, 0) + row(norm_biases, 0)
        narrow_one[rows, :] = scaled.astype(NARROW)
        resid[rows, :] = scaled + row(lin_biases, 3)

    def hidden_cols(plane):
        return pl.ds(pl.multiple_of(plane * 768, 768), 768)

    def inner_block(it):
        turn, i = it // 2, lax.rem(it, 2)
        plane = nearest(z, turn)
        rows, cols = rows_of(i), hidden_cols(plane)
        block = dot_nt(narrow_one[rows, :], inner_t[plane].reshape(768, 768))
        block = block + bias_row[0:1, cols]
        below = 0.5 + 0.5 * lax.erf(block * 0.7071067811865476)
        hidden[rows, cols] = (block * below).astype(NARROW)
        slope[rows, cols] = (below + block * jnp.exp(-0.5 * block * block) * 0.3989422804014327).astype(NARROW)

    def branch_block(turn):
        plane = nearest(z, turn)
        resid[...] += dot_nn(hidden[:, hidden_cols(plane)], branch_w[plane].reshape(768, 768))

    def attend(it):
        attend_pair(2 * it)
        attend_pair(2 * it + 1)

    bodies = {
        "adapters": (2, adapters),
        "project_key": (1, lambda i: project_key()),
        "project_query": (1, lambda i: project_query()),
        "project_value": (1, lambda i: project_value()),
        "attend": (6, attend),
        "close": (2, close_attention),
        "inner": (8, inner_block),
        "branch": (4, branch_block),
    }

    def take_step(step):
        if step[0] == "scales":
            bias_row[...] = ffn_bias[...].astype(WIDE).reshape(1, -1)
            segments(0)
            segments(1)
            scale_copy.wait()
        else:
            gather(*step)

    at = 0
    while at < len(SCHEDULE):
        name = SCHEDULE[at][0]
        if name not in bodies:
            take_step(SCHEDULE[at])
            at += 1
            continue
        count, body = bodies[name]
        between = {}
        done = 0
        while done < count - 1:
            at += 1
            if SCHEDULE[at][0] == name:
                done += 1
            else:
                between.setdefault(done + 1, []).append(SCHEDULE[at])
        at += 1
        if count == 1:
            body(0)
        else:

            @pl.loop(0, count)
            def _(i):
                steps_at(i, between)
                body(i)

    @pl.loop(0, 2)
    def _(i):
        rows = rows_of(i)
        normed, inverse = standardise(resid[rows, :])
        gain = row(norm_gains, 1)
        out_stage[rows, :] = (normed * gain + row(norm_biases, 1)).astype(NARROW)
        grad = standardise_back(normed, inverse, cotangent[rows, :].astype(WIDE) * gain)
        resid[rows, :] = grad
        narrow_one[rows, :] = grad.astype(NARROW)

    out_copy = pltpu.make_async_copy(out_stage, output, local_sems.at[0])
    out_copy.start()

    @pl.loop(0, 4)
    def _(plane):
        cols = hidden_cols(plane)
        for i in range(2):
            rows = pl.ds(i * 256, 256)
            grad = dot_nt(narrow_one[rows, :], branch_w[plane].reshape(768, 768)).astype(NARROW)
            grad = (slope[rows, cols].astype(WIDE) * grad.astype(WIDE)).astype(NARROW)
            resid[rows, :] += dot_nn(grad, inner_t[plane].reshape(768, 768))

    @pl.loop(0, 2)
    def _(i):
        rows = rows_of(i)
        grad = standardise_back(normed_one[rows, :], inverse_one[rows, :], resid[rows, :] * row(norm_gains, 0))
        resid[rows, :] = grad
        narrow_one[rows, :] = dot_nt(grad.astype(NARROW), weight(3)).astype(NARROW)

    def attend_back(it):
        seq, j = it // 6, lax.rem(it, 6)
        rows, cols = rows_of(seq), head_cols(j)
        q_pair, k_pair, v_pair, grad = query[rows, cols], key[rows, cols], value[rows, cols], narrow_one[rows, cols]
        zero = jnp.zeros_like(grad)
        parts_q, parts_k, parts_v = [], [], []
        for half in range(2):
            mine_here = first_half if half == 0 else jnp.logical_not(first_half)
            soft = probs[it * 2 + half]
            wide = soft.astype(WIDE)
            grad_soft = dot_nt(jnp.where(mine_here, grad, zero), v_pair)
            inner_sum = jnp.sum(grad_soft * wide, axis=-1, keepdims=True)
            grad_scores = (wide * (grad_soft - inner_sum)).astype(NARROW)
            parts_v.append(dot_tn(soft, grad))
            parts_q.append(dot_nn(grad_scores, k_pair))
            parts_k.append(dot_tn(grad_scores, q_pair))
        query[rows, cols] = (jnp.where(first_half, parts_q[0], parts_q[1]) * HEAD ** (-0.5)).astype(NARROW)
        key[rows, cols] = jnp.where(first_half, parts_k[0], parts_k[1]).astype(NARROW)
        value[rows, cols] = jnp.where(first_half, parts_v[0], parts_v[1]).astype(NARROW)

    @pl.loop(0, 6)
    def _(it):
        attend_back(2 * it)
        attend_back(2 * it + 1)

    plane_sums[spot] = jnp.zeros((4, 1024), WIDE)
    low_grad = hidden

    @pl.loop(0, 2)
    def _(i):
        rows = rows_of(i)
        grad_q, grad_v = query[rows, :].astype(WIDE), value[rows, :].astype(WIDE)
        plane_sums[spot, 2:3, 0:768] += jnp.sum(extra_q[rows, :] * grad_q, axis=0, keepdims=True)
        plane_sums[spot, 3:4, 0:768] += jnp.sum(extra_v[rows, :] * grad_v, axis=0, keepdims=True)
        grad_q = (row(scale_b, 0) * grad_q).astype(NARROW)
        grad_v = (row(scale_b, 1) * grad_v).astype(NARROW)
        for h in range(2):
            half = slice(h * 512, (h + 1) * 512)
            scaled_q, scaled_v = dot_nn(grad_q, up(h)), dot_nn(grad_v, up(h))
            plane_sums[spot, 0:1, half] += jnp.sum(low[rows, half] * scaled_q, axis=0, keepdims=True)
            plane_sums[spot, 1:2, half] += jnp.sum(low[rows, half] * scaled_v, axis=0, keepdims=True)
            total = scales[h, 0:1, :].astype(WIDE) * scaled_q + scales[h, 1:2, :].astype(WIDE) * scaled_v
            low_grad[rows, half] = total.astype(NARROW)

    def plane_copy(turn, slot):
        return pltpu.make_async_remote_copy(
            plane_sums.at[slot],
            plane_sums.at[slot],
            sum_sems.at[1 + turn],
            sum_sems.at[9 + slot],
            device_id=in_plane(turn)[1],
            device_id_type=MESH_IDS,
        )

    def line_copy(turn, slot):
        return pltpu.make_async_remote_copy(
            line_sums.at[slot],
            line_sums.at[slot],
            sum_sems.at[16 + turn],
            sum_sems.at[20 + slot],
            device_id=in_line(turn)[1],
            device_id_type=MESH_IDS,
        )

    def input_rows(i):
        rows = slice(i * 256, (i + 1) * 256)
        total = resid[rows, :] + dot_nt(query[rows, :], weight(0))
        total = total + dot_nt(key[rows, :], weight(1))
        total = total + dot_nt(value[rows, :], weight(2))
        for h in range(2):
            total = total + dot_nt(low_grad[rows, h * 512 : (h + 1) * 512], down_t(h))
        grad_stage[rows, :] = total.astype(NARROW)
        return pltpu.make_async_copy(grad_stage.at[rows, :], input_grad.at[rows, :], local_sems.at[1 + i])

    for turn in range(1, PLANE):
        plane_copy(turn, spot).start()
    grad_copies = [input_rows(0)]
    grad_copies[0].start()
    for turn in range(1, PLANE):
        plane_copy(turn, in_plane(turn)[0]).wait_recv()
    total = plane_sums[0]
    for other in range(1, PLANE):
        total = total + plane_sums[other]
    line_sums[z] = total
    for turn in range(1, LINE):
        line_copy(turn, z).start()
    grad_copies.append(input_rows(1))
    grad_copies[1].start()
    for turn in range(1, LINE):
        line_copy(turn, in_line(turn)[0]).wait_recv()
    cols = pl.ds(pl.multiple_of(x * 512, 512), 512)
    total_d, total_b = line_sums[0, 0:2, cols], line_sums[0, 2:4, 0:768]
    for other in range(1, LINE):
        total_d = total_d + line_sums[other, 0:2, cols]
        total_b = total_b + line_sums[other, 2:4, 0:768]
    d_grad[...] = total_d * grad_scale
    b_grad[...] = total_b * grad_scale

    for turn in range(1, PLANE):
        plane_copy(turn, spot).wait_send()
    for turn in range(1, LINE):
        line_copy(turn, z).wait_send()
    for g in range(len(GROUPS)):
        gather("finish", g)
    out_copy.wait()
    for copy in grad_copies:
        copy.wait()


def fused_layer(
    tokens,
    cotangent,
    seg_lengths,
    attn_weights,
    out_weight,
    ffn_in,
    ffn_out,
    lin_biases,
    ffn_bias,
    norm_gains,
    norm_biases,
    shared_down,
    shared_up,
    scale_d,
    scale_b,
):
    rows, width = tokens.shape[0] * tokens.shape[1] * tokens.shape[2], tokens.shape[3]
    devices = lax.axis_size("dp") * lax.axis_size("rank")
    in_vmem, anywhere = pl.BlockSpec(memory_space=pltpu.VMEM), pl.BlockSpec(memory_space=pl.ANY)
    in_smem = pl.BlockSpec(memory_space=pltpu.SMEM)
    shapes = [(4, 2, 2, 2) + lead + (cols,) for lead, cols, _ in GROUPS]
    flat = (rows, width)
    scratch = [pltpu.VMEM(shape, NARROW) for shape in shapes] + [
        pltpu.VMEM((2, 2, 512), NARROW),
        pltpu.VMEM((2, 256, 256), WIDE),
        pltpu.VMEM((rows, 1024), WIDE),
        pltpu.VMEM(flat, WIDE),
        pltpu.VMEM(flat, WIDE),
        pltpu.VMEM(flat, NARROW),
        pltpu.VMEM(flat, NARROW),
        pltpu.VMEM(flat, NARROW),
        pltpu.VMEM((24, 256, 256), NARROW),
        pltpu.VMEM(flat, NARROW),
        pltpu.VMEM(flat, WIDE),
        pltpu.VMEM((rows, 1), WIDE),
        pltpu.VMEM(flat, WIDE),
        pltpu.VMEM(flat, NARROW),
        pltpu.VMEM((rows, 3072), NARROW),
        pltpu.VMEM((rows, 3072), NARROW),
        pltpu.VMEM(flat, NARROW),
        pltpu.VMEM(flat, NARROW),
        pltpu.VMEM((PLANE, 4, 1024), WIDE),
        pltpu.VMEM((LINE, 4, 1024), WIDE),
        pltpu.VMEM((1, 3072), WIDE),
        pltpu.SemaphoreType.DMA((len(GROUPS), SEND_SLOTS)),
        pltpu.SemaphoreType.DMA((len(GROUPS), RECV_SLOTS)),
        pltpu.SemaphoreType.DMA((7,)),
        pltpu.SemaphoreType.DMA((24,)),
    ]
    output, input_grad, d_grad, b_grad = pl.pallas_call(
        functools.partial(layer_kernel, 1.0 / math.sqrt(rows * devices)),
        out_shape=(
            jax.ShapeDtypeStruct(flat, NARROW),
            jax.ShapeDtypeStruct(flat, NARROW),
            jax.ShapeDtypeStruct((2, 512), WIDE),
            jax.ShapeDtypeStruct((2, 768), WIDE),
        ),
        in_specs=[in_vmem, in_vmem, in_smem]
        + [anywhere] * 4
        + [in_vmem] * 4
        + [anywhere] * 3
        + [in_vmem],
        out_specs=(anywhere, anywhere, in_vmem, in_vmem),
        scratch_shapes=scratch,
        compiler_params=pltpu.CompilerParams(
            collective_id=0, has_side_effects=True, vmem_limit_bytes=61 << 20
        ),
    )(
        tokens.reshape(flat),
        cotangent.reshape(flat),
        seg_lengths.reshape(-1, seg_lengths.shape[-1]),
        attn_weights,
        out_weight,
        ffn_in.T,
        ffn_out,
        lin_biases,
        ffn_bias,
        norm_gains,
        norm_biases,
        shared_down.T,
        shared_up,
        scale_d,
        scale_b,
    )
    return output.reshape(tokens.shape), input_grad.reshape(tokens.shape), d_grad, b_grad


def gather_weights(attn_weights, out_weight, ffn_in, ffn_out, shared_down, shared_up):
    down_local = lax.all_gather(shared_down, "dp", axis=1, tiled=True)
    up_local = lax.all_gather(shared_up, "dp", axis=0, tiled=True)
    return (
        lax.all_gather(attn_weights, ("dp", "rank"), axis=1, tiled=True),
        lax.all_gather(out_weight, ("dp", "rank"), axis=0, tiled=True),
        lax.all_gather(ffn_in, ("dp", "rank"), axis=1, tiled=True),
        lax.all_gather(ffn_out, ("dp", "rank"), axis=0, tiled=True),
        lax.all_gather(down_local, "rank", axis=0, tiled=True),
        lax.all_gather(up_local, "rank", axis=1, tiled=True),
    )


def per_device(
    tokens,
    cotangent,
    seg_lengths,
    attn_weights,
    out_weight,
    ffn_in,
    ffn_out,
    lin_biases,
    ffn_bias,
    norm_gains,
    norm_biases,
    shared_down,
    shared_up,
    scale_d,
    scale_b,
):
    micro_count, seq_count, length_rows, model_width = tokens.shape
    head_count = model_width // HEAD
    out_shape = tokens.shape
    seq_count = micro_count * seq_count
    row_count = seq_count * length_rows
    head_shape = (seq_count, length_rows, head_count, HEAD)
    float_wide = jnp.float32
    narrow = jnp.bfloat16
    attn_full, output_full, inner_full, branch_full, down_use, up_use = gather_weights(
        attn_weights, out_weight, ffn_in, ffn_out, shared_down, shared_up
    )
    scales_use = lax.all_gather(scale_d, "rank", axis=1, tiled=True)
    rank_cols = scales_use.shape[1]
    sum_d = jnp.zeros((2, rank_cols), float_wide)
    sum_b = jnp.zeros((2, model_width), float_wide)
    outputs = []
    input_grads = []
    for micro_step in range(1):
        token_rows = tokens.reshape(row_count, model_width)
        same_segment = segment_match(seg_lengths.reshape(seq_count, -1), length_rows)
        lowrank = jnp.einsum("rd,kd->rk", token_rows, down_use, preferred_element_type=float_wide)
        scaled = (scales_use[:, None, :] * lowrank[None]).astype(narrow)
        adapted = jnp.concatenate(
            [
                jnp.einsum("rk,dk->rd", scaled[0], up_use, preferred_element_type=float_wide),
                jnp.einsum("rk,dk->rd", scaled[1], up_use, preferred_element_type=float_wide),
            ],
            axis=1,
        )
        extra_query = adapted[:, :model_width]
        extra_value = adapted[:, model_width:]
        query_rows = (
            jnp.dot(token_rows, attn_full[0], preferred_element_type=float_wide)
            + lin_biases[0]
            + scale_b[0] * extra_query
        ).astype(narrow)
        key_rows = jnp.dot(token_rows, attn_full[1], preferred_element_type=float_wide).astype(
            narrow
        )
        value_rows = (
            jnp.dot(token_rows, attn_full[2], preferred_element_type=float_wide)
            + lin_biases[1]
            + scale_b[1] * extra_value
        ).astype(narrow)
        query_heads = query_rows.reshape(head_shape)
        key_heads = key_rows.reshape(head_shape)
        value_heads = value_rows.reshape(head_shape)
        context, log_total = attend(query_heads, key_heads, value_heads, same_segment)
        attended = (
            jnp.dot(
                context.reshape(row_count, model_width),
                output_full,
                preferred_element_type=float_wide,
            )
            + lin_biases[2]
        )
        resid_one = token_rows.astype(float_wide) + attended
        normed_one = layer_norm(resid_one, norm_gains[0], norm_biases[0])
        inner_pre = (
            jnp.dot(normed_one.astype(narrow), inner_full, preferred_element_type=float_wide)
            + ffn_bias
        )
        hidden = gelu_exact(inner_pre).astype(narrow)
        branch = jnp.dot(hidden, branch_full, preferred_element_type=float_wide) + lin_biases[3]
        resid_two = normed_one + branch
        outputs.append(
            layer_norm(resid_two, norm_gains[1], norm_biases[1])
            .astype(narrow)
            .reshape(out_shape)
        )
        grad_out = cotangent.reshape(row_count, model_width).astype(float_wide)
        grad_two = norm_back(resid_two, norm_gains[1], norm_biases[1], grad_out)
        grad_hidden = jnp.einsum(
            "rd,fd->rf", grad_two.astype(narrow), branch_full, preferred_element_type=float_wide
        ).astype(narrow)
        grad_inner = gelu_back(inner_pre, grad_hidden.astype(float_wide)).astype(narrow)
        grad_normed = grad_two + jnp.einsum(
            "rf,df->rd", grad_inner, inner_full, preferred_element_type=float_wide
        )
        grad_one = norm_back(resid_one, norm_gains[0], norm_biases[0], grad_normed)
        grad_attended = grad_one.astype(narrow)
        grad_context = jnp.einsum(
            "ro,io->ri", grad_attended, output_full, preferred_element_type=float_wide
        ).astype(narrow)
        grad_query, grad_keys, grad_values = attend_back(
            query_heads,
            key_heads,
            value_heads,
            same_segment,
            log_total,
            grad_context.reshape(head_shape),
        )
        query_grad = grad_query.reshape(row_count, model_width).astype(narrow)
        key_grad = grad_keys.reshape(row_count, model_width).astype(narrow)
        value_grad = grad_values.reshape(row_count, model_width).astype(narrow)
        grad_input = grad_one + jnp.einsum(
            "ro,io->ri", query_grad, attn_full[0], preferred_element_type=float_wide
        )
        grad_input = grad_input + jnp.einsum(
            "ro,io->ri", key_grad, attn_full[1], preferred_element_type=float_wide
        )
        grad_input = grad_input + jnp.einsum(
            "ro,io->ri", value_grad, attn_full[2], preferred_element_type=float_wide
        )
        query_grad_wide = query_grad.astype(float_wide)
        value_grad_wide = value_grad.astype(float_wide)
        sum_b = sum_b + jnp.stack(
            [
                jnp.sum(extra_query * query_grad_wide, axis=0),
                jnp.sum(extra_value * value_grad_wide, axis=0),
            ]
        )
        grad_extra = jnp.concatenate(
            [
                (scale_b[0] * query_grad_wide).astype(narrow),
                (scale_b[1] * value_grad_wide).astype(narrow),
            ],
            axis=1,
        )
        grad_scaled = jnp.concatenate(
            [
                jnp.dot(grad_extra[:, :model_width], up_use, preferred_element_type=float_wide),
                jnp.dot(grad_extra[:, model_width:], up_use, preferred_element_type=float_wide),
            ],
            axis=1,
        )
        grad_scaled_query = grad_scaled[:, :rank_cols]
        grad_scaled_value = grad_scaled[:, rank_cols:]
        sum_d = sum_d + jnp.stack(
            [
                jnp.sum(lowrank * grad_scaled_query, axis=0),
                jnp.sum(lowrank * grad_scaled_value, axis=0),
            ]
        )
        grad_lowrank = (
            scales_use[0] * grad_scaled_query + scales_use[1] * grad_scaled_value
        ).astype(narrow)
        grad_from_adapter = jnp.dot(grad_lowrank, down_use, preferred_element_type=float_wide)
        input_grads.append(
            (grad_input + grad_from_adapter)
            .astype(narrow)
            .reshape(out_shape)
        )
    grad_scale = 1.0 / math.sqrt(
        row_count * lax.axis_size("dp") * lax.axis_size("rank")
    )
    total_d, total_b = lax.psum((sum_d, sum_b), ("dp", "rank"))
    local_cols = scale_d.shape[1]
    total_d = lax.dynamic_slice_in_dim(total_d, lax.axis_index("rank") * local_cols, local_cols, 1)
    return (outputs[0], input_grads[0], total_d * grad_scale, total_b * grad_scale)


def solution(mesh):
    return jax.shard_map(
        fused_layer if (mesh.shape["dp"], mesh.shape["rank"]) == (16, 2) else per_device,
        mesh=mesh,
        in_specs=(
            P(None, ("dp", "rank"), None, None),
            P(None, ("dp", "rank"), None, None),
            P(None, ("dp", "rank"), None),
            P(None, ("dp", "rank"), None),
            P(("dp", "rank"), None),
            P(None, ("dp", "rank")),
            P(("dp", "rank"), None),
            P(),
            P(),
            P(),
            P(),
            P("rank", "dp"),
            P("dp", "rank"),
            P(None, "rank"),
            P(),
        ),
        out_specs=(
            P(None, ("dp", "rank"), None, None),
            P(None, ("dp", "rank"), None, None),
            P(None, "rank"),
            P(),
        ),
        check_vma=False,
    )
```

```python
import functools
import math

import jax
import jax.numpy as jnp
from jax import lax
from jax.experimental import pallas as pl
from jax.experimental.pallas import tpu as pltpu
from jax.sharding import PartitionSpec as P

HEAD = 64


eps_norm = 1e-05
neg_big = -1000000000.0


def layer_norm(resid, norm_gain, norm_shift):
    row_mean = jnp.mean(resid, axis=-1, keepdims=True)
    centred = resid - row_mean
    variance = jnp.mean(centred * centred, axis=-1, keepdims=True)
    return centred * lax.rsqrt(variance + eps_norm) * norm_gain + norm_shift


def norm_back(resid, norm_gain, norm_shift, grad_normed):

    def forward_norm(values_in):
        return layer_norm(values_in, norm_gain, norm_shift)

    pullback = jax.vjp(forward_norm, resid)[1]
    return pullback(grad_normed)[0]


def gelu_exact(values_in):
    return jax.nn.gelu(values_in, approximate=False)


def gelu_back(inner_pre, grad_hidden):
    pullback = jax.vjp(gelu_exact, inner_pre)[1]
    return pullback(grad_hidden)[0]


def segment_match(lengths, length_rows):
    cumulative = jnp.cumsum(lengths, axis=-1)
    places = jnp.arange(length_rows, dtype=jnp.int32)
    labels = jnp.sum((places[None, :, None] >= cumulative[:, None, :]).astype(jnp.int32), axis=-1)
    return labels[:, :, None] == labels[:, None, :]


def masked_scores(query_heads, key_heads, same_segment):
    scores = jnp.einsum(
        "sqhe,skhe->shqk", query_heads, key_heads, preferred_element_type=jnp.float32
    ) * HEAD ** (-0.5)
    return jnp.where(same_segment[:, None], scores, neg_big)


def attend(query_heads, key_heads, value_heads, same_segment):
    scores = masked_scores(query_heads, key_heads, same_segment)
    row_peak = jnp.max(scores, axis=-1, keepdims=True)
    exponent = jnp.exp(scores - row_peak)
    row_total = jnp.sum(exponent, axis=-1, keepdims=True)
    weights_soft = (exponent / row_total).astype(jnp.bfloat16)
    context = jnp.einsum(
        "shqk,skhe->sqhe", weights_soft, value_heads, preferred_element_type=jnp.float32
    )
    return (context.astype(jnp.bfloat16), row_peak + jnp.log(row_total))


def attend_back(query_heads, key_heads, value_heads, same_segment, log_total, grad_context):
    scores = masked_scores(query_heads, key_heads, same_segment)
    weights_soft = jnp.exp(scores - log_total)
    grad_values = jnp.einsum(
        "shqk,sqhe->skhe",
        weights_soft.astype(jnp.bfloat16),
        grad_context,
        preferred_element_type=jnp.float32,
    )
    grad_weights = jnp.einsum(
        "sqhe,skhe->shqk", grad_context, value_heads, preferred_element_type=jnp.float32
    )
    inner_sum = jnp.sum(grad_weights * weights_soft, axis=-1, keepdims=True)
    grad_scores = (weights_soft * (grad_weights - inner_sum)).astype(jnp.bfloat16)
    grad_query = jnp.einsum(
        "shqk,skhe->sqhe", grad_scores, key_heads, preferred_element_type=jnp.float32
    ) * HEAD ** (-0.5)
    grad_keys = jnp.einsum(
        "shqk,sqhe->skhe", grad_scores, query_heads, preferred_element_type=jnp.float32
    ) * HEAD ** (-0.5)
    return (grad_query, grad_keys, grad_values)


ALL = slice(None)
MESH_IDS = pl.DeviceIdType.MESH
WIDE = jnp.float32
NARROW = jnp.bfloat16
GROUPS = (((2, 48), 512, 256), ((4, 24), 768, 512), ((96,), 768, 384), ((96,), 768, 512))
VERA, SQUARE, INNER, BRANCH = range(4)
SCHEDULE = (
    ("own", VERA),
    ("own", SQUARE),
    ("pair", VERA),
    ("pair", SQUARE),
    ("line_b", VERA, 1),
    ("line_b", SQUARE, 1),
    ("line_a", VERA, 1),
    ("cross", VERA, 1),
    ("cross", SQUARE, 0),
    ("own", INNER),
    ("line_b", VERA, 2),
    ("line_a", SQUARE, 1),
    ("cross", SQUARE, 1),
    ("cross", VERA, 0),
    ("line_b", VERA, 3),
    ("cross", VERA, 2),
    ("line_a", VERA, 2),
    ("line_b", SQUARE, 2),
    ("pair", INNER),
    ("cross", VERA, 3),
    ("cross", SQUARE, 2),
    ("hand_on", VERA, 2),
    ("line_a", SQUARE, 2),
    ("cross", INNER, 0),
    ("line_a", VERA, 3),
    ("hand_on", SQUARE, 0),
    ("hand_on", VERA, 0),
    ("hand_on", SQUARE, 2),
    ("line_b", SQUARE, 3),
    ("own", BRANCH),
    ("hand_on", VERA, 3),
    ("cross", SQUARE, 3),
    ("hand_on", VERA, 1),
    ("hand_on", SQUARE, 1),
    ("line_b", INNER, 1),
    ("line_a", SQUARE, 3),
    ("line_b", BRANCH, 1),
    ("hand_on", INNER, 0),
    ("line_b", INNER, 2),
    ("line_a", INNER, 1),
    ("take", VERA, 0),
    ("take", VERA, 1),
    ("take", SQUARE, 2),
    ("take", VERA, 3),
    ("take", INNER, 0),
    ("take", SQUARE, 1),
    ("take", SQUARE, 0),
    ("take", VERA, 2),
    ("line_b", BRANCH, 2),
    ("scales",),
    ("adapters", 0),
    ("cross", INNER, 2),
    ("hand_on", SQUARE, 3),
    ("adapters", 1),
    ("cross", INNER, 1),
    ("pair", BRANCH),
    ("take", SQUARE, 3),
    ("project_key", 0),
    ("line_a", INNER, 2),
    ("project_query", 0),
    ("project_value", 0),
    ("cross", BRANCH, 0),
    ("attend", 0),
    ("line_b", INNER, 3),
    ("attend", 1),
    ("attend", 2),
    ("line_a", BRANCH, 1),
    ("line_b", BRANCH, 3),
    ("attend", 3),
    ("hand_on", INNER, 1),
    ("attend", 4),
    ("cross", INNER, 3),
    ("hand_on", INNER, 2),
    ("line_a", INNER, 3),
    ("attend", 5),
    ("hand_on", BRANCH, 0),
    ("cross", BRANCH, 1),
    ("cross", BRANCH, 2),
    ("take", INNER, 1),
    ("close", 0),
    ("line_a", BRANCH, 2),
    ("close", 1),
    ("inner", 0),
    ("cross", BRANCH, 3),
    ("inner", 1),
    ("hand_on", INNER, 3),
    ("inner", 2),
    ("take", INNER, 2),
    ("inner", 3),
    ("line_a", BRANCH, 3),
    ("hand_on", BRANCH, 1),
    ("inner", 4),
    ("hand_on", BRANCH, 2),
    ("inner", 5),
    ("take", INNER, 3),
    ("inner", 6),
    ("take", BRANCH, 0),
    ("take", BRANCH, 1),
    ("inner", 7),
    ("branch", 0),
    ("hand_on", BRANCH, 3),
    ("take", BRANCH, 2),
    ("branch", 1),
    ("branch", 2),
    ("take", BRANCH, 3),
    ("branch", 3),
)
SEND_SLOTS = 39
RECV_SLOTS = 25
LINE = 4
PLANE = 8


def nearest(z, turn):
    upper = z // 2
    inner = z * (1 - upper) + (3 - z) * upper
    plane = turn + inner * (1 - 2 * turn) * (1 - turn // 2)
    return plane * (1 - upper) + (3 - plane) * upper


class Relay:
    def __init__(self, buffers, send_sems, recv_sems):
        self.buffers, self.send_sems, self.recv_sems = buffers, send_sems, recv_sems
        place = lax.axis_index("dp")
        self.x = lax.axis_index("rank")
        self.z, self.y, self.c = place // 4, (place // 2) % 2, place % 2

    def device(self, z, y, c, x):
        return {"dp": z * 4 + y * 2 + c, "rank": x}

    def neighbour(self, c, which):
        z, y, x = self.z, self.y, self.x
        if which == "s":
            return self.device(z, y, 1 - c, x)
        if which == "u":
            return self.device(z + 1, y, c, x)
        if which == "d":
            return self.device(z - 1, y, c, x)
        if (which == "p") == (c == 0):
            return self.device(z, y, c, 1 - x)
        return self.device(z, 1 - y, c, x)

    def view(self, g, c, plane, p, q, part):
        lead, cols, split = GROUPS[g]
        window = {"A": pl.ds(0, split), "B": pl.ds(split, cols - split), "F": pl.ds(0, cols)}[part]
        place = (plane, q, c, p) if c == 0 else (plane, p, c, q)
        return self.buffers[g].at[place + (ALL,) * len(lead) + (window,)]

    def copy(self, g, c, plane, p, q, part, to, send, recv):
        block = self.view(g, c, plane, p, q, part)
        return pltpu.make_async_remote_copy(
            block,
            block,
            self.send_sems.at[g, send],
            self.recv_sems.at[g, recv],
            device_id=self.neighbour(c, to),
            device_id_type=MESH_IDS,
        )


class Steps:
    def __init__(self, relay, g, c):
        self.relay, self.g, self.c = relay, g, c
        self.z = relay.z
        self.p, self.q = (relay.x, relay.y) if c == 0 else (relay.y, relay.x)
        self.closing = False

    def send(self, cond, *where):
        def act():
            copy = self.relay.copy(self.g, self.c, *where)
            if self.closing:
                copy.wait_send()
            else:
                copy.start()

        if cond is None:
            act()
        else:
            pl.when(cond)(act)

    def finish(self):
        self.closing = True
        self.own()
        self.pair()
        for far in (1, 2, 3):
            self.line_a(far)
            self.line_b(far)
        for turn in range(4):
            self.cross(turn)
            self.hand_on(turn)

    def got(self, *where):
        if not self.closing:
            self.relay.copy(self.g, self.c, *where).wait_recv()

    def own(self):
        z, p, q = self.z, self.p, self.q
        self.send(None, z, p, q, "A", "p", 0, 0)
        self.send(z < 3, z, p, q, "B", "u", 1, 9 + z)
        self.send(z > 0, z, p, q, "B", "d", 2, 9 + z)
        self.send(None, z, p, q, "B", "p", 3, 13 + z)

    def pair(self):
        z, p, q = self.z, self.p, self.q
        self.got(z, 1 - p, q, "A", "p", 0, 0)
        self.send(z < 3, z, ALL, q, "A", "u", 4, 1 + z)
        self.send(z > 0, z, ALL, q, "A", "d", 5, 1 + z)
        self.send(None, z, ALL, q, "A", "q", 6, 5 + z)

    def line(self, part, far):
        z, p, q = self.z, self.p, self.q
        for side in (0, 1):
            plane = z - far if side == 0 else z + far
            cond = plane >= 0 if side == 0 else plane <= 3
            more = z < 3 if side == 0 else z > 0
            to = "u" if side == 0 else "d"
            slot = 6 * far + 1 + 3 * side
            if part == "A":

                @pl.when(cond)
                def _():
                    self.got(plane, ALL, q, "A", to, 0, 1 + plane)

                if far < 3:
                    self.send(jnp.logical_and(cond, more), plane, ALL, q, "A", to, slot, 1 + plane)
                self.send(cond, plane, ALL, q, "A", "q", slot + 1, 5 + plane)
            else:

                @pl.when(cond)
                def _():
                    self.got(plane, p, q, "B", to, 0, 9 + plane)

                if far < 3:
                    self.send(jnp.logical_and(cond, more), plane, p, q, "B", to, slot + 2, 9 + plane)
                self.send(cond, plane, p, q, "B", "p", 23 + 2 * far + side, 13 + plane)

    def line_a(self, far):
        self.line("A", far)

    def line_b(self, far):
        self.line("B", far)

    def cross(self, turn):
        plane = nearest(self.z, turn)
        self.got(plane, 1 - self.p, self.q, "B", "p", 0, 13 + plane)
        self.send(None, plane, ALL, self.q, "B", "q", 31 + turn, 17 + plane)

    def hand_on(self, turn):
        plane = nearest(self.z, turn)
        self.got(plane, ALL, 1 - self.q, "A", "q", 0, 5 + plane)
        self.got(plane, ALL, 1 - self.q, "B", "q", 0, 17 + plane)
        self.send(None, plane, ALL, ALL, "F", "s", 35 + turn, 21 + plane)

    def take(self, turn):
        plane = nearest(self.z, turn)
        self.relay.copy(self.g, 1 - self.c, plane, ALL, ALL, "F", "s", 0, 21 + plane).wait_recv()


class Gather:
    def __init__(self, relay):
        self.relay = relay
        self.steps = [[Steps(relay, g, c) for g in range(len(GROUPS))] for c in (0, 1)]

    def __call__(self, name, g, *where):
        for core in (0, 1):

            @pl.when(self.relay.c == core)
            def _():
                getattr(self.steps[core][g], name)(*where)


def dot_nn(left, right):
    return jnp.dot(left, right, preferred_element_type=WIDE)


def dot_nt(left, right):
    return lax.dot_general(left, right, (((1,), (1,)), ((), ())), preferred_element_type=WIDE)


def dot_tn(left, right):
    return lax.dot_general(left, right, (((0,), (0,)), ((), ())), preferred_element_type=WIDE)


def standardise(resid):
    centred = resid - jnp.mean(resid, axis=-1, keepdims=True)
    inverse = lax.rsqrt(jnp.mean(centred * centred, axis=-1, keepdims=True) + eps_norm)
    return centred * inverse, inverse


def standardise_back(normed, inverse, grad):
    along = jnp.mean(grad * normed, axis=-1, keepdims=True)
    return inverse * (grad - jnp.mean(grad, axis=-1, keepdims=True) - normed * along)


def layer_kernel(grad_scale, *refs):
    (
        tokens_in,
        cotangent_in,
        seg_lengths,
        attn_piece,
        out_piece,
        inner_piece,
        branch_piece,
        lin_biases,
        ffn_bias,
        norm_gains,
        norm_biases,
        down_piece,
        up_piece,
        scale_d,
        scale_b,
        output,
        input_grad,
        d_grad,
        b_grad,
        vera,
        square,
        inner_t,
        branch_w,
        scales,
        same,
        low,
        extra_q,
        extra_v,
        query,
        key,
        value,
        probs,
        context,
        normed_one,
        inverse_one,
        resid,
        narrow_one,
        hidden,
        slope,
        out_stage,
        grad_stage,
        plane_sums,
        line_sums,
        bias_row,
        tokens,
        cotangent,
        send_sems,
        recv_sems,
        local_sems,
        sum_sems,
    ) = refs
    relay = Relay((vera, square, inner_t, branch_w), send_sems, recv_sems)
    gather = Gather(relay)
    z, y, c, x = relay.z, relay.y, relay.c, relay.x
    spot = c * 4 + y * 2 + x

    def in_plane(turn):
        other = lax.rem(spot + turn, PLANE)
        return other, relay.device(z, (other // 2) % 2, other // 4, other % 2)

    def in_line(turn):
        other = lax.rem(z + turn, LINE)
        return other, relay.device(other, y, c, x)

    mine = [
        pltpu.make_async_copy(up_piece, vera.at[z, y, c, x, 1], local_sems.at[0]),
        pltpu.make_async_copy(attn_piece, square.at[z, y, c, x, pl.ds(0, 3)], local_sems.at[1]),
        pltpu.make_async_copy(out_piece, square.at[z, y, c, x, 3], local_sems.at[2]),
        pltpu.make_async_copy(branch_piece, branch_w.at[z, y, c, x], local_sems.at[3]),
        pltpu.make_async_copy(scale_d, scales.at[x], local_sems.at[4]),
        pltpu.make_async_copy(inner_piece, inner_t.at[z, y, c, x], local_sems.at[5]),
        pltpu.make_async_copy(down_piece, vera.at[z, y, c, x, 0], local_sems.at[6]),
    ]
    tokens_copy = pltpu.make_async_copy(tokens_in, tokens, local_sems.at[7])
    cotangent_copy = pltpu.make_async_copy(cotangent_in, cotangent, local_sems.at[8])
    for copy in mine + [tokens_copy, cotangent_copy]:
        copy.start()
    barrier = pltpu.get_barrier_semaphore()

    def greet(device):
        pl.semaphore_signal(barrier, 1, device_id=device, device_id_type=MESH_IDS)

    greet(relay.device(z, y, 1 - c, x))
    greet(relay.device(z, y, c, 1 - x))
    greet(relay.device(z, 1 - y, c, x))

    @pl.when(z < 3)
    def _():
        greet(relay.device(z + 1, y, c, x))

    @pl.when(z > 0)
    def _():
        greet(relay.device(z - 1, y, c, x))

    for copy in mine:
        copy.wait()
    pl.semaphore_wait(barrier, 3 + jnp.where(z < 3, 1, 0) + jnp.where(z > 0, 1, 0))

    scale_copy = pltpu.make_async_remote_copy(
        scales.at[x],
        scales.at[x],
        sum_sems.at[0],
        sum_sems.at[1],
        device_id=relay.device(z, y, c, 1 - x),
        device_id_type=MESH_IDS,
    )
    scale_copy.start()

    def segments(seq):
        row_place = lax.broadcasted_iota(jnp.int32, (256, 256), 0)
        col_place = lax.broadcasted_iota(jnp.int32, (256, 256), 1)
        row_label = jnp.zeros((256, 256), jnp.int32)
        col_label = jnp.zeros((256, 256), jnp.int32)
        end = jnp.int32(0)
        for k in range(seg_lengths.shape[1]):
            end = end + seg_lengths[seq, k]
            row_label = row_label + (row_place >= end).astype(jnp.int32)
            col_label = col_label + (col_place >= end).astype(jnp.int32)
        same[seq] = jnp.where(row_label == col_label, 0.0, neg_big)

    def row(ref, k):
        return ref[k : k + 1, :].astype(WIDE)

    def rows_of(i):
        return pl.ds(pl.multiple_of(i * 256, 256), 256)

    def down_t(h):
        return vera[:, :, :, h, 0].reshape(768, 512)

    def up(h):
        return vera[:, :, :, h, 1].reshape(768, 512)

    def weight(k):
        return square[:, :, :, :, k].reshape(768, 768)

    def steps_at(i, relays):
        for k, steps in relays.items():

            @pl.when(i == k)
            def _():
                for step in steps:
                    take_step(step)

    def adapters(i):
        rows = rows_of(i)
        token_rows = tokens[rows, :]
        parts_q, parts_v = [], []
        for h in range(2):
            lowrank = dot_nn(token_rows, down_t(h))
            low[rows, h * 512 : (h + 1) * 512] = lowrank
            parts_q.append(dot_nt((scales[h, 0:1, :].astype(WIDE) * lowrank).astype(NARROW), up(h)))
            parts_v.append(dot_nt((scales[h, 1:2, :].astype(WIDE) * lowrank).astype(NARROW), up(h)))
        extra_q[rows, :] = parts_q[0] + parts_q[1]
        extra_v[rows, :] = parts_v[0] + parts_v[1]

    def project_key():
        key[...] = dot_nn(tokens[...], weight(1)).astype(NARROW)

    def project_query():
        total = dot_nn(tokens[...], weight(0)) + row(lin_biases, 0) + row(scale_b, 0) * extra_q[...]
        query[...] = (total * HEAD ** (-0.5)).astype(NARROW)

    def project_value():
        total = dot_nn(tokens[...], weight(2)) + row(lin_biases, 1) + row(scale_b, 1) * extra_v[...]
        value[...] = total.astype(NARROW)

    def head_cols(j):
        return pl.ds(pl.multiple_of(j * 128, 128), 128)

    lane = lax.broadcasted_iota(jnp.int32, (256, 128), 1)
    first_half = lane < HEAD

    def attend_pair(it):
        seq, j = it // 6, lax.rem(it, 6)
        rows, cols = rows_of(seq), head_cols(j)
        q_pair, k_pair, v_pair = query[rows, cols], key[rows, cols], value[rows, cols]
        zero = jnp.zeros_like(q_pair)
        queries = jnp.concatenate([jnp.where(first_half, q_pair, zero), jnp.where(first_half, zero, q_pair)])
        both = dot_nt(queries, k_pair)
        parts = []
        for half in range(2):
            scores = both[half * 256 : (half + 1) * 256] + same[seq]
            peak = jnp.max(scores, axis=-1, keepdims=True)
            exponent = jnp.exp(scores - peak)
            total = jnp.sum(exponent, axis=-1, keepdims=True)
            soft = (exponent * (1.0 / total)).astype(NARROW)
            probs[it * 2 + half] = soft
            parts.append(soft)
        both = dot_nn(jnp.concatenate(parts), v_pair)
        context[rows, cols] = jnp.where(first_half, both[:256], both[256:]).astype(NARROW)

    def close_attention(i):
        rows = rows_of(i)
        attended = dot_nn(context[rows, :], weight(3)) + row(lin_biases, 2)
        normed, inverse = standardise(tokens[rows, :].astype(WIDE) + attended)
        normed_one[rows, :] = normed
        inverse_one[rows, :] = inverse
        scaled = normed * row(norm_gains, 0) + row(norm_biases, 0)
        narrow_one[rows, :] = scaled.astype(NARROW)
        resid[rows, :] = scaled + row(lin_biases, 3)

    def hidden_cols(plane):
        return pl.ds(pl.multiple_of(plane * 768, 768), 768)

    def inner_block(it):
        turn, i = it // 2, lax.rem(it, 2)
        plane = nearest(z, turn)
        rows, cols = rows_of(i), hidden_cols(plane)
        block = dot_nt(narrow_one[rows, :], inner_t[plane].reshape(768, 768))
        block = block + bias_row[0:1, cols]
        below = 0.5 + 0.5 * lax.erf(block * 0.7071067811865476)
        hidden[rows, cols] = (block * below).astype(NARROW)
        slope[rows, cols] = (below + block * jnp.exp(-0.5 * block * block) * 0.3989422804014327).astype(NARROW)

    def branch_block(turn):
        plane = nearest(z, turn)
        resid[...] += dot_nn(hidden[:, hidden_cols(plane)], branch_w[plane].reshape(768, 768))

    def attend(it):
        attend_pair(2 * it)
        attend_pair(2 * it + 1)

    bodies = {
        "adapters": (2, adapters),
        "project_key": (1, lambda i: project_key()),
        "project_query": (1, lambda i: project_query()),
        "project_value": (1, lambda i: project_value()),
        "attend": (6, attend),
        "close": (2, close_attention),
        "inner": (8, inner_block),
        "branch": (4, branch_block),
    }

    def take_step(step):
        if step[0] == "scales":
            bias_row[...] = ffn_bias[...].astype(WIDE).reshape(1, -1)
            segments(0)
            segments(1)
            scale_copy.wait()
            tokens_copy.wait()
        else:
            gather(*step)

    at = 0
    while at < len(SCHEDULE):
        name = SCHEDULE[at][0]
        if name not in bodies:
            take_step(SCHEDULE[at])
            at += 1
            continue
        count, body = bodies[name]
        between = {}
        done = 0
        while done < count - 1:
            at += 1
            if SCHEDULE[at][0] == name:
                done += 1
            else:
                between.setdefault(done + 1, []).append(SCHEDULE[at])
        at += 1
        if count == 1:
            body(0)
        else:

            @pl.loop(0, count)
            def _(i):
                steps_at(i, between)
                body(i)

    cotangent_copy.wait()

    @pl.loop(0, 2)
    def _(i):
        rows = rows_of(i)
        normed, inverse = standardise(resid[rows, :])
        gain = row(norm_gains, 1)
        out_stage[rows, :] = (normed * gain + row(norm_biases, 1)).astype(NARROW)
        grad = standardise_back(normed, inverse, cotangent[rows, :].astype(WIDE) * gain)
        resid[rows, :] = grad
        narrow_one[rows, :] = grad.astype(NARROW)

    out_copy = pltpu.make_async_copy(out_stage, output, local_sems.at[0])
    out_copy.start()

    @pl.loop(0, 4)
    def _(plane):
        cols = hidden_cols(plane)
        for i in range(2):
            rows = pl.ds(i * 256, 256)
            grad = dot_nt(narrow_one[rows, :], branch_w[plane].reshape(768, 768)).astype(NARROW)
            grad = (slope[rows, cols].astype(WIDE) * grad.astype(WIDE)).astype(NARROW)
            resid[rows, :] += dot_nn(grad, inner_t[plane].reshape(768, 768))

    @pl.loop(0, 2)
    def _(i):
        rows = rows_of(i)
        grad = standardise_back(normed_one[rows, :], inverse_one[rows, :], resid[rows, :] * row(norm_gains, 0))
        resid[rows, :] = grad
        narrow_one[rows, :] = dot_nt(grad.astype(NARROW), weight(3)).astype(NARROW)

    def attend_back(it):
        seq, j = it // 6, lax.rem(it, 6)
        rows, cols = rows_of(seq), head_cols(j)
        q_pair, k_pair, v_pair, grad = query[rows, cols], key[rows, cols], value[rows, cols], narrow_one[rows, cols]
        product = grad.astype(WIDE) * context[rows, cols].astype(WIDE)
        zero = jnp.zeros_like(grad)
        grads = jnp.concatenate([jnp.where(first_half, grad, zero), jnp.where(first_half, zero, grad)])
        grad_soft = dot_nt(grads, v_pair)
        soft, grad_scores = [], []
        for half in range(2):
            mine_here = first_half if half == 0 else jnp.logical_not(first_half)
            inner_sum = jnp.sum(jnp.where(mine_here, product, 0.0), axis=-1, keepdims=True)
            soft.append(probs[it * 2 + half])
            change = grad_soft[half * 256 : (half + 1) * 256] - inner_sum
            grad_scores.append((soft[half].astype(WIDE) * change).astype(NARROW))
        grad_q = dot_nn(jnp.concatenate(grad_scores), k_pair)
        grad_k = dot_tn(jnp.concatenate(grad_scores, axis=1), q_pair)
        grad_v = dot_tn(jnp.concatenate(soft, axis=1), grad)
        query[rows, cols] = (jnp.where(first_half, grad_q[:256], grad_q[256:]) * HEAD ** (-0.5)).astype(NARROW)
        key[rows, cols] = jnp.where(first_half, grad_k[:256], grad_k[256:]).astype(NARROW)
        value[rows, cols] = jnp.where(first_half, grad_v[:256], grad_v[256:]).astype(NARROW)

    @pl.loop(0, 6)
    def _(it):
        attend_back(2 * it)
        attend_back(2 * it + 1)

    plane_sums[spot] = jnp.zeros((4, 1024), WIDE)
    low_grad = hidden

    @pl.loop(0, 2)
    def _(i):
        rows = rows_of(i)
        grad_q, grad_v = query[rows, :].astype(WIDE), value[rows, :].astype(WIDE)
        plane_sums[spot, 2:3, 0:768] += jnp.sum(extra_q[rows, :] * grad_q, axis=0, keepdims=True)
        plane_sums[spot, 3:4, 0:768] += jnp.sum(extra_v[rows, :] * grad_v, axis=0, keepdims=True)
        grad_q = (row(scale_b, 0) * grad_q).astype(NARROW)
        grad_v = (row(scale_b, 1) * grad_v).astype(NARROW)
        for h in range(2):
            half = slice(h * 512, (h + 1) * 512)
            scaled_q, scaled_v = dot_nn(grad_q, up(h)), dot_nn(grad_v, up(h))
            plane_sums[spot, 0:1, half] += jnp.sum(low[rows, half] * scaled_q, axis=0, keepdims=True)
            plane_sums[spot, 1:2, half] += jnp.sum(low[rows, half] * scaled_v, axis=0, keepdims=True)
            total = scales[h, 0:1, :].astype(WIDE) * scaled_q + scales[h, 1:2, :].astype(WIDE) * scaled_v
            low_grad[rows, half] = total.astype(NARROW)

    def plane_copy(turn, slot):
        return pltpu.make_async_remote_copy(
            plane_sums.at[slot],
            plane_sums.at[slot],
            sum_sems.at[1 + turn],
            sum_sems.at[9 + slot],
            device_id=in_plane(turn)[1],
            device_id_type=MESH_IDS,
        )

    def line_copy(turn, slot):
        return pltpu.make_async_remote_copy(
            line_sums.at[slot],
            line_sums.at[slot],
            sum_sems.at[16 + turn],
            sum_sems.at[20 + slot],
            device_id=in_line(turn)[1],
            device_id_type=MESH_IDS,
        )

    def input_rows(i):
        rows = slice(i * 256, (i + 1) * 256)
        total = resid[rows, :] + dot_nt(query[rows, :], weight(0))
        total = total + dot_nt(key[rows, :], weight(1))
        total = total + dot_nt(value[rows, :], weight(2))
        for h in range(2):
            total = total + dot_nt(low_grad[rows, h * 512 : (h + 1) * 512], down_t(h))
        grad_stage[rows, :] = total.astype(NARROW)
        return pltpu.make_async_copy(grad_stage.at[rows, :], input_grad.at[rows, :], local_sems.at[1 + i])

    for turn in range(1, PLANE):
        plane_copy(turn, spot).start()
    grad_copies = [input_rows(0)]
    grad_copies[0].start()
    for turn in range(1, PLANE):
        plane_copy(turn, in_plane(turn)[0]).wait_recv()
    total = plane_sums[0]
    for other in range(1, PLANE):
        total = total + plane_sums[other]
    line_sums[z] = total
    for turn in range(1, LINE):
        line_copy(turn, z).start()
    grad_copies.append(input_rows(1))
    grad_copies[1].start()
    for turn in range(1, LINE):
        line_copy(turn, in_line(turn)[0]).wait_recv()
    cols = pl.ds(pl.multiple_of(x * 512, 512), 512)
    total_d, total_b = line_sums[0, 0:2, cols], line_sums[0, 2:4, 0:768]
    for other in range(1, LINE):
        total_d = total_d + line_sums[other, 0:2, cols]
        total_b = total_b + line_sums[other, 2:4, 0:768]
    d_grad[...] = total_d * grad_scale
    b_grad[...] = total_b * grad_scale

    for turn in range(1, PLANE):
        plane_copy(turn, spot).wait_send()
    for turn in range(1, LINE):
        line_copy(turn, z).wait_send()
    for g in range(len(GROUPS)):
        gather("finish", g)
    out_copy.wait()
    for copy in grad_copies:
        copy.wait()


def settle_kernel(*refs):
    sources, targets, sems = refs[:4], refs[4:8], refs[8]
    copies = [pltpu.make_async_copy(sources[k], targets[k], sems.at[k]) for k in range(4)]
    for copy in copies:
        copy.start()
    for copy in copies:
        copy.wait()


def settle(results):
    anywhere = pl.BlockSpec(memory_space=pl.ANY)
    return pl.pallas_call(
        settle_kernel,
        out_shape=[jax.ShapeDtypeStruct(result.shape, result.dtype) for result in results],
        in_specs=[pl.BlockSpec(memory_space=pltpu.VMEM)] * 4,
        out_specs=[anywhere] * 4,
        scratch_shapes=[pltpu.SemaphoreType.DMA((4,))],
    )(*results)


def fused_layer(
    tokens,
    cotangent,
    seg_lengths,
    attn_weights,
    out_weight,
    ffn_in,
    ffn_out,
    lin_biases,
    ffn_bias,
    norm_gains,
    norm_biases,
    shared_down,
    shared_up,
    scale_d,
    scale_b,
):
    rows, width = tokens.shape[0] * tokens.shape[1] * tokens.shape[2], tokens.shape[3]
    devices = lax.axis_size("dp") * lax.axis_size("rank")
    in_vmem, anywhere = pl.BlockSpec(memory_space=pltpu.VMEM), pl.BlockSpec(memory_space=pl.ANY)
    in_smem = pl.BlockSpec(memory_space=pltpu.SMEM)
    shapes = [(4, 2, 2, 2) + lead + (cols,) for lead, cols, _ in GROUPS]
    flat = (rows, width)
    scratch = [pltpu.VMEM(shape, NARROW) for shape in shapes] + [
        pltpu.VMEM((2, 2, 512), NARROW),
        pltpu.VMEM((2, 256, 256), WIDE),
        pltpu.VMEM((rows, 1024), WIDE),
        pltpu.VMEM(flat, WIDE),
        pltpu.VMEM(flat, WIDE),
        pltpu.VMEM(flat, NARROW),
        pltpu.VMEM(flat, NARROW),
        pltpu.VMEM(flat, NARROW),
        pltpu.VMEM((24, 256, 256), NARROW),
        pltpu.VMEM(flat, NARROW),
        pltpu.VMEM(flat, WIDE),
        pltpu.VMEM((rows, 1), WIDE),
        pltpu.VMEM(flat, WIDE),
        pltpu.VMEM(flat, NARROW),
        pltpu.VMEM((rows, 3072), NARROW),
        pltpu.VMEM((rows, 3072), NARROW),
        pltpu.VMEM(flat, NARROW),
        pltpu.VMEM(flat, NARROW),
        pltpu.VMEM((PLANE, 4, 1024), WIDE),
        pltpu.VMEM((LINE, 4, 1024), WIDE),
        pltpu.VMEM((1, 3072), WIDE),
        pltpu.VMEM(flat, NARROW),
        pltpu.VMEM(flat, NARROW),
        pltpu.SemaphoreType.DMA((len(GROUPS), SEND_SLOTS)),
        pltpu.SemaphoreType.DMA((len(GROUPS), RECV_SLOTS)),
        pltpu.SemaphoreType.DMA((9,)),
        pltpu.SemaphoreType.DMA((24,)),
    ]
    results = pl.pallas_call(
        functools.partial(layer_kernel, 1.0 / math.sqrt(rows * devices)),
        out_shape=(
            jax.ShapeDtypeStruct(flat, NARROW),
            jax.ShapeDtypeStruct(flat, NARROW),
            jax.ShapeDtypeStruct((2, 512), WIDE),
            jax.ShapeDtypeStruct((2, 768), WIDE),
        ),
        in_specs=[anywhere, anywhere, in_smem]
        + [anywhere] * 4
        + [in_vmem] * 4
        + [anywhere] * 3
        + [in_vmem],
        out_specs=(anywhere, anywhere, in_vmem, in_vmem),
        scratch_shapes=scratch,
        compiler_params=pltpu.CompilerParams(
            collective_id=0, has_side_effects=True, vmem_limit_bytes=61 << 20
        ),
    )(
        tokens.reshape(flat),
        cotangent.reshape(flat),
        seg_lengths.reshape(-1, seg_lengths.shape[-1]),
        attn_weights,
        out_weight,
        ffn_in.T,
        ffn_out,
        lin_biases,
        ffn_bias,
        norm_gains,
        norm_biases,
        shared_down.T,
        shared_up,
        scale_d,
        scale_b,
    )
    output, input_grad, d_grad, b_grad = settle(results)
    return output.reshape(tokens.shape), input_grad.reshape(tokens.shape), d_grad, b_grad


def gather_weights(attn_weights, out_weight, ffn_in, ffn_out, shared_down, shared_up):
    down_local = lax.all_gather(shared_down, "dp", axis=1, tiled=True)
    up_local = lax.all_gather(shared_up, "dp", axis=0, tiled=True)
    return (
        lax.all_gather(attn_weights, ("dp", "rank"), axis=1, tiled=True),
        lax.all_gather(out_weight, ("dp", "rank"), axis=0, tiled=True),
        lax.all_gather(ffn_in, ("dp", "rank"), axis=1, tiled=True),
        lax.all_gather(ffn_out, ("dp", "rank"), axis=0, tiled=True),
        lax.all_gather(down_local, "rank", axis=0, tiled=True),
        lax.all_gather(up_local, "rank", axis=1, tiled=True),
    )


def per_device(
    tokens,
    cotangent,
    seg_lengths,
    attn_weights,
    out_weight,
    ffn_in,
    ffn_out,
    lin_biases,
    ffn_bias,
    norm_gains,
    norm_biases,
    shared_down,
    shared_up,
    scale_d,
    scale_b,
):
    micro_count, seq_count, length_rows, model_width = tokens.shape
    head_count = model_width // HEAD
    out_shape = tokens.shape
    seq_count = micro_count * seq_count
    row_count = seq_count * length_rows
    head_shape = (seq_count, length_rows, head_count, HEAD)
    float_wide = jnp.float32
    narrow = jnp.bfloat16
    attn_full, output_full, inner_full, branch_full, down_use, up_use = gather_weights(
        attn_weights, out_weight, ffn_in, ffn_out, shared_down, shared_up
    )
    scales_use = lax.all_gather(scale_d, "rank", axis=1, tiled=True)
    rank_cols = scales_use.shape[1]
    sum_d = jnp.zeros((2, rank_cols), float_wide)
    sum_b = jnp.zeros((2, model_width), float_wide)
    outputs = []
    input_grads = []
    for micro_step in range(1):
        token_rows = tokens.reshape(row_count, model_width)
        same_segment = segment_match(seg_lengths.reshape(seq_count, -1), length_rows)
        lowrank = jnp.einsum("rd,kd->rk", token_rows, down_use, preferred_element_type=float_wide)
        scaled = (scales_use[:, None, :] * lowrank[None]).astype(narrow)
        adapted = jnp.concatenate(
            [
                jnp.einsum("rk,dk->rd", scaled[0], up_use, preferred_element_type=float_wide),
                jnp.einsum("rk,dk->rd", scaled[1], up_use, preferred_element_type=float_wide),
            ],
            axis=1,
        )
        extra_query = adapted[:, :model_width]
        extra_value = adapted[:, model_width:]
        query_rows = (
            jnp.dot(token_rows, attn_full[0], preferred_element_type=float_wide)
            + lin_biases[0]
            + scale_b[0] * extra_query
        ).astype(narrow)
        key_rows = jnp.dot(token_rows, attn_full[1], preferred_element_type=float_wide).astype(
            narrow
        )
        value_rows = (
            jnp.dot(token_rows, attn_full[2], preferred_element_type=float_wide)
            + lin_biases[1]
            + scale_b[1] * extra_value
        ).astype(narrow)
        query_heads = query_rows.reshape(head_shape)
        key_heads = key_rows.reshape(head_shape)
        value_heads = value_rows.reshape(head_shape)
        context, log_total = attend(query_heads, key_heads, value_heads, same_segment)
        attended = (
            jnp.dot(
                context.reshape(row_count, model_width),
                output_full,
                preferred_element_type=float_wide,
            )
            + lin_biases[2]
        )
        resid_one = token_rows.astype(float_wide) + attended
        normed_one = layer_norm(resid_one, norm_gains[0], norm_biases[0])
        inner_pre = (
            jnp.dot(normed_one.astype(narrow), inner_full, preferred_element_type=float_wide)
            + ffn_bias
        )
        hidden = gelu_exact(inner_pre).astype(narrow)
        branch = jnp.dot(hidden, branch_full, preferred_element_type=float_wide) + lin_biases[3]
        resid_two = normed_one + branch
        outputs.append(
            layer_norm(resid_two, norm_gains[1], norm_biases[1])
            .astype(narrow)
            .reshape(out_shape)
        )
        grad_out = cotangent.reshape(row_count, model_width).astype(float_wide)
        grad_two = norm_back(resid_two, norm_gains[1], norm_biases[1], grad_out)
        grad_hidden = jnp.einsum(
            "rd,fd->rf", grad_two.astype(narrow), branch_full, preferred_element_type=float_wide
        ).astype(narrow)
        grad_inner = gelu_back(inner_pre, grad_hidden.astype(float_wide)).astype(narrow)
        grad_normed = grad_two + jnp.einsum(
            "rf,df->rd", grad_inner, inner_full, preferred_element_type=float_wide
        )
        grad_one = norm_back(resid_one, norm_gains[0], norm_biases[0], grad_normed)
        grad_attended = grad_one.astype(narrow)
        grad_context = jnp.einsum(
            "ro,io->ri", grad_attended, output_full, preferred_element_type=float_wide
        ).astype(narrow)
        grad_query, grad_keys, grad_values = attend_back(
            query_heads,
            key_heads,
            value_heads,
            same_segment,
            log_total,
            grad_context.reshape(head_shape),
        )
        query_grad = grad_query.reshape(row_count, model_width).astype(narrow)
        key_grad = grad_keys.reshape(row_count, model_width).astype(narrow)
        value_grad = grad_values.reshape(row_count, model_width).astype(narrow)
        grad_input = grad_one + jnp.einsum(
            "ro,io->ri", query_grad, attn_full[0], preferred_element_type=float_wide
        )
        grad_input = grad_input + jnp.einsum(
            "ro,io->ri", key_grad, attn_full[1], preferred_element_type=float_wide
        )
        grad_input = grad_input + jnp.einsum(
            "ro,io->ri", value_grad, attn_full[2], preferred_element_type=float_wide
        )
        query_grad_wide = query_grad.astype(float_wide)
        value_grad_wide = value_grad.astype(float_wide)
        sum_b = sum_b + jnp.stack(
            [
                jnp.sum(extra_query * query_grad_wide, axis=0),
                jnp.sum(extra_value * value_grad_wide, axis=0),
            ]
        )
        grad_extra = jnp.concatenate(
            [
                (scale_b[0] * query_grad_wide).astype(narrow),
                (scale_b[1] * value_grad_wide).astype(narrow),
            ],
            axis=1,
        )
        grad_scaled = jnp.concatenate(
            [
                jnp.dot(grad_extra[:, :model_width], up_use, preferred_element_type=float_wide),
                jnp.dot(grad_extra[:, model_width:], up_use, preferred_element_type=float_wide),
            ],
            axis=1,
        )
        grad_scaled_query = grad_scaled[:, :rank_cols]
        grad_scaled_value = grad_scaled[:, rank_cols:]
        sum_d = sum_d + jnp.stack(
            [
                jnp.sum(lowrank * grad_scaled_query, axis=0),
                jnp.sum(lowrank * grad_scaled_value, axis=0),
            ]
        )
        grad_lowrank = (
            scales_use[0] * grad_scaled_query + scales_use[1] * grad_scaled_value
        ).astype(narrow)
        grad_from_adapter = jnp.dot(grad_lowrank, down_use, preferred_element_type=float_wide)
        input_grads.append(
            (grad_input + grad_from_adapter)
            .astype(narrow)
            .reshape(out_shape)
        )
    grad_scale = 1.0 / math.sqrt(
        row_count * lax.axis_size("dp") * lax.axis_size("rank")
    )
    total_d, total_b = lax.psum((sum_d, sum_b), ("dp", "rank"))
    local_cols = scale_d.shape[1]
    total_d = lax.dynamic_slice_in_dim(total_d, lax.axis_index("rank") * local_cols, local_cols, 1)
    return (outputs[0], input_grads[0], total_d * grad_scale, total_b * grad_scale)


def solution(mesh):
    return jax.shard_map(
        fused_layer if (mesh.shape["dp"], mesh.shape["rank"]) == (16, 2) else per_device,
        mesh=mesh,
        in_specs=(
            P(None, ("dp", "rank"), None, None),
            P(None, ("dp", "rank"), None, None),
            P(None, ("dp", "rank"), None),
            P(None, ("dp", "rank"), None),
            P(("dp", "rank"), None),
            P(None, ("dp", "rank")),
            P(("dp", "rank"), None),
            P(),
            P(),
            P(),
            P(),
            P("rank", "dp"),
            P("dp", "rank"),
            P(None, "rank"),
            P(),
        ),
        out_specs=(
            P(None, ("dp", "rank"), None, None),
            P(None, ("dp", "rank"), None, None),
            P(None, "rank"),
            P(),
        ),
        check_vma=False,
    )
```

```python
import functools
import math

import jax
import jax.numpy as jnp
from jax import lax
from jax.experimental import pallas as pl
from jax.experimental.pallas import tpu as pltpu
from jax.sharding import PartitionSpec as P

HEAD = 64


eps_norm = 1e-05
neg_big = -1000000000.0


def layer_norm(resid, norm_gain, norm_shift):
    row_mean = jnp.mean(resid, axis=-1, keepdims=True)
    centred = resid - row_mean
    variance = jnp.mean(centred * centred, axis=-1, keepdims=True)
    return centred * lax.rsqrt(variance + eps_norm) * norm_gain + norm_shift


def norm_back(resid, norm_gain, norm_shift, grad_normed):

    def forward_norm(values_in):
        return layer_norm(values_in, norm_gain, norm_shift)

    pullback = jax.vjp(forward_norm, resid)[1]
    return pullback(grad_normed)[0]


def gelu_exact(values_in):
    return jax.nn.gelu(values_in, approximate=False)


def gelu_back(inner_pre, grad_hidden):
    pullback = jax.vjp(gelu_exact, inner_pre)[1]
    return pullback(grad_hidden)[0]


def segment_match(lengths, length_rows):
    cumulative = jnp.cumsum(lengths, axis=-1)
    places = jnp.arange(length_rows, dtype=jnp.int32)
    labels = jnp.sum((places[None, :, None] >= cumulative[:, None, :]).astype(jnp.int32), axis=-1)
    return labels[:, :, None] == labels[:, None, :]


def masked_scores(query_heads, key_heads, same_segment):
    scores = jnp.einsum(
        "sqhe,skhe->shqk", query_heads, key_heads, preferred_element_type=jnp.float32
    ) * HEAD ** (-0.5)
    return jnp.where(same_segment[:, None], scores, neg_big)


def attend(query_heads, key_heads, value_heads, same_segment):
    scores = masked_scores(query_heads, key_heads, same_segment)
    row_peak = jnp.max(scores, axis=-1, keepdims=True)
    exponent = jnp.exp(scores - row_peak)
    row_total = jnp.sum(exponent, axis=-1, keepdims=True)
    weights_soft = (exponent / row_total).astype(jnp.bfloat16)
    context = jnp.einsum(
        "shqk,skhe->sqhe", weights_soft, value_heads, preferred_element_type=jnp.float32
    )
    return (context.astype(jnp.bfloat16), row_peak + jnp.log(row_total))


def attend_back(query_heads, key_heads, value_heads, same_segment, log_total, grad_context):
    scores = masked_scores(query_heads, key_heads, same_segment)
    weights_soft = jnp.exp(scores - log_total)
    grad_values = jnp.einsum(
        "shqk,sqhe->skhe",
        weights_soft.astype(jnp.bfloat16),
        grad_context,
        preferred_element_type=jnp.float32,
    )
    grad_weights = jnp.einsum(
        "sqhe,skhe->shqk", grad_context, value_heads, preferred_element_type=jnp.float32
    )
    inner_sum = jnp.sum(grad_weights * weights_soft, axis=-1, keepdims=True)
    grad_scores = (weights_soft * (grad_weights - inner_sum)).astype(jnp.bfloat16)
    grad_query = jnp.einsum(
        "shqk,skhe->sqhe", grad_scores, key_heads, preferred_element_type=jnp.float32
    ) * HEAD ** (-0.5)
    grad_keys = jnp.einsum(
        "shqk,sqhe->skhe", grad_scores, query_heads, preferred_element_type=jnp.float32
    ) * HEAD ** (-0.5)
    return (grad_query, grad_keys, grad_values)


ALL = slice(None)
MESH_IDS = pl.DeviceIdType.MESH
WIDE = jnp.float32
NARROW = jnp.bfloat16
GROUPS = (((2, 48), 512, 256), ((4, 24), 768, 512), ((96,), 768, 384), ((96,), 768, 512))
VERA, SQUARE, INNER, BRANCH = range(4)
SCHEDULE = (
    ("own", INNER),
    ("own", SQUARE),
    ("own", VERA),
    ("line_b", SQUARE, 1),
    ("line_b", VERA, 1),
    ("cross", VERA, 0),
    ("own", BRANCH),
    ("pair", VERA),
    ("pair", SQUARE),
    ("line_b", VERA, 2),
    ("cross", VERA, 1),
    ("cross", SQUARE, 1),
    ("cross", SQUARE, 0),
    ("line_b", SQUARE, 2),
    ("line_a", VERA, 1),
    ("cross", BRANCH, 0),
    ("line_b", VERA, 3),
    ("hand_on", VERA, 0),
    ("cross", VERA, 2),
    ("line_a", VERA, 2),
    ("pair", INNER),
    ("line_b", BRANCH, 1),
    ("line_a", VERA, 3),
    ("line_a", SQUARE, 1),
    ("cross", VERA, 3),
    ("line_b", INNER, 1),
    ("hand_on", VERA, 2),
    ("line_b", BRANCH, 2),
    ("cross", SQUARE, 2),
    ("take", VERA, 0),
    ("hand_on", SQUARE, 1),
    ("hand_on", VERA, 3),
    ("cross", INNER, 0),
    ("line_b", SQUARE, 3),
    ("take", VERA, 2),
    ("hand_on", SQUARE, 0),
    ("hand_on", VERA, 1),
    ("line_a", SQUARE, 2),
    ("cross", SQUARE, 3),
    ("take", VERA, 3),
    ("line_b", BRANCH, 3),
    ("cross", INNER, 1),
    ("line_a", SQUARE, 3),
    ("take", VERA, 1),
    ("scales",),
    ("adapters", 0),
    ("line_a", INNER, 1),
    ("line_b", INNER, 2),
    ("cross", BRANCH, 2),
    ("hand_on", SQUARE, 2),
    ("take", SQUARE, 0),
    ("take", SQUARE, 1),
    ("adapters", 1),
    ("pair", BRANCH),
    ("hand_on", SQUARE, 3),
    ("hand_on", INNER, 0),
    ("take", SQUARE, 2),
    ("take", SQUARE, 3),
    ("cross", INNER, 2),
    ("line_b", INNER, 3),
    ("line_a", INNER, 2),
    ("project_key", 0),
    ("project_query", 0),
    ("project_value", 0),
    ("attend", 0),
    ("attend", 1),
    ("attend", 2),
    ("cross", INNER, 3),
    ("line_a", INNER, 3),
    ("line_a", BRANCH, 1),
    ("attend", 3),
    ("cross", BRANCH, 1),
    ("attend", 4),
    ("hand_on", INNER, 2),
    ("attend", 5),
    ("hand_on", INNER, 1),
    ("close", 0),
    ("hand_on", BRANCH, 0),
    ("line_a", BRANCH, 2),
    ("take", INNER, 0),
    ("close", 1),
    ("cross", BRANCH, 3),
    ("take", INNER, 1),
    ("hand_on", INNER, 3),
    ("inner", 0),
    ("take", INNER, 2),
    ("take", BRANCH, 0),
    ("inner", 1),
    ("inner", 2),
    ("take", INNER, 3),
    ("inner", 3),
    ("line_a", BRANCH, 3),
    ("inner", 4),
    ("hand_on", BRANCH, 1),
    ("inner", 5),
    ("inner", 6),
    ("hand_on", BRANCH, 2),
    ("inner", 7),
    ("branch", 0),
    ("hand_on", BRANCH, 3),
    ("take", BRANCH, 1),
    ("branch", 1),
    ("take", BRANCH, 2),
    ("branch", 2),
    ("take", BRANCH, 3),
    ("branch", 3),
)
SEND_SLOTS = 29
RECV_SLOTS = 21
LINE = 4
PLANE = 8


def nearest(z, turn):
    upper = z // 2
    inner = z * (1 - upper) + (3 - z) * upper
    plane = turn + inner * (1 - 2 * turn) * (1 - turn // 2)
    return plane * (1 - upper) + (3 - plane) * upper


class Relay:
    def __init__(self, buffers, send_sems, recv_sems):
        self.buffers, self.send_sems, self.recv_sems = buffers, send_sems, recv_sems
        place = lax.axis_index("dp")
        self.x = lax.axis_index("rank")
        self.z, self.y, self.c = place // 4, (place // 2) % 2, place % 2

    def device(self, z, y, c, x):
        return {"dp": z * 4 + y * 2 + c, "rank": x}

    def neighbour(self, c, which):
        z, y, x = self.z, self.y, self.x
        if which == "s":
            return self.device(z, y, 1 - c, x)
        if which == "u":
            return self.device(z + 1, y, c, x)
        if which == "d":
            return self.device(z - 1, y, c, x)
        if (which == "p") == (c == 0):
            return self.device(z, y, c, 1 - x)
        return self.device(z, 1 - y, c, x)

    def view(self, g, c, plane, p, q, part):
        lead, cols, split = GROUPS[g]
        window = {"A": pl.ds(0, split), "B": pl.ds(split, cols - split), "F": pl.ds(0, cols)}[part]
        place = (plane, q, c, p) if c == 0 else (plane, p, c, q)
        return self.buffers[g].at[place + (ALL,) * len(lead) + (window,)]

    def copy(self, g, c, plane, p, q, part, to, send, recv):
        block = self.view(g, c, plane, p, q, part)
        return pltpu.make_async_remote_copy(
            block,
            block,
            self.send_sems.at[g, send],
            self.recv_sems.at[g, recv],
            device_id=self.neighbour(c, to),
            device_id_type=MESH_IDS,
        )


class Steps:
    def __init__(self, relay, g, c):
        self.relay, self.g, self.c = relay, g, c
        self.z = relay.z
        self.p, self.q = (relay.x, relay.y) if c == 0 else (relay.y, relay.x)
        self.closing = False

    def send(self, cond, *where):
        def act():
            copy = self.relay.copy(self.g, self.c, *where)
            if self.closing:
                copy.wait_send()
            else:
                copy.start()

        if cond is None:
            act()
        else:
            pl.when(cond)(act)

    def finish(self):
        self.closing = True
        self.own()
        self.pair()
        for far in (1, 2, 3):
            self.line_a(far)
            self.line_b(far)
        for turn in range(4):
            self.cross(turn)
            self.hand_on(turn)

    def got(self, *where):
        if not self.closing:
            self.relay.copy(self.g, self.c, *where).wait_recv()

    def own(self):
        z, p, q = self.z, self.p, self.q
        self.send(None, z, p, q, "A", "p", 0, 0)
        self.send(z < 3, z, p, q, "B", "u", 1, 9 + z)
        self.send(z > 0, z, p, q, "B", "d", 2, 9 + z)
        self.send(None, z, p, q, "B", "p", 3, 13 + z)

    def pair(self):
        z, p, q = self.z, self.p, self.q
        self.got(z, 1 - p, q, "A", "p", 0, 0)
        self.send(z < 3, z, ALL, q, "A", "u", 4, 1 + z)
        self.send(z > 0, z, ALL, q, "A", "d", 5, 1 + z)
        self.send(None, z, ALL, q, "A", "q", 6, 5 + z)

    def line(self, part, far):
        z, p, q = self.z, self.p, self.q
        for side in (0, 1):
            plane = z - far if side == 0 else z + far
            cond = plane >= 0 if side == 0 else plane <= 3
            more = z < 3 if side == 0 else z > 0
            to = "u" if side == 0 else "d"
            slot = {1: 7 + 3 * side, 2: 13, 3: 15}[far]
            slot_p = {1: 17 + side, 2: 19, 3: 20}[far]
            if part == "A":

                @pl.when(cond)
                def _():
                    self.got(plane, ALL, q, "A", to, 0, 1 + plane)

                if far < 3:
                    self.send(jnp.logical_and(cond, more), plane, ALL, q, "A", to, slot, 1 + plane)
                self.send(cond, plane, ALL, q, "A", "q", slot + 1, 5 + plane)
            else:

                @pl.when(cond)
                def _():
                    self.got(plane, p, q, "B", to, 0, 9 + plane)

                if far < 3:
                    self.send(jnp.logical_and(cond, more), plane, p, q, "B", to, slot + 2, 9 + plane)
                self.send(cond, plane, p, q, "B", "p", slot_p, 13 + plane)

    def line_a(self, far):
        self.line("A", far)

    def line_b(self, far):
        self.line("B", far)

    def cross(self, turn):
        plane = nearest(self.z, turn)
        self.got(plane, 1 - self.p, self.q, "B", "p", 0, 13 + plane)
        self.send(None, plane, ALL, self.q, "B", "q", 21 + turn, 5 + plane)

    def hand_on(self, turn):
        plane = nearest(self.z, turn)
        self.got(plane, ALL, 1 - self.q, "F", "q", 0, 5 + plane)
        self.send(None, plane, ALL, ALL, "F", "s", 25 + turn, 17 + plane)

    def take(self, turn):
        plane = nearest(self.z, turn)
        self.relay.copy(self.g, 1 - self.c, plane, ALL, ALL, "F", "s", 0, 17 + plane).wait_recv()


class Gather:
    def __init__(self, relay):
        self.relay = relay
        self.steps = [[Steps(relay, g, c) for g in range(len(GROUPS))] for c in (0, 1)]

    def __call__(self, name, g, *where):
        for core in (0, 1):

            @pl.when(self.relay.c == core)
            def _():
                getattr(self.steps[core][g], name)(*where)


def dot_nn(left, right):
    return jnp.dot(left, right, preferred_element_type=WIDE)


def dot_nt(left, right):
    return lax.dot_general(left, right, (((1,), (1,)), ((), ())), preferred_element_type=WIDE)


def dot_tn(left, right):
    return lax.dot_general(left, right, (((0,), (0,)), ((), ())), preferred_element_type=WIDE)


def standardise(resid):
    centred = resid - jnp.mean(resid, axis=-1, keepdims=True)
    inverse = lax.rsqrt(jnp.mean(centred * centred, axis=-1, keepdims=True) + eps_norm)
    return centred * inverse, inverse


def standardise_back(normed, inverse, grad):
    along = jnp.mean(grad * normed, axis=-1, keepdims=True)
    return inverse * (grad - jnp.mean(grad, axis=-1, keepdims=True) - normed * along)


def layer_kernel(grad_scale, *refs):
    (
        tokens_in,
        cotangent_in,
        seg_lengths,
        attn_piece,
        out_piece,
        inner_piece,
        branch_piece,
        lin_biases,
        ffn_bias,
        norm_gains,
        norm_biases,
        down_piece,
        up_piece,
        scale_d,
        scale_b,
        output,
        input_grad,
        d_grad,
        b_grad,
        vera,
        square,
        inner_t,
        branch_w,
        scales,
        same,
        low,
        extra_q,
        extra_v,
        query,
        key,
        value,
        probs,
        context,
        normed_one,
        inverse_one,
        resid,
        narrow_one,
        hidden,
        slope,
        out_stage,
        grad_stage,
        plane_sums,
        line_sums,
        bias_row,
        tokens,
        cotangent,
        send_sems,
        recv_sems,
        local_sems,
        sum_sems,
    ) = refs
    relay = Relay((vera, square, inner_t, branch_w), send_sems, recv_sems)
    gather = Gather(relay)
    z, y, c, x = relay.z, relay.y, relay.c, relay.x
    spot = c * 4 + y * 2 + x

    def in_plane(turn):
        other = lax.rem(spot + turn, PLANE)
        return other, relay.device(z, (other // 2) % 2, other // 4, other % 2)

    def in_line(turn):
        other = lax.rem(z + turn, LINE)
        return other, relay.device(other, y, c, x)

    mine = [
        pltpu.make_async_copy(up_piece, vera.at[z, y, c, x, 1], local_sems.at[0]),
        pltpu.make_async_copy(attn_piece, square.at[z, y, c, x, pl.ds(0, 3)], local_sems.at[1]),
        pltpu.make_async_copy(out_piece, square.at[z, y, c, x, 3], local_sems.at[2]),
        pltpu.make_async_copy(branch_piece, branch_w.at[z, y, c, x], local_sems.at[3]),
        pltpu.make_async_copy(scale_d, scales.at[x], local_sems.at[4]),
        pltpu.make_async_copy(inner_piece, inner_t.at[z, y, c, x], local_sems.at[5]),
        pltpu.make_async_copy(down_piece, vera.at[z, y, c, x, 0], local_sems.at[6]),
    ]
    tokens_copy = pltpu.make_async_copy(tokens_in, tokens, local_sems.at[7])
    cotangent_copy = pltpu.make_async_copy(cotangent_in, cotangent, local_sems.at[8])
    for copy in mine + [tokens_copy, cotangent_copy]:
        copy.start()
    barrier = pltpu.get_barrier_semaphore()

    def greet(device):
        pl.semaphore_signal(barrier, 1, device_id=device, device_id_type=MESH_IDS)

    greet(relay.device(z, y, 1 - c, x))
    greet(relay.device(z, y, c, 1 - x))
    greet(relay.device(z, 1 - y, c, x))

    @pl.when(z < 3)
    def _():
        greet(relay.device(z + 1, y, c, x))

    @pl.when(z > 0)
    def _():
        greet(relay.device(z - 1, y, c, x))

    for copy in mine:
        copy.wait()
    pl.semaphore_wait(barrier, 3 + jnp.where(z < 3, 1, 0) + jnp.where(z > 0, 1, 0))

    scale_copy = pltpu.make_async_remote_copy(
        scales.at[x],
        scales.at[x],
        sum_sems.at[0],
        sum_sems.at[1],
        device_id=relay.device(z, y, c, 1 - x),
        device_id_type=MESH_IDS,
    )
    scale_copy.start()

    def segments(seq):
        row_place = lax.broadcasted_iota(jnp.int32, (256, 256), 0)
        col_place = lax.broadcasted_iota(jnp.int32, (256, 256), 1)
        row_label = jnp.zeros((256, 256), jnp.int32)
        col_label = jnp.zeros((256, 256), jnp.int32)
        end = jnp.int32(0)
        for k in range(seg_lengths.shape[1]):
            end = end + seg_lengths[seq, k]
            row_label = row_label + (row_place >= end).astype(jnp.int32)
            col_label = col_label + (col_place >= end).astype(jnp.int32)
        same[seq] = jnp.where(row_label == col_label, 0.0, neg_big)

    def row(ref, k):
        return ref[k : k + 1, :].astype(WIDE)

    def rows_of(i):
        return pl.ds(pl.multiple_of(i * 256, 256), 256)

    def down_t(h):
        return vera[:, :, :, h, 0].reshape(768, 512)

    def up(h):
        return vera[:, :, :, h, 1].reshape(768, 512)

    def weight(k):
        return square[:, :, :, :, k].reshape(768, 768)

    def steps_at(i, relays):
        for k, steps in relays.items():

            @pl.when(i == k)
            def _():
                for step in steps:
                    take_step(step)

    def adapters(i):
        rows = rows_of(i)
        token_rows = tokens[rows, :]
        parts_q, parts_v = [], []
        for h in range(2):
            lowrank = dot_nn(token_rows, down_t(h))
            low[rows, h * 512 : (h + 1) * 512] = lowrank
            parts_q.append(dot_nt((scales[h, 0:1, :].astype(WIDE) * lowrank).astype(NARROW), up(h)))
            parts_v.append(dot_nt((scales[h, 1:2, :].astype(WIDE) * lowrank).astype(NARROW), up(h)))
        extra_q[rows, :] = parts_q[0] + parts_q[1]
        extra_v[rows, :] = parts_v[0] + parts_v[1]

    def project_key():
        key[...] = dot_nn(tokens[...], weight(1)).astype(NARROW)

    def project_query():
        total = dot_nn(tokens[...], weight(0)) + row(lin_biases, 0) + row(scale_b, 0) * extra_q[...]
        query[...] = (total * HEAD ** (-0.5)).astype(NARROW)

    def project_value():
        total = dot_nn(tokens[...], weight(2)) + row(lin_biases, 1) + row(scale_b, 1) * extra_v[...]
        value[...] = total.astype(NARROW)

    def head_cols(j):
        return pl.ds(pl.multiple_of(j * 128, 128), 128)

    lane = lax.broadcasted_iota(jnp.int32, (256, 128), 1)
    first_half = lane < HEAD

    def attend_pair(it):
        seq, j = it // 6, lax.rem(it, 6)
        rows, cols = rows_of(seq), head_cols(j)
        q_pair, k_pair, v_pair = query[rows, cols], key[rows, cols], value[rows, cols]
        zero = jnp.zeros_like(q_pair)
        queries = jnp.concatenate([jnp.where(first_half, q_pair, zero), jnp.where(first_half, zero, q_pair)])
        both = dot_nt(queries, k_pair)
        parts = []
        for half in range(2):
            scores = both[half * 256 : (half + 1) * 256] + same[seq]
            peak = jnp.max(scores, axis=-1, keepdims=True)
            exponent = jnp.exp(scores - peak)
            total = jnp.sum(exponent, axis=-1, keepdims=True)
            soft = (exponent * (1.0 / total)).astype(NARROW)
            probs[it * 2 + half] = soft
            parts.append(soft)
        both = dot_nn(jnp.concatenate(parts), v_pair)
        context[rows, cols] = jnp.where(first_half, both[:256], both[256:]).astype(NARROW)

    def close_attention(i):
        rows = rows_of(i)
        attended = dot_nn(context[rows, :], weight(3)) + row(lin_biases, 2)
        normed, inverse = standardise(tokens[rows, :].astype(WIDE) + attended)
        normed_one[rows, :] = normed
        inverse_one[rows, :] = inverse
        scaled = normed * row(norm_gains, 0) + row(norm_biases, 0)
        narrow_one[rows, :] = scaled.astype(NARROW)
        resid[rows, :] = scaled + row(lin_biases, 3)

    def hidden_cols(plane):
        return pl.ds(pl.multiple_of(plane * 768, 768), 768)

    def inner_block(it):
        turn, i = it // 2, lax.rem(it, 2)
        plane = nearest(z, turn)
        rows, cols = rows_of(i), hidden_cols(plane)
        block = dot_nt(narrow_one[rows, :], inner_t[plane].reshape(768, 768))
        block = block + bias_row[0:1, cols]
        below = 0.5 + 0.5 * lax.erf(block * 0.7071067811865476)
        hidden[rows, cols] = (block * below).astype(NARROW)
        slope[rows, cols] = (below + block * jnp.exp(-0.5 * block * block) * 0.3989422804014327).astype(NARROW)

    def branch_block(turn):
        plane = nearest(z, turn)
        resid[...] += dot_nn(hidden[:, hidden_cols(plane)], branch_w[plane].reshape(768, 768))

    def attend(it):
        attend_pair(2 * it)
        attend_pair(2 * it + 1)

    bodies = {
        "adapters": (2, adapters),
        "project_key": (1, lambda i: project_key()),
        "project_query": (1, lambda i: project_query()),
        "project_value": (1, lambda i: project_value()),
        "attend": (6, attend),
        "close": (2, close_attention),
        "inner": (8, inner_block),
        "branch": (4, branch_block),
    }

    def take_step(step):
        if step[0] == "scales":
            bias_row[...] = ffn_bias[...].astype(WIDE).reshape(1, -1)
            segments(0)
            segments(1)
            scale_copy.wait()
            tokens_copy.wait()
        else:
            gather(*step)

    at = 0
    while at < len(SCHEDULE):
        name = SCHEDULE[at][0]
        if name not in bodies:
            take_step(SCHEDULE[at])
            at += 1
            continue
        count, body = bodies[name]
        between = {}
        done = 0
        while done < count - 1:
            at += 1
            if SCHEDULE[at][0] == name:
                done += 1
            else:
                between.setdefault(done + 1, []).append(SCHEDULE[at])
        at += 1
        if count == 1:
            body(0)
        else:

            @pl.loop(0, count)
            def _(i):
                steps_at(i, between)
                body(i)

    cotangent_copy.wait()

    for i in range(2):
        rows = slice(i * 256, (i + 1) * 256)
        normed, inverse = standardise(resid[rows, :])
        gain = row(norm_gains, 1)
        out_stage[rows, :] = (normed * gain + row(norm_biases, 1)).astype(NARROW)
        grad = standardise_back(normed, inverse, cotangent[rows, :].astype(WIDE) * gain)
        resid[rows, :] = grad
        narrow_one[rows, :] = grad.astype(NARROW)

    out_copy = pltpu.make_async_copy(out_stage, output, local_sems.at[0])
    out_copy.start()

    @pl.loop(0, 4)
    def _(plane):
        cols = hidden_cols(plane)
        for i in range(2):
            rows = pl.ds(i * 256, 256)
            grad = dot_nt(narrow_one[rows, :], branch_w[plane].reshape(768, 768)).astype(NARROW)
            hidden[rows, cols] = (slope[rows, cols].astype(WIDE) * grad.astype(WIDE)).astype(NARROW)

    for i in range(2):
        rows = slice(i * 256, (i + 1) * 256)
        grad = resid[rows, :] + dot_nn(hidden[rows, :], inner_t[...].reshape(3072, 768))
        grad = standardise_back(normed_one[rows, :], inverse_one[rows, :], grad * row(norm_gains, 0))
        resid[rows, :] = grad
        narrow_one[rows, :] = dot_nt(grad.astype(NARROW), weight(3)).astype(NARROW)

    def attend_back(it):
        seq, j = it // 6, lax.rem(it, 6)
        rows, cols = rows_of(seq), head_cols(j)
        k_pair, v_pair, grad = key[rows, cols], value[rows, cols], narrow_one[rows, cols]
        product = (grad.astype(WIDE) * context[rows, cols].astype(WIDE)).astype(NARROW)
        zero = jnp.zeros_like(grad)
        left = jnp.concatenate([jnp.where(first_half, grad, zero), jnp.where(first_half, zero, grad)])
        sums = jnp.concatenate([jnp.where(first_half, -product, zero), jnp.where(first_half, zero, -product)])
        change = dot_nt(
            jnp.concatenate([left, sums], axis=1), jnp.concatenate([v_pair, jnp.ones_like(v_pair)], axis=1)
        )
        soft = [probs[it * 2 + half] for half in range(2)]
        grad_scores = [
            (soft[half].astype(WIDE) * change[half * 256 : (half + 1) * 256]).astype(NARROW) for half in range(2)
        ]
        grad_q = dot_nn(jnp.concatenate(grad_scores), k_pair)
        grad_v = dot_tn(jnp.concatenate(soft, axis=1), grad)
        for half in range(2):
            probs[it * 2 + half] = grad_scores[half]
        narrow_one[rows, cols] = (jnp.where(first_half, grad_q[:256], grad_q[256:]) * HEAD ** (-0.5)).astype(NARROW)
        value[rows, cols] = jnp.where(first_half, grad_v[:256], grad_v[256:]).astype(NARROW)

    def key_back(it):
        rows, cols = rows_of(it // 6), head_cols(lax.rem(it, 6))
        both = jnp.concatenate([probs[it * 2], probs[it * 2 + 1]], axis=1)
        grad_k = dot_tn(both, query[rows, cols])
        key[rows, cols] = jnp.where(first_half, grad_k[:256], grad_k[256:]).astype(NARROW)

    @pl.loop(0, 6)
    def _(it):
        attend_back(2 * it)
        attend_back(2 * it + 1)

    plane_sums[spot] = jnp.zeros((4, 1024), WIDE)
    low_grad = hidden

    for i in range(2):
        rows = slice(i * 256, (i + 1) * 256)
        grad_q, grad_v = narrow_one[rows, :].astype(WIDE), value[rows, :].astype(WIDE)
        plane_sums[spot, 2:3, 0:768] += jnp.sum(extra_q[rows, :] * grad_q, axis=0, keepdims=True)
        plane_sums[spot, 3:4, 0:768] += jnp.sum(extra_v[rows, :] * grad_v, axis=0, keepdims=True)
        grad_q = (row(scale_b, 0) * grad_q).astype(NARROW)
        grad_v = (row(scale_b, 1) * grad_v).astype(NARROW)
        for h in range(2):
            half = slice(h * 512, (h + 1) * 512)
            scaled_q, scaled_v = dot_nn(grad_q, up(h)), dot_nn(grad_v, up(h))
            plane_sums[spot, 0:1, half] += jnp.sum(low[rows, half] * scaled_q, axis=0, keepdims=True)
            plane_sums[spot, 1:2, half] += jnp.sum(low[rows, half] * scaled_v, axis=0, keepdims=True)
            total = scales[h, 0:1, :].astype(WIDE) * scaled_q + scales[h, 1:2, :].astype(WIDE) * scaled_v
            low_grad[rows, half] = total.astype(NARROW)

    def plane_copy(turn, slot):
        return pltpu.make_async_remote_copy(
            plane_sums.at[slot],
            plane_sums.at[slot],
            sum_sems.at[1 + turn],
            sum_sems.at[9 + slot],
            device_id=in_plane(turn)[1],
            device_id_type=MESH_IDS,
        )

    def line_copy(turn, slot):
        return pltpu.make_async_remote_copy(
            line_sums.at[slot],
            line_sums.at[slot],
            sum_sems.at[16 + turn],
            sum_sems.at[20 + slot],
            device_id=in_line(turn)[1],
            device_id_type=MESH_IDS,
        )

    def input_rows(i):
        rows = slice(i * 256, (i + 1) * 256)
        total = resid[rows, :] + dot_nt(narrow_one[rows, :], weight(0))
        total = total + dot_nt(key[rows, :], weight(1))
        total = total + dot_nt(value[rows, :], weight(2))
        for h in range(2):
            total = total + dot_nt(low_grad[rows, h * 512 : (h + 1) * 512], down_t(h))
        grad_stage[rows, :] = total.astype(NARROW)
        return pltpu.make_async_copy(grad_stage.at[rows, :], input_grad.at[rows, :], local_sems.at[1 + i])

    for turn in range(1, PLANE):
        plane_copy(turn, spot).start()

    @pl.loop(0, 4)
    def _(it):
        for k in range(3):
            key_back(3 * it + k)

    for turn in range(1, PLANE):
        plane_copy(turn, in_plane(turn)[0]).wait_recv()
    total = plane_sums[0]
    for other in range(1, PLANE):
        total = total + plane_sums[other]
    line_sums[z] = total
    for turn in range(1, LINE):
        line_copy(turn, z).start()
    grad_copies = []
    for i in range(2):
        grad_copies.append(input_rows(i))
        grad_copies[i].start()
    for turn in range(1, LINE):
        line_copy(turn, in_line(turn)[0]).wait_recv()
    cols = pl.ds(pl.multiple_of(x * 512, 512), 512)
    total_d, total_b = line_sums[0, 0:2, cols], line_sums[0, 2:4, 0:768]
    for other in range(1, LINE):
        total_d = total_d + line_sums[other, 0:2, cols]
        total_b = total_b + line_sums[other, 2:4, 0:768]
    d_grad[...] = total_d * grad_scale
    b_grad[...] = total_b * grad_scale

    for turn in range(1, PLANE):
        plane_copy(turn, spot).wait_send()
    for turn in range(1, LINE):
        line_copy(turn, z).wait_send()
    for g in range(len(GROUPS)):
        gather("finish", g)
    out_copy.wait()
    for copy in grad_copies:
        copy.wait()


def settle_kernel(*refs):
    sources, targets, sems = refs[:4], refs[4:8], refs[8]
    copies = [pltpu.make_async_copy(sources[k], targets[k], sems.at[k]) for k in range(4)]
    for copy in copies:
        copy.start()
    for copy in copies:
        copy.wait()


def settle(results):
    anywhere = pl.BlockSpec(memory_space=pl.ANY)
    return pl.pallas_call(
        settle_kernel,
        out_shape=[jax.ShapeDtypeStruct(result.shape, result.dtype) for result in results],
        in_specs=[pl.BlockSpec(memory_space=pltpu.VMEM)] * 4,
        out_specs=[anywhere] * 4,
        scratch_shapes=[pltpu.SemaphoreType.DMA((4,))],
    )(*results)


def fused_layer(
    tokens,
    cotangent,
    seg_lengths,
    attn_weights,
    out_weight,
    ffn_in,
    ffn_out,
    lin_biases,
    ffn_bias,
    norm_gains,
    norm_biases,
    shared_down,
    shared_up,
    scale_d,
    scale_b,
):
    rows, width = tokens.shape[0] * tokens.shape[1] * tokens.shape[2], tokens.shape[3]
    devices = lax.axis_size("dp") * lax.axis_size("rank")
    in_vmem, anywhere = pl.BlockSpec(memory_space=pltpu.VMEM), pl.BlockSpec(memory_space=pl.ANY)
    in_smem = pl.BlockSpec(memory_space=pltpu.SMEM)
    shapes = [(4, 2, 2, 2) + lead + (cols,) for lead, cols, _ in GROUPS]
    flat = (rows, width)
    scratch = [pltpu.VMEM(shape, NARROW) for shape in shapes] + [
        pltpu.VMEM((2, 2, 512), NARROW),
        pltpu.VMEM((2, 256, 256), WIDE),
        pltpu.VMEM((rows, 1024), WIDE),
        pltpu.VMEM(flat, WIDE),
        pltpu.VMEM(flat, WIDE),
        pltpu.VMEM(flat, NARROW),
        pltpu.VMEM(flat, NARROW),
        pltpu.VMEM(flat, NARROW),
        pltpu.VMEM((24, 256, 256), NARROW),
        pltpu.VMEM(flat, NARROW),
        pltpu.VMEM(flat, WIDE),
        pltpu.VMEM((rows, 1), WIDE),
        pltpu.VMEM(flat, WIDE),
        pltpu.VMEM(flat, NARROW),
        pltpu.VMEM((rows, 3072), NARROW),
        pltpu.VMEM((rows, 3072), NARROW),
        pltpu.VMEM(flat, NARROW),
        pltpu.VMEM(flat, NARROW),
        pltpu.VMEM((PLANE, 4, 1024), WIDE),
        pltpu.VMEM((LINE, 4, 1024), WIDE),
        pltpu.VMEM((1, 3072), WIDE),
        pltpu.VMEM(flat, NARROW),
        pltpu.VMEM(flat, NARROW),
        pltpu.SemaphoreType.DMA((len(GROUPS), SEND_SLOTS)),
        pltpu.SemaphoreType.DMA((len(GROUPS), RECV_SLOTS)),
        pltpu.SemaphoreType.DMA((9,)),
        pltpu.SemaphoreType.DMA((24,)),
    ]
    results = pl.pallas_call(
        functools.partial(layer_kernel, 1.0 / math.sqrt(rows * devices)),
        out_shape=(
            jax.ShapeDtypeStruct(flat, NARROW),
            jax.ShapeDtypeStruct(flat, NARROW),
            jax.ShapeDtypeStruct((2, 512), WIDE),
            jax.ShapeDtypeStruct((2, 768), WIDE),
        ),
        in_specs=[anywhere, anywhere, in_smem]
        + [anywhere] * 4
        + [in_vmem] * 4
        + [anywhere] * 3
        + [in_vmem],
        out_specs=(anywhere, anywhere, in_vmem, in_vmem),
        scratch_shapes=scratch,
        compiler_params=pltpu.CompilerParams(
            collective_id=0, has_side_effects=True, vmem_limit_bytes=61 << 20
        ),
    )(
        tokens.reshape(flat),
        cotangent.reshape(flat),
        seg_lengths.reshape(-1, seg_lengths.shape[-1]),
        attn_weights,
        out_weight,
        ffn_in.T,
        ffn_out,
        lin_biases,
        ffn_bias,
        norm_gains,
        norm_biases,
        shared_down.T,
        shared_up,
        scale_d,
        scale_b,
    )
    output, input_grad, d_grad, b_grad = settle(results)
    return output.reshape(tokens.shape), input_grad.reshape(tokens.shape), d_grad, b_grad


def gather_weights(attn_weights, out_weight, ffn_in, ffn_out, shared_down, shared_up):
    down_local = lax.all_gather(shared_down, "dp", axis=1, tiled=True)
    up_local = lax.all_gather(shared_up, "dp", axis=0, tiled=True)
    return (
        lax.all_gather(attn_weights, ("dp", "rank"), axis=1, tiled=True),
        lax.all_gather(out_weight, ("dp", "rank"), axis=0, tiled=True),
        lax.all_gather(ffn_in, ("dp", "rank"), axis=1, tiled=True),
        lax.all_gather(ffn_out, ("dp", "rank"), axis=0, tiled=True),
        lax.all_gather(down_local, "rank", axis=0, tiled=True),
        lax.all_gather(up_local, "rank", axis=1, tiled=True),
    )


def per_device(
    tokens,
    cotangent,
    seg_lengths,
    attn_weights,
    out_weight,
    ffn_in,
    ffn_out,
    lin_biases,
    ffn_bias,
    norm_gains,
    norm_biases,
    shared_down,
    shared_up,
    scale_d,
    scale_b,
):
    micro_count, seq_count, length_rows, model_width = tokens.shape
    head_count = model_width // HEAD
    out_shape = tokens.shape
    seq_count = micro_count * seq_count
    row_count = seq_count * length_rows
    head_shape = (seq_count, length_rows, head_count, HEAD)
    float_wide = jnp.float32
    narrow = jnp.bfloat16
    attn_full, output_full, inner_full, branch_full, down_use, up_use = gather_weights(
        attn_weights, out_weight, ffn_in, ffn_out, shared_down, shared_up
    )
    scales_use = lax.all_gather(scale_d, "rank", axis=1, tiled=True)
    rank_cols = scales_use.shape[1]
    sum_d = jnp.zeros((2, rank_cols), float_wide)
    sum_b = jnp.zeros((2, model_width), float_wide)
    outputs = []
    input_grads = []
    for micro_step in range(1):
        token_rows = tokens.reshape(row_count, model_width)
        same_segment = segment_match(seg_lengths.reshape(seq_count, -1), length_rows)
        lowrank = jnp.einsum("rd,kd->rk", token_rows, down_use, preferred_element_type=float_wide)
        scaled = (scales_use[:, None, :] * lowrank[None]).astype(narrow)
        adapted = jnp.concatenate(
            [
                jnp.einsum("rk,dk->rd", scaled[0], up_use, preferred_element_type=float_wide),
                jnp.einsum("rk,dk->rd", scaled[1], up_use, preferred_element_type=float_wide),
            ],
            axis=1,
        )
        extra_query = adapted[:, :model_width]
        extra_value = adapted[:, model_width:]
        query_rows = (
            jnp.dot(token_rows, attn_full[0], preferred_element_type=float_wide)
            + lin_biases[0]
            + scale_b[0] * extra_query
        ).astype(narrow)
        key_rows = jnp.dot(token_rows, attn_full[1], preferred_element_type=float_wide).astype(
            narrow
        )
        value_rows = (
            jnp.dot(token_rows, attn_full[2], preferred_element_type=float_wide)
            + lin_biases[1]
            + scale_b[1] * extra_value
        ).astype(narrow)
        query_heads = query_rows.reshape(head_shape)
        key_heads = key_rows.reshape(head_shape)
        value_heads = value_rows.reshape(head_shape)
        context, log_total = attend(query_heads, key_heads, value_heads, same_segment)
        attended = (
            jnp.dot(
                context.reshape(row_count, model_width),
                output_full,
                preferred_element_type=float_wide,
            )
            + lin_biases[2]
        )
        resid_one = token_rows.astype(float_wide) + attended
        normed_one = layer_norm(resid_one, norm_gains[0], norm_biases[0])
        inner_pre = (
            jnp.dot(normed_one.astype(narrow), inner_full, preferred_element_type=float_wide)
            + ffn_bias
        )
        hidden = gelu_exact(inner_pre).astype(narrow)
        branch = jnp.dot(hidden, branch_full, preferred_element_type=float_wide) + lin_biases[3]
        resid_two = normed_one + branch
        outputs.append(
            layer_norm(resid_two, norm_gains[1], norm_biases[1])
            .astype(narrow)
            .reshape(out_shape)
        )
        grad_out = cotangent.reshape(row_count, model_width).astype(float_wide)
        grad_two = norm_back(resid_two, norm_gains[1], norm_biases[1], grad_out)
        grad_hidden = jnp.einsum(
            "rd,fd->rf", grad_two.astype(narrow), branch_full, preferred_element_type=float_wide
        ).astype(narrow)
        grad_inner = gelu_back(inner_pre, grad_hidden.astype(float_wide)).astype(narrow)
        grad_normed = grad_two + jnp.einsum(
            "rf,df->rd", grad_inner, inner_full, preferred_element_type=float_wide
        )
        grad_one = norm_back(resid_one, norm_gains[0], norm_biases[0], grad_normed)
        grad_attended = grad_one.astype(narrow)
        grad_context = jnp.einsum(
            "ro,io->ri", grad_attended, output_full, preferred_element_type=float_wide
        ).astype(narrow)
        grad_query, grad_keys, grad_values = attend_back(
            query_heads,
            key_heads,
            value_heads,
            same_segment,
            log_total,
            grad_context.reshape(head_shape),
        )
        query_grad = grad_query.reshape(row_count, model_width).astype(narrow)
        key_grad = grad_keys.reshape(row_count, model_width).astype(narrow)
        value_grad = grad_values.reshape(row_count, model_width).astype(narrow)
        grad_input = grad_one + jnp.einsum(
            "ro,io->ri", query_grad, attn_full[0], preferred_element_type=float_wide
        )
        grad_input = grad_input + jnp.einsum(
            "ro,io->ri", key_grad, attn_full[1], preferred_element_type=float_wide
        )
        grad_input = grad_input + jnp.einsum(
            "ro,io->ri", value_grad, attn_full[2], preferred_element_type=float_wide
        )
        query_grad_wide = query_grad.astype(float_wide)
        value_grad_wide = value_grad.astype(float_wide)
        sum_b = sum_b + jnp.stack(
            [
                jnp.sum(extra_query * query_grad_wide, axis=0),
                jnp.sum(extra_value * value_grad_wide, axis=0),
            ]
        )
        grad_extra = jnp.concatenate(
            [
                (scale_b[0] * query_grad_wide).astype(narrow),
                (scale_b[1] * value_grad_wide).astype(narrow),
            ],
            axis=1,
        )
        grad_scaled = jnp.concatenate(
            [
                jnp.dot(grad_extra[:, :model_width], up_use, preferred_element_type=float_wide),
                jnp.dot(grad_extra[:, model_width:], up_use, preferred_element_type=float_wide),
            ],
            axis=1,
        )
        grad_scaled_query = grad_scaled[:, :rank_cols]
        grad_scaled_value = grad_scaled[:, rank_cols:]
        sum_d = sum_d + jnp.stack(
            [
                jnp.sum(lowrank * grad_scaled_query, axis=0),
                jnp.sum(lowrank * grad_scaled_value, axis=0),
            ]
        )
        grad_lowrank = (
            scales_use[0] * grad_scaled_query + scales_use[1] * grad_scaled_value
        ).astype(narrow)
        grad_from_adapter = jnp.dot(grad_lowrank, down_use, preferred_element_type=float_wide)
        input_grads.append(
            (grad_input + grad_from_adapter)
            .astype(narrow)
            .reshape(out_shape)
        )
    grad_scale = 1.0 / math.sqrt(
        row_count * lax.axis_size("dp") * lax.axis_size("rank")
    )
    total_d, total_b = lax.psum((sum_d, sum_b), ("dp", "rank"))
    local_cols = scale_d.shape[1]
    total_d = lax.dynamic_slice_in_dim(total_d, lax.axis_index("rank") * local_cols, local_cols, 1)
    return (outputs[0], input_grads[0], total_d * grad_scale, total_b * grad_scale)


def solution(mesh):
    return jax.shard_map(
        fused_layer if (mesh.shape["dp"], mesh.shape["rank"]) == (16, 2) else per_device,
        mesh=mesh,
        in_specs=(
            P(None, ("dp", "rank"), None, None),
            P(None, ("dp", "rank"), None, None),
            P(None, ("dp", "rank"), None),
            P(None, ("dp", "rank"), None),
            P(("dp", "rank"), None),
            P(None, ("dp", "rank")),
            P(("dp", "rank"), None),
            P(),
            P(),
            P(),
            P(),
            P("rank", "dp"),
            P("dp", "rank"),
            P(None, "rank"),
            P(),
        ),
        out_specs=(
            P(None, ("dp", "rank"), None, None),
            P(None, ("dp", "rank"), None, None),
            P(None, "rank"),
            P(),
        ),
        check_vma=False,
    )
```

```python
import functools
import math

import jax
import jax.numpy as jnp
from jax import lax
from jax.experimental import pallas as pl
from jax.experimental.pallas import tpu as pltpu
from jax.sharding import PartitionSpec as P

HEAD = 64


eps_norm = 1e-05
neg_big = -1000000000.0


def layer_norm(resid, norm_gain, norm_shift):
    row_mean = jnp.mean(resid, axis=-1, keepdims=True)
    centred = resid - row_mean
    variance = jnp.mean(centred * centred, axis=-1, keepdims=True)
    return centred * lax.rsqrt(variance + eps_norm) * norm_gain + norm_shift


def norm_back(resid, norm_gain, norm_shift, grad_normed):

    def forward_norm(values_in):
        return layer_norm(values_in, norm_gain, norm_shift)

    pullback = jax.vjp(forward_norm, resid)[1]
    return pullback(grad_normed)[0]


def gelu_exact(values_in):
    return jax.nn.gelu(values_in, approximate=False)


def gelu_back(inner_pre, grad_hidden):
    pullback = jax.vjp(gelu_exact, inner_pre)[1]
    return pullback(grad_hidden)[0]


def segment_match(lengths, length_rows):
    cumulative = jnp.cumsum(lengths, axis=-1)
    places = jnp.arange(length_rows, dtype=jnp.int32)
    labels = jnp.sum((places[None, :, None] >= cumulative[:, None, :]).astype(jnp.int32), axis=-1)
    return labels[:, :, None] == labels[:, None, :]


def masked_scores(query_heads, key_heads, same_segment):
    scores = jnp.einsum(
        "sqhe,skhe->shqk", query_heads, key_heads, preferred_element_type=jnp.float32
    ) * HEAD ** (-0.5)
    return jnp.where(same_segment[:, None], scores, neg_big)


def attend(query_heads, key_heads, value_heads, same_segment):
    scores = masked_scores(query_heads, key_heads, same_segment)
    row_peak = jnp.max(scores, axis=-1, keepdims=True)
    exponent = jnp.exp(scores - row_peak)
    row_total = jnp.sum(exponent, axis=-1, keepdims=True)
    weights_soft = (exponent / row_total).astype(jnp.bfloat16)
    context = jnp.einsum(
        "shqk,skhe->sqhe", weights_soft, value_heads, preferred_element_type=jnp.float32
    )
    return (context.astype(jnp.bfloat16), row_peak + jnp.log(row_total))


def attend_back(query_heads, key_heads, value_heads, same_segment, log_total, grad_context):
    scores = masked_scores(query_heads, key_heads, same_segment)
    weights_soft = jnp.exp(scores - log_total)
    grad_values = jnp.einsum(
        "shqk,sqhe->skhe",
        weights_soft.astype(jnp.bfloat16),
        grad_context,
        preferred_element_type=jnp.float32,
    )
    grad_weights = jnp.einsum(
        "sqhe,skhe->shqk", grad_context, value_heads, preferred_element_type=jnp.float32
    )
    inner_sum = jnp.sum(grad_weights * weights_soft, axis=-1, keepdims=True)
    grad_scores = (weights_soft * (grad_weights - inner_sum)).astype(jnp.bfloat16)
    grad_query = jnp.einsum(
        "shqk,skhe->sqhe", grad_scores, key_heads, preferred_element_type=jnp.float32
    ) * HEAD ** (-0.5)
    grad_keys = jnp.einsum(
        "shqk,sqhe->skhe", grad_scores, query_heads, preferred_element_type=jnp.float32
    ) * HEAD ** (-0.5)
    return (grad_query, grad_keys, grad_values)


ALL = slice(None)
MESH_IDS = pl.DeviceIdType.MESH
WIDE = jnp.float32
NARROW = jnp.bfloat16
GROUPS = (((2, 48), 512, 256), ((4, 24), 768, 512), ((96,), 768, 384), ((96,), 768, 512))
VERA, SQUARE, INNER, BRANCH = range(4)
SCHEDULE = (
    ("own", INNER),
    ("own", SQUARE),
    ("own", VERA),
    ("line_b", SQUARE, 1),
    ("line_b", VERA, 1),
    ("cross", VERA, 0),
    ("own", BRANCH),
    ("pair", VERA),
    ("pair", SQUARE),
    ("line_b", VERA, 2),
    ("cross", VERA, 1),
    ("cross", SQUARE, 1),
    ("cross", SQUARE, 0),
    ("line_b", SQUARE, 2),
    ("line_a", VERA, 1),
    ("cross", BRANCH, 0),
    ("line_b", VERA, 3),
    ("hand_on", VERA, 0),
    ("cross", VERA, 2),
    ("line_a", VERA, 2),
    ("pair", INNER),
    ("line_b", BRANCH, 1),
    ("line_a", VERA, 3),
    ("line_a", SQUARE, 1),
    ("cross", VERA, 3),
    ("line_b", INNER, 1),
    ("hand_on", VERA, 2),
    ("line_b", BRANCH, 2),
    ("cross", SQUARE, 2),
    ("take", VERA, 0),
    ("hand_on", SQUARE, 1),
    ("hand_on", VERA, 3),
    ("cross", INNER, 0),
    ("line_b", SQUARE, 3),
    ("take", VERA, 2),
    ("hand_on", SQUARE, 0),
    ("hand_on", VERA, 1),
    ("line_a", SQUARE, 2),
    ("cross", SQUARE, 3),
    ("take", VERA, 3),
    ("line_b", BRANCH, 3),
    ("cross", INNER, 1),
    ("line_a", SQUARE, 3),
    ("take", VERA, 1),
    ("scales",),
    ("adapters", 0),
    ("line_a", INNER, 1),
    ("line_b", INNER, 2),
    ("cross", BRANCH, 2),
    ("hand_on", SQUARE, 2),
    ("take", SQUARE, 0),
    ("take", SQUARE, 1),
    ("adapters", 1),
    ("pair", BRANCH),
    ("hand_on", SQUARE, 3),
    ("hand_on", INNER, 0),
    ("take", SQUARE, 2),
    ("take", SQUARE, 3),
    ("cross", INNER, 2),
    ("line_b", INNER, 3),
    ("line_a", INNER, 2),
    ("project_key", 0),
    ("project_query", 0),
    ("project_value", 0),
    ("attend", 0),
    ("attend", 1),
    ("attend", 2),
    ("cross", INNER, 3),
    ("line_a", INNER, 3),
    ("line_a", BRANCH, 1),
    ("attend", 3),
    ("cross", BRANCH, 1),
    ("attend", 4),
    ("hand_on", INNER, 2),
    ("attend", 5),
    ("hand_on", INNER, 1),
    ("close", 0),
    ("hand_on", BRANCH, 0),
    ("line_a", BRANCH, 2),
    ("take", INNER, 0),
    ("close", 1),
    ("cross", BRANCH, 3),
    ("take", INNER, 1),
    ("hand_on", INNER, 3),
    ("inner", 0),
    ("take", INNER, 2),
    ("take", BRANCH, 0),
    ("inner", 1),
    ("inner", 2),
    ("take", INNER, 3),
    ("inner", 3),
    ("line_a", BRANCH, 3),
    ("inner", 4),
    ("hand_on", BRANCH, 1),
    ("inner", 5),
    ("inner", 6),
    ("hand_on", BRANCH, 2),
    ("inner", 7),
    ("branch", 0),
    ("hand_on", BRANCH, 3),
    ("take", BRANCH, 1),
    ("branch", 1),
    ("take", BRANCH, 2),
    ("branch", 2),
    ("take", BRANCH, 3),
    ("branch", 3),
)
SEND_SLOTS = 29
RECV_SLOTS = 21
LINE = 4
PLANE = 8


def nearest(z, turn):
    upper = z // 2
    inner = z * (1 - upper) + (3 - z) * upper
    plane = turn + inner * (1 - 2 * turn) * (1 - turn // 2)
    return plane * (1 - upper) + (3 - plane) * upper


class Relay:
    def __init__(self, buffers, own_sems, send_sems, recv_sems):
        self.buffers, self.own_sems, self.send_sems, self.recv_sems = buffers, own_sems, send_sems, recv_sems
        place = lax.axis_index("dp")
        self.x = lax.axis_index("rank")
        self.z, self.y, self.c = place // 4, (place // 2) % 2, place % 2

    def device(self, z, y, c, x):
        return {"dp": z * 4 + y * 2 + c, "rank": x}

    def neighbour(self, c, which):
        z, y, x = self.z, self.y, self.x
        if which == "s":
            return self.device(z, y, 1 - c, x)
        if which == "u":
            return self.device(z + 1, y, c, x)
        if which == "d":
            return self.device(z - 1, y, c, x)
        if (which == "p") == (c == 0):
            return self.device(z, y, c, 1 - x)
        return self.device(z, 1 - y, c, x)

    def view(self, g, c, plane, p, q, part):
        lead, cols, split = GROUPS[g]
        window = {"A": pl.ds(0, split), "B": pl.ds(split, cols - split), "F": pl.ds(0, cols)}[part]
        place = (plane, q, c, p) if c == 0 else (plane, p, c, q)
        return self.buffers[g].at[place + (ALL,) * len(lead) + (window,)]

    def copy(self, g, c, plane, p, q, part, to, send, recv):
        block = self.view(g, c, plane, p, q, part)
        return pltpu.make_async_remote_copy(
            block,
            block,
            self.own_sems.at[g, send] if send < 4 else self.send_sems.at[g % 2, send - 4],
            self.recv_sems.at[g, recv],
            device_id=self.neighbour(c, to),
            device_id_type=MESH_IDS,
        )


class Steps:
    def __init__(self, relay, g, c):
        self.relay, self.g, self.c = relay, g, c
        self.z = relay.z
        self.p, self.q = (relay.x, relay.y) if c == 0 else (relay.y, relay.x)
        self.closing = False

    def send(self, cond, *where):
        def act():
            copy = self.relay.copy(self.g, self.c, *where)
            if self.closing:
                copy.wait_send()
                return
            if self.g > 1 and where[-2] >= 4:
                self.relay.copy(self.g - 2, self.c, *where).wait_send()
            copy.start()

        if cond is None:
            act()
        else:
            pl.when(cond)(act)

    def finish(self):
        self.closing = True
        self.own()
        if self.g < 2:
            return
        self.pair()
        for far in (1, 2, 3):
            self.line_a(far)
            self.line_b(far)
        for turn in range(4):
            self.cross(turn)
            self.hand_on(turn)

    def got(self, *where):
        if not self.closing:
            self.relay.copy(self.g, self.c, *where).wait_recv()

    def own(self):
        z, p, q = self.z, self.p, self.q
        self.send(None, z, p, q, "A", "p", 0, 0)
        self.send(z < 3, z, p, q, "B", "u", 1, 9 + z)
        self.send(z > 0, z, p, q, "B", "d", 2, 9 + z)
        self.send(None, z, p, q, "B", "p", 3, 13 + z)

    def pair(self):
        z, p, q = self.z, self.p, self.q
        self.got(z, 1 - p, q, "A", "p", 0, 0)
        self.send(z < 3, z, ALL, q, "A", "u", 4, 1 + z)
        self.send(z > 0, z, ALL, q, "A", "d", 5, 1 + z)
        self.send(None, z, ALL, q, "A", "q", 6, 5 + z)

    def line(self, part, far):
        z, p, q = self.z, self.p, self.q
        for side in (0, 1):
            plane = z - far if side == 0 else z + far
            cond = plane >= 0 if side == 0 else plane <= 3
            more = z < 3 if side == 0 else z > 0
            to = "u" if side == 0 else "d"
            slot = {1: 7 + 3 * side, 2: 13, 3: 15}[far]
            slot_p = {1: 17 + side, 2: 19, 3: 20}[far]
            if part == "A":

                @pl.when(cond)
                def _():
                    self.got(plane, ALL, q, "A", to, 0, 1 + plane)

                if far < 3:
                    self.send(jnp.logical_and(cond, more), plane, ALL, q, "A", to, slot, 1 + plane)
                self.send(cond, plane, ALL, q, "A", "q", slot + 1, 5 + plane)
            else:

                @pl.when(cond)
                def _():
                    self.got(plane, p, q, "B", to, 0, 9 + plane)

                if far < 3:
                    self.send(jnp.logical_and(cond, more), plane, p, q, "B", to, slot + 2, 9 + plane)
                self.send(cond, plane, p, q, "B", "p", slot_p, 13 + plane)

    def line_a(self, far):
        self.line("A", far)

    def line_b(self, far):
        self.line("B", far)

    def cross(self, turn):
        plane = nearest(self.z, turn)
        self.got(plane, 1 - self.p, self.q, "B", "p", 0, 13 + plane)
        self.send(None, plane, ALL, self.q, "B", "q", 21 + turn, 5 + plane)

    def hand_on(self, turn):
        plane = nearest(self.z, turn)
        self.got(plane, ALL, 1 - self.q, "F", "q", 0, 5 + plane)
        self.send(None, plane, ALL, ALL, "F", "s", 25 + turn, 17 + plane)

    def take(self, turn):
        plane = nearest(self.z, turn)
        self.relay.copy(self.g, 1 - self.c, plane, ALL, ALL, "F", "s", 0, 17 + plane).wait_recv()


class Gather:
    def __init__(self, relay):
        self.relay = relay
        self.steps = [[Steps(relay, g, c) for g in range(len(GROUPS))] for c in (0, 1)]

    def __call__(self, name, g, *where):
        for core in (0, 1):

            @pl.when(self.relay.c == core)
            def _():
                getattr(self.steps[core][g], name)(*where)


def dot_nn(left, right):
    return jnp.dot(left, right, preferred_element_type=WIDE)


def dot_nt(left, right):
    return lax.dot_general(left, right, (((1,), (1,)), ((), ())), preferred_element_type=WIDE)


def dot_tn(left, right):
    return lax.dot_general(left, right, (((0,), (0,)), ((), ())), preferred_element_type=WIDE)


def standardise(resid):
    centred = resid - jnp.mean(resid, axis=-1, keepdims=True)
    inverse = lax.rsqrt(jnp.mean(centred * centred, axis=-1, keepdims=True) + eps_norm)
    return centred * inverse, inverse


def standardise_back(normed, inverse, grad):
    along = jnp.mean(grad * normed, axis=-1, keepdims=True)
    return inverse * (grad - jnp.mean(grad, axis=-1, keepdims=True) - normed * along)


def layer_kernel(grad_scale, *refs):
    (
        tokens_in,
        cotangent_in,
        seg_lengths,
        attn_piece,
        out_piece,
        inner_piece,
        branch_piece,
        lin_biases,
        ffn_bias,
        norm_gains,
        norm_biases,
        down_piece,
        up_piece,
        scale_d,
        scale_b,
        output,
        input_grad,
        d_grad,
        b_grad,
        vera,
        square,
        inner_t,
        branch_w,
        scales,
        same,
        low,
        extra_q,
        extra_v,
        query,
        key,
        value,
        probs,
        context,
        normed_one,
        inverse_one,
        resid,
        narrow_one,
        hidden,
        slope,
        out_stage,
        grad_stage,
        plane_sums,
        line_sums,
        bias_row,
        tokens,
        cotangent,
        own_sems,
        send_sems,
        recv_sems,
        local_sems,
        sum_sems,
    ) = refs
    relay = Relay((vera, square, inner_t, branch_w), own_sems, send_sems, recv_sems)
    gather = Gather(relay)
    z, y, c, x = relay.z, relay.y, relay.c, relay.x
    spot = c * 4 + y * 2 + x

    def in_plane(turn):
        other = lax.rem(spot + turn, PLANE)
        return other, relay.device(z, (other // 2) % 2, other // 4, other % 2)

    def in_line(turn):
        other = lax.rem(z + turn, LINE)
        return other, relay.device(other, y, c, x)

    mine = [
        pltpu.make_async_copy(up_piece, vera.at[z, y, c, x, 1], local_sems.at[0]),
        pltpu.make_async_copy(attn_piece, square.at[z, y, c, x, pl.ds(0, 3)], local_sems.at[1]),
        pltpu.make_async_copy(out_piece, square.at[z, y, c, x, 3], local_sems.at[2]),
        pltpu.make_async_copy(branch_piece, branch_w.at[z, y, c, x], local_sems.at[3]),
        pltpu.make_async_copy(scale_d, scales.at[x], local_sems.at[4]),
        pltpu.make_async_copy(inner_piece, inner_t.at[z, y, c, x], local_sems.at[5]),
        pltpu.make_async_copy(down_piece, vera.at[z, y, c, x, 0], local_sems.at[6]),
    ]
    tokens_copy = pltpu.make_async_copy(tokens_in, tokens, local_sems.at[7])
    cotangent_copy = pltpu.make_async_copy(cotangent_in, cotangent, local_sems.at[8])
    for copy in mine + [tokens_copy, cotangent_copy]:
        copy.start()
    barrier = pltpu.get_barrier_semaphore()

    def greet(device):
        pl.semaphore_signal(barrier, 1, device_id=device, device_id_type=MESH_IDS)

    greet(relay.device(z, y, 1 - c, x))
    greet(relay.device(z, y, c, 1 - x))
    greet(relay.device(z, 1 - y, c, x))

    @pl.when(z < 3)
    def _():
        greet(relay.device(z + 1, y, c, x))

    @pl.when(z > 0)
    def _():
        greet(relay.device(z - 1, y, c, x))

    for copy in mine:
        copy.wait()
    pl.semaphore_wait(barrier, 3 + jnp.where(z < 3, 1, 0) + jnp.where(z > 0, 1, 0))

    scale_copy = pltpu.make_async_remote_copy(
        scales.at[x],
        scales.at[x],
        sum_sems.at[0],
        sum_sems.at[1],
        device_id=relay.device(z, y, c, 1 - x),
        device_id_type=MESH_IDS,
    )
    scale_copy.start()

    def segments(seq):
        row_place = lax.broadcasted_iota(jnp.int32, (256, 256), 0)
        col_place = lax.broadcasted_iota(jnp.int32, (256, 256), 1)
        row_label = jnp.zeros((256, 256), jnp.int32)
        col_label = jnp.zeros((256, 256), jnp.int32)
        end = jnp.int32(0)
        for k in range(seg_lengths.shape[1]):
            end = end + seg_lengths[seq, k]
            row_label = row_label + (row_place >= end).astype(jnp.int32)
            col_label = col_label + (col_place >= end).astype(jnp.int32)
        same[seq] = jnp.where(row_label == col_label, 0.0, neg_big)

    def row(ref, k):
        return ref[k : k + 1, :].astype(WIDE)

    def rows_of(i):
        return pl.ds(pl.multiple_of(i * 256, 256), 256)

    def down_t(h):
        return vera[:, :, :, h, 0].reshape(768, 512)

    def up(h):
        return vera[:, :, :, h, 1].reshape(768, 512)

    def weight(k):
        return square[:, :, :, :, k].reshape(768, 768)

    def steps_at(i, relays):
        for k, steps in relays.items():

            @pl.when(i == k)
            def _():
                for step in steps:
                    take_step(step)

    def adapters(i):
        rows = rows_of(i)
        token_rows = tokens[rows, :]
        parts_q, parts_v = [], []
        for h in range(2):
            lowrank = dot_nn(token_rows, down_t(h))
            low[rows, h * 512 : (h + 1) * 512] = lowrank
            parts_q.append(dot_nt((scales[h, 0:1, :].astype(WIDE) * lowrank).astype(NARROW), up(h)))
            parts_v.append(dot_nt((scales[h, 1:2, :].astype(WIDE) * lowrank).astype(NARROW), up(h)))
        extra_q[rows, :] = parts_q[0] + parts_q[1]
        extra_v[rows, :] = parts_v[0] + parts_v[1]

    def project_key():
        key[...] = dot_nn(tokens[...], weight(1)).astype(NARROW)

    def project_query():
        total = dot_nn(tokens[...], weight(0)) + row(lin_biases, 0) + row(scale_b, 0) * extra_q[...]
        query[...] = (total * HEAD ** (-0.5)).astype(NARROW)

    def project_value():
        total = dot_nn(tokens[...], weight(2)) + row(lin_biases, 1) + row(scale_b, 1) * extra_v[...]
        value[...] = total.astype(NARROW)

    def head_cols(j):
        return pl.ds(pl.multiple_of(j * 128, 128), 128)

    lane = lax.broadcasted_iota(jnp.int32, (256, 128), 1)
    first_half = lane < HEAD

    def attend_pair(it):
        seq, j = it // 6, lax.rem(it, 6)
        rows, cols = rows_of(seq), head_cols(j)
        q_pair, k_pair, v_pair = query[rows, cols], key[rows, cols], value[rows, cols]
        zero = jnp.zeros_like(q_pair)
        queries = jnp.concatenate([jnp.where(first_half, q_pair, zero), jnp.where(first_half, zero, q_pair)])
        both = dot_nt(queries, k_pair)
        parts = []
        for half in range(2):
            scores = both[half * 256 : (half + 1) * 256] + same[seq]
            peak = jnp.max(scores, axis=-1, keepdims=True)
            exponent = jnp.exp(scores - peak)
            total = jnp.sum(exponent, axis=-1, keepdims=True)
            soft = (exponent * (1.0 / total)).astype(NARROW)
            probs[it * 2 + half] = soft
            parts.append(soft)
        both = dot_nn(jnp.concatenate(parts), v_pair)
        context[rows, cols] = jnp.where(first_half, both[:256], both[256:]).astype(NARROW)

    def close_attention(i):
        rows = rows_of(i)
        attended = dot_nn(context[rows, :], weight(3)) + row(lin_biases, 2)
        normed, inverse = standardise(tokens[rows, :].astype(WIDE) + attended)
        normed_one[rows, :] = normed
        inverse_one[rows, :] = inverse
        scaled = normed * row(norm_gains, 0) + row(norm_biases, 0)
        narrow_one[rows, :] = scaled.astype(NARROW)
        resid[rows, :] = scaled + row(lin_biases, 3)

    def hidden_cols(plane):
        return pl.ds(pl.multiple_of(plane * 768, 768), 768)

    def inner_block(it):
        turn, i = it // 2, lax.rem(it, 2)
        plane = nearest(z, turn)
        rows, cols = rows_of(i), hidden_cols(plane)
        block = dot_nt(narrow_one[rows, :], inner_t[plane].reshape(768, 768))
        block = block + bias_row[0:1, cols]
        below = 0.5 + 0.5 * lax.erf(block * 0.7071067811865476)
        hidden[rows, cols] = (block * below).astype(NARROW)
        slope[rows, cols] = (below + block * jnp.exp(-0.5 * block * block) * 0.3989422804014327).astype(NARROW)

    def branch_block(turn):
        plane = nearest(z, turn)
        resid[...] += dot_nn(hidden[:, hidden_cols(plane)], branch_w[plane].reshape(768, 768))

    def attend(it):
        attend_pair(2 * it)
        attend_pair(2 * it + 1)

    bodies = {
        "adapters": (2, adapters),
        "project_key": (1, lambda i: project_key()),
        "project_query": (1, lambda i: project_query()),
        "project_value": (1, lambda i: project_value()),
        "attend": (6, attend),
        "close": (2, close_attention),
        "inner": (8, inner_block),
        "branch": (4, branch_block),
    }

    def take_step(step):
        if step[0] == "scales":
            bias_row[...] = ffn_bias[...].astype(WIDE).reshape(1, -1)
            segments(0)
            segments(1)
            scale_copy.wait()
            tokens_copy.wait()
        else:
            gather(*step)

    at = 0
    while at < len(SCHEDULE):
        name = SCHEDULE[at][0]
        if name not in bodies:
            take_step(SCHEDULE[at])
            at += 1
            continue
        count, body = bodies[name]
        between = {}
        done = 0
        while done < count - 1:
            at += 1
            if SCHEDULE[at][0] == name:
                done += 1
            else:
                between.setdefault(done + 1, []).append(SCHEDULE[at])
        at += 1
        if count == 1:
            body(0)
        else:

            @pl.loop(0, count)
            def _(i):
                steps_at(i, between)
                body(i)

    cotangent_copy.wait()

    for i in range(2):
        rows = slice(i * 256, (i + 1) * 256)
        normed, inverse = standardise(resid[rows, :])
        gain = row(norm_gains, 1)
        out_stage[rows, :] = (normed * gain + row(norm_biases, 1)).astype(NARROW)
        grad = standardise_back(normed, inverse, cotangent[rows, :].astype(WIDE) * gain)
        resid[rows, :] = grad
        narrow_one[rows, :] = grad.astype(NARROW)

    out_copy = pltpu.make_async_copy(out_stage, output, local_sems.at[0])
    out_copy.start()

    for plane in range(4):
        cols = slice(plane * 768, (plane + 1) * 768)
        for i in range(2):
            rows = slice(i * 256, (i + 1) * 256)
            grad = dot_nt(narrow_one[rows, :], branch_w[plane].reshape(768, 768)).astype(NARROW)
            hidden[rows, cols] = (slope[rows, cols].astype(WIDE) * grad.astype(WIDE)).astype(NARROW)

    for i in range(2):
        rows = slice(i * 256, (i + 1) * 256)
        grad = resid[rows, :] + dot_nn(hidden[rows, :], inner_t[...].reshape(3072, 768))
        grad = standardise_back(normed_one[rows, :], inverse_one[rows, :], grad * row(norm_gains, 0))
        resid[rows, :] = grad
        narrow_one[rows, :] = dot_nt(grad.astype(NARROW), weight(3)).astype(NARROW)

    def attend_back(it):
        seq, j = it // 6, lax.rem(it, 6)
        rows, cols = rows_of(seq), head_cols(j)
        k_pair, v_pair, grad = key[rows, cols], value[rows, cols], narrow_one[rows, cols]
        product = (grad.astype(WIDE) * context[rows, cols].astype(WIDE)).astype(NARROW)
        zero = jnp.zeros_like(grad)
        left = jnp.concatenate([jnp.where(first_half, grad, zero), jnp.where(first_half, zero, grad)])
        sums = jnp.concatenate([jnp.where(first_half, -product, zero), jnp.where(first_half, zero, -product)])
        change = dot_nt(
            jnp.concatenate([left, sums], axis=1), jnp.concatenate([v_pair, jnp.ones_like(v_pair)], axis=1)
        )
        soft = [probs[it * 2 + half] for half in range(2)]
        grad_scores = [
            (soft[half].astype(WIDE) * change[half * 256 : (half + 1) * 256]).astype(NARROW) for half in range(2)
        ]
        grad_q = dot_nn(jnp.concatenate(grad_scores), k_pair)
        grad_v = dot_tn(jnp.concatenate(soft, axis=1), grad)
        for half in range(2):
            probs[it * 2 + half] = grad_scores[half]
        narrow_one[rows, cols] = (jnp.where(first_half, grad_q[:256], grad_q[256:]) * HEAD ** (-0.5)).astype(NARROW)
        value[rows, cols] = jnp.where(first_half, grad_v[:256], grad_v[256:]).astype(NARROW)

    def key_back(it):
        rows, cols = rows_of(it // 6), head_cols(lax.rem(it, 6))
        both = jnp.concatenate([probs[it * 2], probs[it * 2 + 1]], axis=1)
        grad_k = dot_tn(both, query[rows, cols])
        key[rows, cols] = jnp.where(first_half, grad_k[:256], grad_k[256:]).astype(NARROW)

    @pl.loop(0, 2)
    def _(it):
        for k in range(6):
            attend_back(6 * it + k)

    plane_sums[spot] = jnp.zeros((4, 1024), WIDE)
    low_grad = hidden

    for i in range(2):
        rows = slice(i * 256, (i + 1) * 256)
        grad_q, grad_v = narrow_one[rows, :].astype(WIDE), value[rows, :].astype(WIDE)
        plane_sums[spot, 2:3, 0:768] += jnp.sum(extra_q[rows, :] * grad_q, axis=0, keepdims=True)
        plane_sums[spot, 3:4, 0:768] += jnp.sum(extra_v[rows, :] * grad_v, axis=0, keepdims=True)
        grad_q = (row(scale_b, 0) * grad_q).astype(NARROW)
        grad_v = (row(scale_b, 1) * grad_v).astype(NARROW)
        for h in range(2):
            half = slice(h * 512, (h + 1) * 512)
            scaled_q, scaled_v = dot_nn(grad_q, up(h)), dot_nn(grad_v, up(h))
            plane_sums[spot, 0:1, half] += jnp.sum(low[rows, half] * scaled_q, axis=0, keepdims=True)
            plane_sums[spot, 1:2, half] += jnp.sum(low[rows, half] * scaled_v, axis=0, keepdims=True)
            total = scales[h, 0:1, :].astype(WIDE) * scaled_q + scales[h, 1:2, :].astype(WIDE) * scaled_v
            low_grad[rows, half] = total.astype(NARROW)

    def plane_copy(turn, slot):
        return pltpu.make_async_remote_copy(
            plane_sums.at[slot],
            plane_sums.at[slot],
            sum_sems.at[1 + turn],
            sum_sems.at[9 + slot],
            device_id=in_plane(turn)[1],
            device_id_type=MESH_IDS,
        )

    def line_copy(turn, slot):
        return pltpu.make_async_remote_copy(
            line_sums.at[slot],
            line_sums.at[slot],
            sum_sems.at[16 + turn],
            sum_sems.at[20 + slot],
            device_id=in_line(turn)[1],
            device_id_type=MESH_IDS,
        )

    def input_rows(i):
        rows = slice(i * 256, (i + 1) * 256)
        total = resid[rows, :] + dot_nt(narrow_one[rows, :], weight(0))
        total = total + dot_nt(key[rows, :], weight(1))
        total = total + dot_nt(value[rows, :], weight(2))
        for h in range(2):
            total = total + dot_nt(low_grad[rows, h * 512 : (h + 1) * 512], down_t(h))
        grad_stage[rows, :] = total.astype(NARROW)
        return pltpu.make_async_copy(grad_stage.at[rows, :], input_grad.at[rows, :], local_sems.at[1 + i])

    for turn in range(1, PLANE):
        plane_copy(turn, spot).start()

    @pl.loop(0, 2)
    def _(it):
        for k in range(6):
            key_back(6 * it + k)

    for turn in range(1, PLANE):
        plane_copy(turn, in_plane(turn)[0]).wait_recv()
    total = plane_sums[0]
    for other in range(1, PLANE):
        total = total + plane_sums[other]
    line_sums[z] = total
    for turn in range(1, LINE):
        line_copy(turn, z).start()
    grad_copies = []
    for i in range(2):
        grad_copies.append(input_rows(i))
        grad_copies[i].start()
    for turn in range(1, LINE):
        line_copy(turn, in_line(turn)[0]).wait_recv()
    cols = pl.ds(pl.multiple_of(x * 512, 512), 512)
    total_d, total_b = line_sums[0, 0:2, cols], line_sums[0, 2:4, 0:768]
    for other in range(1, LINE):
        total_d = total_d + line_sums[other, 0:2, cols]
        total_b = total_b + line_sums[other, 2:4, 0:768]
    d_grad[...] = total_d * grad_scale
    b_grad[...] = total_b * grad_scale

    for turn in range(1, PLANE):
        plane_copy(turn, spot).wait_send()
    for turn in range(1, LINE):
        line_copy(turn, z).wait_send()
    for g in range(len(GROUPS)):
        gather("finish", g)
    out_copy.wait()
    for copy in grad_copies:
        copy.wait()


def settle_kernel(*refs):
    sources, targets, sems = refs[:4], refs[4:8], refs[8]
    copies = [pltpu.make_async_copy(sources[k], targets[k], sems.at[k]) for k in range(4)]
    for copy in copies:
        copy.start()
    for copy in copies:
        copy.wait()


def settle(results):
    anywhere = pl.BlockSpec(memory_space=pl.ANY)
    return pl.pallas_call(
        settle_kernel,
        out_shape=[jax.ShapeDtypeStruct(result.shape, result.dtype) for result in results],
        in_specs=[pl.BlockSpec(memory_space=pltpu.VMEM)] * 4,
        out_specs=[anywhere] * 4,
        scratch_shapes=[pltpu.SemaphoreType.DMA((4,))],
    )(*results)


def fused_layer(
    tokens,
    cotangent,
    seg_lengths,
    attn_weights,
    out_weight,
    ffn_in,
    ffn_out,
    lin_biases,
    ffn_bias,
    norm_gains,
    norm_biases,
    shared_down,
    shared_up,
    scale_d,
    scale_b,
):
    rows, width = tokens.shape[0] * tokens.shape[1] * tokens.shape[2], tokens.shape[3]
    devices = lax.axis_size("dp") * lax.axis_size("rank")
    in_vmem, anywhere = pl.BlockSpec(memory_space=pltpu.VMEM), pl.BlockSpec(memory_space=pl.ANY)
    in_smem = pl.BlockSpec(memory_space=pltpu.SMEM)
    shapes = [(4, 2, 2, 2) + lead + (cols,) for lead, cols, _ in GROUPS]
    flat = (rows, width)
    scratch = [pltpu.VMEM(shape, NARROW) for shape in shapes] + [
        pltpu.VMEM((2, 2, 512), NARROW),
        pltpu.VMEM((2, 256, 256), WIDE),
        pltpu.VMEM((rows, 1024), WIDE),
        pltpu.VMEM(flat, WIDE),
        pltpu.VMEM(flat, WIDE),
        pltpu.VMEM(flat, NARROW),
        pltpu.VMEM(flat, NARROW),
        pltpu.VMEM(flat, NARROW),
        pltpu.VMEM((24, 256, 256), NARROW),
        pltpu.VMEM(flat, NARROW),
        pltpu.VMEM(flat, WIDE),
        pltpu.VMEM((rows, 1), WIDE),
        pltpu.VMEM(flat, WIDE),
        pltpu.VMEM(flat, NARROW),
        pltpu.VMEM((rows, 3072), NARROW),
        pltpu.VMEM((rows, 3072), NARROW),
        pltpu.VMEM(flat, NARROW),
        pltpu.VMEM(flat, NARROW),
        pltpu.VMEM((PLANE, 4, 1024), WIDE),
        pltpu.VMEM((LINE, 4, 1024), WIDE),
        pltpu.VMEM((1, 3072), WIDE),
        pltpu.VMEM(flat, NARROW),
        pltpu.VMEM(flat, NARROW),
        pltpu.SemaphoreType.DMA((len(GROUPS), 4)),
        pltpu.SemaphoreType.DMA((2, SEND_SLOTS - 4)),
        pltpu.SemaphoreType.DMA((len(GROUPS), RECV_SLOTS)),
        pltpu.SemaphoreType.DMA((9,)),
        pltpu.SemaphoreType.DMA((24,)),
    ]
    results = pl.pallas_call(
        functools.partial(layer_kernel, 1.0 / math.sqrt(rows * devices)),
        out_shape=(
            jax.ShapeDtypeStruct(flat, NARROW),
            jax.ShapeDtypeStruct(flat, NARROW),
            jax.ShapeDtypeStruct((2, 512), WIDE),
            jax.ShapeDtypeStruct((2, 768), WIDE),
        ),
        in_specs=[anywhere, anywhere, in_smem]
        + [anywhere] * 4
        + [in_vmem] * 4
        + [anywhere] * 3
        + [in_vmem],
        out_specs=(anywhere, anywhere, in_vmem, in_vmem),
        scratch_shapes=scratch,
        compiler_params=pltpu.CompilerParams(
            collective_id=0, has_side_effects=True, vmem_limit_bytes=61 << 20
        ),
    )(
        tokens.reshape(flat),
        cotangent.reshape(flat),
        seg_lengths.reshape(-1, seg_lengths.shape[-1]),
        attn_weights,
        out_weight,
        ffn_in.T,
        ffn_out,
        lin_biases,
        ffn_bias,
        norm_gains,
        norm_biases,
        shared_down.T,
        shared_up,
        scale_d,
        scale_b,
    )
    output, input_grad, d_grad, b_grad = settle(results)
    return output.reshape(tokens.shape), input_grad.reshape(tokens.shape), d_grad, b_grad


def gather_weights(attn_weights, out_weight, ffn_in, ffn_out, shared_down, shared_up):
    down_local = lax.all_gather(shared_down, "dp", axis=1, tiled=True)
    up_local = lax.all_gather(shared_up, "dp", axis=0, tiled=True)
    return (
        lax.all_gather(attn_weights, ("dp", "rank"), axis=1, tiled=True),
        lax.all_gather(out_weight, ("dp", "rank"), axis=0, tiled=True),
        lax.all_gather(ffn_in, ("dp", "rank"), axis=1, tiled=True),
        lax.all_gather(ffn_out, ("dp", "rank"), axis=0, tiled=True),
        lax.all_gather(down_local, "rank", axis=0, tiled=True),
        lax.all_gather(up_local, "rank", axis=1, tiled=True),
    )


def per_device(
    tokens,
    cotangent,
    seg_lengths,
    attn_weights,
    out_weight,
    ffn_in,
    ffn_out,
    lin_biases,
    ffn_bias,
    norm_gains,
    norm_biases,
    shared_down,
    shared_up,
    scale_d,
    scale_b,
):
    micro_count, seq_count, length_rows, model_width = tokens.shape
    head_count = model_width // HEAD
    out_shape = tokens.shape
    seq_count = micro_count * seq_count
    row_count = seq_count * length_rows
    head_shape = (seq_count, length_rows, head_count, HEAD)
    float_wide = jnp.float32
    narrow = jnp.bfloat16
    attn_full, output_full, inner_full, branch_full, down_use, up_use = gather_weights(
        attn_weights, out_weight, ffn_in, ffn_out, shared_down, shared_up
    )
    scales_use = lax.all_gather(scale_d, "rank", axis=1, tiled=True)
    rank_cols = scales_use.shape[1]
    sum_d = jnp.zeros((2, rank_cols), float_wide)
    sum_b = jnp.zeros((2, model_width), float_wide)
    outputs = []
    input_grads = []
    for micro_step in range(1):
        token_rows = tokens.reshape(row_count, model_width)
        same_segment = segment_match(seg_lengths.reshape(seq_count, -1), length_rows)
        lowrank = jnp.einsum("rd,kd->rk", token_rows, down_use, preferred_element_type=float_wide)
        scaled = (scales_use[:, None, :] * lowrank[None]).astype(narrow)
        adapted = jnp.concatenate(
            [
                jnp.einsum("rk,dk->rd", scaled[0], up_use, preferred_element_type=float_wide),
                jnp.einsum("rk,dk->rd", scaled[1], up_use, preferred_element_type=float_wide),
            ],
            axis=1,
        )
        extra_query = adapted[:, :model_width]
        extra_value = adapted[:, model_width:]
        query_rows = (
            jnp.dot(token_rows, attn_full[0], preferred_element_type=float_wide)
            + lin_biases[0]
            + scale_b[0] * extra_query
        ).astype(narrow)
        key_rows = jnp.dot(token_rows, attn_full[1], preferred_element_type=float_wide).astype(
            narrow
        )
        value_rows = (
            jnp.dot(token_rows, attn_full[2], preferred_element_type=float_wide)
            + lin_biases[1]
            + scale_b[1] * extra_value
        ).astype(narrow)
        query_heads = query_rows.reshape(head_shape)
        key_heads = key_rows.reshape(head_shape)
        value_heads = value_rows.reshape(head_shape)
        context, log_total = attend(query_heads, key_heads, value_heads, same_segment)
        attended = (
            jnp.dot(
                context.reshape(row_count, model_width),
                output_full,
                preferred_element_type=float_wide,
            )
            + lin_biases[2]
        )
        resid_one = token_rows.astype(float_wide) + attended
        normed_one = layer_norm(resid_one, norm_gains[0], norm_biases[0])
        inner_pre = (
            jnp.dot(normed_one.astype(narrow), inner_full, preferred_element_type=float_wide)
            + ffn_bias
        )
        hidden = gelu_exact(inner_pre).astype(narrow)
        branch = jnp.dot(hidden, branch_full, preferred_element_type=float_wide) + lin_biases[3]
        resid_two = normed_one + branch
        outputs.append(
            layer_norm(resid_two, norm_gains[1], norm_biases[1])
            .astype(narrow)
            .reshape(out_shape)
        )
        grad_out = cotangent.reshape(row_count, model_width).astype(float_wide)
        grad_two = norm_back(resid_two, norm_gains[1], norm_biases[1], grad_out)
        grad_hidden = jnp.einsum(
            "rd,fd->rf", grad_two.astype(narrow), branch_full, preferred_element_type=float_wide
        ).astype(narrow)
        grad_inner = gelu_back(inner_pre, grad_hidden.astype(float_wide)).astype(narrow)
        grad_normed = grad_two + jnp.einsum(
            "rf,df->rd", grad_inner, inner_full, preferred_element_type=float_wide
        )
        grad_one = norm_back(resid_one, norm_gains[0], norm_biases[0], grad_normed)
        grad_attended = grad_one.astype(narrow)
        grad_context = jnp.einsum(
            "ro,io->ri", grad_attended, output_full, preferred_element_type=float_wide
        ).astype(narrow)
        grad_query, grad_keys, grad_values = attend_back(
            query_heads,
            key_heads,
            value_heads,
            same_segment,
            log_total,
            grad_context.reshape(head_shape),
        )
        query_grad = grad_query.reshape(row_count, model_width).astype(narrow)
        key_grad = grad_keys.reshape(row_count, model_width).astype(narrow)
        value_grad = grad_values.reshape(row_count, model_width).astype(narrow)
        grad_input = grad_one + jnp.einsum(
            "ro,io->ri", query_grad, attn_full[0], preferred_element_type=float_wide
        )
        grad_input = grad_input + jnp.einsum(
            "ro,io->ri", key_grad, attn_full[1], preferred_element_type=float_wide
        )
        grad_input = grad_input + jnp.einsum(
            "ro,io->ri", value_grad, attn_full[2], preferred_element_type=float_wide
        )
        query_grad_wide = query_grad.astype(float_wide)
        value_grad_wide = value_grad.astype(float_wide)
        sum_b = sum_b + jnp.stack(
            [
                jnp.sum(extra_query * query_grad_wide, axis=0),
                jnp.sum(extra_value * value_grad_wide, axis=0),
            ]
        )
        grad_extra = jnp.concatenate(
            [
                (scale_b[0] * query_grad_wide).astype(narrow),
                (scale_b[1] * value_grad_wide).astype(narrow),
            ],
            axis=1,
        )
        grad_scaled = jnp.concatenate(
            [
                jnp.dot(grad_extra[:, :model_width], up_use, preferred_element_type=float_wide),
                jnp.dot(grad_extra[:, model_width:], up_use, preferred_element_type=float_wide),
            ],
            axis=1,
        )
        grad_scaled_query = grad_scaled[:, :rank_cols]
        grad_scaled_value = grad_scaled[:, rank_cols:]
        sum_d = sum_d + jnp.stack(
            [
                jnp.sum(lowrank * grad_scaled_query, axis=0),
                jnp.sum(lowrank * grad_scaled_value, axis=0),
            ]
        )
        grad_lowrank = (
            scales_use[0] * grad_scaled_query + scales_use[1] * grad_scaled_value
        ).astype(narrow)
        grad_from_adapter = jnp.dot(grad_lowrank, down_use, preferred_element_type=float_wide)
        input_grads.append(
            (grad_input + grad_from_adapter)
            .astype(narrow)
            .reshape(out_shape)
        )
    grad_scale = 1.0 / math.sqrt(
        row_count * lax.axis_size("dp") * lax.axis_size("rank")
    )
    total_d, total_b = lax.psum((sum_d, sum_b), ("dp", "rank"))
    local_cols = scale_d.shape[1]
    total_d = lax.dynamic_slice_in_dim(total_d, lax.axis_index("rank") * local_cols, local_cols, 1)
    return (outputs[0], input_grads[0], total_d * grad_scale, total_b * grad_scale)


def solution(mesh):
    return jax.shard_map(
        fused_layer if (mesh.shape["dp"], mesh.shape["rank"]) == (16, 2) else per_device,
        mesh=mesh,
        in_specs=(
            P(None, ("dp", "rank"), None, None),
            P(None, ("dp", "rank"), None, None),
            P(None, ("dp", "rank"), None),
            P(None, ("dp", "rank"), None),
            P(("dp", "rank"), None),
            P(None, ("dp", "rank")),
            P(("dp", "rank"), None),
            P(),
            P(),
            P(),
            P(),
            P("rank", "dp"),
            P("dp", "rank"),
            P(None, "rank"),
            P(),
        ),
        out_specs=(
            P(None, ("dp", "rank"), None, None),
            P(None, ("dp", "rank"), None, None),
            P(None, "rank"),
            P(),
        ),
        check_vma=False,
    )
```

```python
import functools
import math

import jax
import jax.numpy as jnp
from jax import lax
from jax.experimental import pallas as pl
from jax.experimental.pallas import tpu as pltpu
from jax.sharding import PartitionSpec as P

HEAD = 64


eps_norm = 1e-05
neg_big = -1000000000.0


def layer_norm(resid, norm_gain, norm_shift):
    row_mean = jnp.mean(resid, axis=-1, keepdims=True)
    centred = resid - row_mean
    variance = jnp.mean(centred * centred, axis=-1, keepdims=True)
    return centred * lax.rsqrt(variance + eps_norm) * norm_gain + norm_shift


def norm_back(resid, norm_gain, norm_shift, grad_normed):

    def forward_norm(values_in):
        return layer_norm(values_in, norm_gain, norm_shift)

    pullback = jax.vjp(forward_norm, resid)[1]
    return pullback(grad_normed)[0]


def gelu_exact(values_in):
    return jax.nn.gelu(values_in, approximate=False)


def gelu_back(inner_pre, grad_hidden):
    pullback = jax.vjp(gelu_exact, inner_pre)[1]
    return pullback(grad_hidden)[0]


def segment_match(lengths, length_rows):
    cumulative = jnp.cumsum(lengths, axis=-1)
    places = jnp.arange(length_rows, dtype=jnp.int32)
    labels = jnp.sum((places[None, :, None] >= cumulative[:, None, :]).astype(jnp.int32), axis=-1)
    return labels[:, :, None] == labels[:, None, :]


def masked_scores(query_heads, key_heads, same_segment):
    scores = jnp.einsum(
        "sqhe,skhe->shqk", query_heads, key_heads, preferred_element_type=jnp.float32
    ) * HEAD ** (-0.5)
    return jnp.where(same_segment[:, None], scores, neg_big)


def attend(query_heads, key_heads, value_heads, same_segment):
    scores = masked_scores(query_heads, key_heads, same_segment)
    row_peak = jnp.max(scores, axis=-1, keepdims=True)
    exponent = jnp.exp(scores - row_peak)
    row_total = jnp.sum(exponent, axis=-1, keepdims=True)
    weights_soft = (exponent / row_total).astype(jnp.bfloat16)
    context = jnp.einsum(
        "shqk,skhe->sqhe", weights_soft, value_heads, preferred_element_type=jnp.float32
    )
    return (context.astype(jnp.bfloat16), row_peak + jnp.log(row_total))


def attend_back(query_heads, key_heads, value_heads, same_segment, log_total, grad_context):
    scores = masked_scores(query_heads, key_heads, same_segment)
    weights_soft = jnp.exp(scores - log_total)
    grad_values = jnp.einsum(
        "shqk,sqhe->skhe",
        weights_soft.astype(jnp.bfloat16),
        grad_context,
        preferred_element_type=jnp.float32,
    )
    grad_weights = jnp.einsum(
        "sqhe,skhe->shqk", grad_context, value_heads, preferred_element_type=jnp.float32
    )
    inner_sum = jnp.sum(grad_weights * weights_soft, axis=-1, keepdims=True)
    grad_scores = (weights_soft * (grad_weights - inner_sum)).astype(jnp.bfloat16)
    grad_query = jnp.einsum(
        "shqk,skhe->sqhe", grad_scores, key_heads, preferred_element_type=jnp.float32
    ) * HEAD ** (-0.5)
    grad_keys = jnp.einsum(
        "shqk,sqhe->skhe", grad_scores, query_heads, preferred_element_type=jnp.float32
    ) * HEAD ** (-0.5)
    return (grad_query, grad_keys, grad_values)


ALL = slice(None)
MESH_IDS = pl.DeviceIdType.MESH
WIDE = jnp.float32
NARROW = jnp.bfloat16
GROUPS = (((2, 48), 512, 256), ((4, 24), 768, 512), ((96,), 768, 384), ((96,), 768, 512))
VERA, SQUARE, INNER, BRANCH = range(4)
SCHEDULE = (
    ("own", SQUARE),
    ("own", VERA),
    ("own", INNER),
    ("line_b", SQUARE, 1),
    ("pair", VERA),
    ("pair", SQUARE),
    ("line_b", VERA, 1),
    ("cross", VERA, 0),
    ("line_a", VERA, 1),
    ("line_b", SQUARE, 2),
    ("cross", VERA, 1),
    ("pair", INNER),
    ("line_b", VERA, 2),
    ("cross", SQUARE, 0),
    ("line_a", SQUARE, 1),
    ("line_a", VERA, 2),
    ("cross", VERA, 2),
    ("line_b", INNER, 1),
    ("cross", SQUARE, 2),
    ("cross", INNER, 0),
    ("cross", SQUARE, 1),
    ("line_b", SQUARE, 3),
    ("line_b", VERA, 3),
    ("own", BRANCH),
    ("cross", VERA, 3),
    ("cross", SQUARE, 3),
    ("line_a", SQUARE, 2),
    ("hand_on", VERA, 0),
    ("cross", INNER, 1),
    ("hand_on", VERA, 2),
    ("hand_on", SQUARE, 1),
    ("line_a", VERA, 3),
    ("line_b", INNER, 2),
    ("take", SQUARE, 1),
    ("line_a", INNER, 1),
    ("line_b", BRANCH, 1),
    ("hand_on", VERA, 3),
    ("take", VERA, 0),
    ("line_a", SQUARE, 3),
    ("hand_on", VERA, 1),
    ("hand_on", SQUARE, 2),
    ("take", VERA, 3),
    ("hand_on", SQUARE, 0),
    ("line_b", INNER, 3),
    ("pair", BRANCH),
    ("hand_on", SQUARE, 3),
    ("cross", INNER, 3),
    ("take", VERA, 1),
    ("take", SQUARE, 0),
    ("take", VERA, 2),
    ("cross", INNER, 2),
    ("scales",),
    ("adapters", 0),
    ("take", SQUARE, 2),
    ("line_b", BRANCH, 2),
    ("hand_on", INNER, 0),
    ("adapters", 1),
    ("cross", BRANCH, 0),
    ("hand_on", INNER, 1),
    ("take", SQUARE, 3),
    ("project_key", 0),
    ("line_a", INNER, 2),
    ("line_a", BRANCH, 1),
    ("project_query", 0),
    ("project_value", 0),
    ("cross", BRANCH, 1),
    ("attend", 0),
    ("attend", 1),
    ("attend", 2),
    ("line_a", INNER, 3),
    ("attend", 3),
    ("attend", 4),
    ("attend", 5),
    ("take", INNER, 0),
    ("line_b", BRANCH, 3),
    ("cross", BRANCH, 2),
    ("hand_on", INNER, 2),
    ("close", 0),
    ("line_a", BRANCH, 2),
    ("close", 1),
    ("inner", 0),
    ("cross", BRANCH, 3),
    ("hand_on", INNER, 3),
    ("take", INNER, 1),
    ("inner", 1),
    ("inner", 2),
    ("hand_on", BRANCH, 0),
    ("inner", 3),
    ("take", INNER, 3),
    ("take", INNER, 2),
    ("hand_on", BRANCH, 1),
    ("line_a", BRANCH, 3),
    ("inner", 4),
    ("hand_on", BRANCH, 2),
    ("inner", 5),
    ("inner", 6),
    ("take", BRANCH, 1),
    ("inner", 7),
    ("take", BRANCH, 2),
    ("take", BRANCH, 0),
    ("branch", 0),
    ("hand_on", BRANCH, 3),
    ("branch", 1),
    ("branch", 2),
    ("take", BRANCH, 3),
    ("branch", 3),
)
SEND_SLOTS = 29
RECV_SLOTS = 21
LINE = 4
PLANE = 8


def nearest(z, turn):
    upper = z // 2
    inner = z * (1 - upper) + (3 - z) * upper
    plane = turn + inner * (1 - 2 * turn) * (1 - turn // 2)
    return plane * (1 - upper) + (3 - plane) * upper


class Relay:
    def __init__(self, buffers, own_sems, send_sems, recv_sems):
        self.buffers, self.own_sems, self.send_sems, self.recv_sems = buffers, own_sems, send_sems, recv_sems
        place = lax.axis_index("dp")
        self.x = lax.axis_index("rank")
        self.z, self.y, self.c = place // 4, (place // 2) % 2, place % 2

    def device(self, z, y, c, x):
        return {"dp": z * 4 + y * 2 + c, "rank": x}

    def neighbour(self, c, which):
        z, y, x = self.z, self.y, self.x
        if which == "s":
            return self.device(z, y, 1 - c, x)
        if which == "u":
            return self.device(z + 1, y, c, x)
        if which == "d":
            return self.device(z - 1, y, c, x)
        if (which == "p") == (c == 0):
            return self.device(z, y, c, 1 - x)
        return self.device(z, 1 - y, c, x)

    def view(self, g, c, plane, p, q, part):
        lead, cols, split = GROUPS[g]
        window = {"A": pl.ds(0, split), "B": pl.ds(split, cols - split), "F": pl.ds(0, cols)}[part]
        place = (plane, q, c, p) if c == 0 else (plane, p, c, q)
        return self.buffers[g].at[place + (ALL,) * len(lead) + (window,)]

    def copy(self, g, c, plane, p, q, part, to, send, recv):
        block = self.view(g, c, plane, p, q, part)
        return pltpu.make_async_remote_copy(
            block,
            block,
            self.own_sems.at[g, send] if send < 4 else self.send_sems.at[g % 2, send - 4],
            self.recv_sems.at[g, recv],
            device_id=self.neighbour(c, to),
            device_id_type=MESH_IDS,
        )


class Steps:
    def __init__(self, relay, g, c):
        self.relay, self.g, self.c = relay, g, c
        self.z = relay.z
        self.p, self.q = (relay.x, relay.y) if c == 0 else (relay.y, relay.x)
        self.closing = False

    def send(self, cond, *where):
        def act():
            copy = self.relay.copy(self.g, self.c, *where)
            if self.closing:
                copy.wait_send()
                return
            if self.g > 1 and where[-2] >= 4:
                self.relay.copy(self.g - 2, self.c, *where).wait_send()
            copy.start()

        if cond is None:
            act()
        else:
            pl.when(cond)(act)

    def finish(self):
        self.closing = True
        self.own()
        if self.g < 2:
            return
        self.pair()
        for far in (1, 2, 3):
            self.line_a(far)
            self.line_b(far)
        for turn in range(4):
            self.cross(turn)
            self.hand_on(turn)

    def got(self, *where):
        if not self.closing:
            self.relay.copy(self.g, self.c, *where).wait_recv()

    def own(self):
        z, p, q = self.z, self.p, self.q
        self.send(None, z, p, q, "A", "p", 0, 0)
        self.send(z < 3, z, p, q, "B", "u", 1, 9 + z)
        self.send(z > 0, z, p, q, "B", "d", 2, 9 + z)
        self.send(None, z, p, q, "B", "p", 3, 13 + z)

    def pair(self):
        z, p, q = self.z, self.p, self.q
        self.got(z, 1 - p, q, "A", "p", 0, 0)
        self.send(z < 3, z, ALL, q, "A", "u", 4, 1 + z)
        self.send(z > 0, z, ALL, q, "A", "d", 5, 1 + z)
        self.send(None, z, ALL, q, "A", "q", 6, 5 + z)

    def line(self, part, far):
        z, p, q = self.z, self.p, self.q
        for side in (0, 1):
            plane = z - far if side == 0 else z + far
            cond = plane >= 0 if side == 0 else plane <= 3
            more = z < 3 if side == 0 else z > 0
            to = "u" if side == 0 else "d"
            slot = {1: 7 + 3 * side, 2: 13, 3: 15}[far]
            slot_p = {1: 17 + side, 2: 19, 3: 20}[far]
            if part == "A":

                @pl.when(cond)
                def _():
                    self.got(plane, ALL, q, "A", to, 0, 1 + plane)

                if far < 3:
                    self.send(jnp.logical_and(cond, more), plane, ALL, q, "A", to, slot, 1 + plane)
                self.send(cond, plane, ALL, q, "A", "q", slot + 1, 5 + plane)
            else:

                @pl.when(cond)
                def _():
                    self.got(plane, p, q, "B", to, 0, 9 + plane)

                if far < 3:
                    self.send(jnp.logical_and(cond, more), plane, p, q, "B", to, slot + 2, 9 + plane)
                self.send(cond, plane, p, q, "B", "p", slot_p, 13 + plane)

    def line_a(self, far):
        self.line("A", far)

    def line_b(self, far):
        self.line("B", far)

    def cross(self, turn):
        plane = nearest(self.z, turn)
        self.got(plane, 1 - self.p, self.q, "B", "p", 0, 13 + plane)
        self.send(None, plane, ALL, self.q, "B", "q", 21 + turn, 5 + plane)

    def hand_on(self, turn):
        plane = nearest(self.z, turn)
        self.got(plane, ALL, 1 - self.q, "F", "q", 0, 5 + plane)
        self.send(None, plane, ALL, ALL, "F", "s", 25 + turn, 17 + plane)

    def take(self, turn):
        plane = nearest(self.z, turn)
        self.relay.copy(self.g, 1 - self.c, plane, ALL, ALL, "F", "s", 0, 17 + plane).wait_recv()


class Gather:
    def __init__(self, relay):
        self.relay = relay
        self.steps = [[Steps(relay, g, c) for g in range(len(GROUPS))] for c in (0, 1)]

    def __call__(self, name, g, *where):
        for core in (0, 1):

            @pl.when(self.relay.c == core)
            def _():
                getattr(self.steps[core][g], name)(*where)


def dot_nn(left, right):
    return jnp.dot(left, right, preferred_element_type=WIDE)


def dot_nt(left, right):
    return lax.dot_general(left, right, (((1,), (1,)), ((), ())), preferred_element_type=WIDE)


def dot_tn(left, right):
    return lax.dot_general(left, right, (((0,), (0,)), ((), ())), preferred_element_type=WIDE)


def standardise(resid):
    centred = resid - jnp.mean(resid, axis=-1, keepdims=True)
    inverse = lax.rsqrt(jnp.mean(centred * centred, axis=-1, keepdims=True) + eps_norm)
    return centred * inverse, inverse


def standardise_back(normed, inverse, grad):
    along = jnp.mean(grad * normed, axis=-1, keepdims=True)
    return inverse * (grad - jnp.mean(grad, axis=-1, keepdims=True) - normed * along)


def layer_kernel(grad_scale, *refs):
    (
        tokens_in,
        cotangent_in,
        seg_lengths,
        attn_piece,
        out_piece,
        inner_piece,
        branch_piece,
        lin_biases,
        ffn_bias,
        norm_gains,
        norm_biases,
        down_piece,
        up_piece,
        scale_d,
        scale_b,
        output,
        input_grad,
        d_grad,
        b_grad,
        vera,
        square,
        inner_t,
        branch_w,
        scales,
        same,
        low,
        extra_q,
        extra_v,
        query,
        key,
        value,
        probs,
        context,
        normed_one,
        inverse_one,
        resid,
        narrow_one,
        hidden,
        slope,
        out_stage,
        grad_stage,
        plane_sums,
        line_sums,
        bias_row,
        tokens,
        cotangent,
        own_sems,
        send_sems,
        recv_sems,
        local_sems,
        sum_sems,
    ) = refs
    relay = Relay((vera, square, inner_t, branch_w), own_sems, send_sems, recv_sems)
    gather = Gather(relay)
    z, y, c, x = relay.z, relay.y, relay.c, relay.x
    spot = c * 4 + y * 2 + x

    def in_plane(turn):
        other = lax.rem(spot + turn, PLANE)
        return other, relay.device(z, (other // 2) % 2, other // 4, other % 2)

    def in_line(turn):
        other = lax.rem(z + turn, LINE)
        return other, relay.device(other, y, c, x)

    mine = [
        pltpu.make_async_copy(up_piece, vera.at[z, y, c, x, 1], local_sems.at[0]),
        pltpu.make_async_copy(attn_piece, square.at[z, y, c, x, pl.ds(0, 3)], local_sems.at[1]),
        pltpu.make_async_copy(out_piece, square.at[z, y, c, x, 3], local_sems.at[2]),
        pltpu.make_async_copy(branch_piece, branch_w.at[z, y, c, x], local_sems.at[3]),
        pltpu.make_async_copy(scale_d, scales.at[x], local_sems.at[4]),
        pltpu.make_async_copy(inner_piece, inner_t.at[z, y, c, x], local_sems.at[5]),
        pltpu.make_async_copy(down_piece, vera.at[z, y, c, x, 0], local_sems.at[6]),
    ]
    tokens_copy = pltpu.make_async_copy(tokens_in, tokens, local_sems.at[7])
    cotangent_copy = pltpu.make_async_copy(cotangent_in, cotangent, local_sems.at[8])
    for copy in mine + [tokens_copy, cotangent_copy]:
        copy.start()
    barrier = pltpu.get_barrier_semaphore()

    def greet(device):
        pl.semaphore_signal(barrier, 1, device_id=device, device_id_type=MESH_IDS)

    greet(relay.device(z, y, 1 - c, x))
    greet(relay.device(z, y, c, 1 - x))
    greet(relay.device(z, 1 - y, c, x))

    @pl.when(z < 3)
    def _():
        greet(relay.device(z + 1, y, c, x))

    @pl.when(z > 0)
    def _():
        greet(relay.device(z - 1, y, c, x))

    for copy in mine:
        copy.wait()
    pl.semaphore_wait(barrier, 3 + jnp.where(z < 3, 1, 0) + jnp.where(z > 0, 1, 0))

    scale_copy = pltpu.make_async_remote_copy(
        scales.at[x],
        scales.at[x],
        sum_sems.at[0],
        sum_sems.at[1],
        device_id=relay.device(z, y, c, 1 - x),
        device_id_type=MESH_IDS,
    )
    scale_copy.start()

    def segments(seq):
        row_place = lax.broadcasted_iota(jnp.int32, (256, 256), 0)
        col_place = lax.broadcasted_iota(jnp.int32, (256, 256), 1)
        row_label = jnp.zeros((256, 256), jnp.int32)
        col_label = jnp.zeros((256, 256), jnp.int32)
        end = jnp.int32(0)
        for k in range(seg_lengths.shape[1]):
            end = end + seg_lengths[seq, k]
            row_label = row_label + (row_place >= end).astype(jnp.int32)
            col_label = col_label + (col_place >= end).astype(jnp.int32)
        same[seq] = jnp.where(row_label == col_label, 0.0, neg_big)

    def row(ref, k):
        return ref[k : k + 1, :].astype(WIDE)

    def rows_of(i):
        return pl.ds(pl.multiple_of(i * 256, 256), 256)

    def down_t(h):
        return vera[:, :, :, h, 0].reshape(768, 512)

    def up(h):
        return vera[:, :, :, h, 1].reshape(768, 512)

    def weight(k):
        return square[:, :, :, :, k].reshape(768, 768)

    def steps_at(i, relays):
        for k, steps in relays.items():

            @pl.when(i == k)
            def _():
                for step in steps:
                    take_step(step)

    def adapters(i):
        rows = rows_of(i)
        token_rows = tokens[rows, :]
        parts_q, parts_v = [], []
        for h in range(2):
            lowrank = dot_nn(token_rows, down_t(h))
            low[rows, h * 512 : (h + 1) * 512] = lowrank
            parts_q.append(dot_nt((scales[h, 0:1, :].astype(WIDE) * lowrank).astype(NARROW), up(h)))
            parts_v.append(dot_nt((scales[h, 1:2, :].astype(WIDE) * lowrank).astype(NARROW), up(h)))
        extra_q[rows, :] = parts_q[0] + parts_q[1]
        extra_v[rows, :] = parts_v[0] + parts_v[1]

    def project_key():
        key[...] = dot_nn(tokens[...], weight(1)).astype(NARROW)

    def project_query():
        total = dot_nn(tokens[...], weight(0)) + row(lin_biases, 0) + row(scale_b, 0) * extra_q[...]
        query[...] = (total * HEAD ** (-0.5)).astype(NARROW)

    def project_value():
        total = dot_nn(tokens[...], weight(2)) + row(lin_biases, 1) + row(scale_b, 1) * extra_v[...]
        value[...] = total.astype(NARROW)

    def head_cols(j):
        return pl.ds(pl.multiple_of(j * 128, 128), 128)

    lane = lax.broadcasted_iota(jnp.int32, (256, 128), 1)
    first_half = lane < HEAD

    def attend_pair(it):
        seq, j = it // 6, lax.rem(it, 6)
        rows, cols = rows_of(seq), head_cols(j)
        q_pair, k_pair, v_pair = query[rows, cols], key[rows, cols], value[rows, cols]
        zero = jnp.zeros_like(q_pair)
        queries = jnp.concatenate([jnp.where(first_half, q_pair, zero), jnp.where(first_half, zero, q_pair)])
        both = dot_nt(queries, k_pair)
        parts = []
        for half in range(2):
            scores = both[half * 256 : (half + 1) * 256] + same[seq]
            peak = jnp.max(scores, axis=-1, keepdims=True)
            exponent = jnp.exp(scores - peak)
            total = jnp.sum(exponent, axis=-1, keepdims=True)
            soft = (exponent * (1.0 / total)).astype(NARROW)
            probs[it * 2 + half] = soft
            parts.append(soft)
        both = dot_nn(jnp.concatenate(parts), v_pair)
        context[rows, cols] = jnp.where(first_half, both[:256], both[256:]).astype(NARROW)

    def close_attention(i):
        rows = rows_of(i)
        attended = dot_nn(context[rows, :], weight(3)) + row(lin_biases, 2)
        normed, inverse = standardise(tokens[rows, :].astype(WIDE) + attended)
        normed_one[rows, :] = normed
        inverse_one[rows, :] = inverse
        scaled = normed * row(norm_gains, 0) + row(norm_biases, 0)
        narrow_one[rows, :] = scaled.astype(NARROW)
        resid[rows, :] = scaled + row(lin_biases, 3)

    def hidden_cols(plane):
        return pl.ds(pl.multiple_of(plane * 768, 768), 768)

    def inner_block(it):
        turn, i = it // 2, lax.rem(it, 2)
        plane = nearest(z, turn)
        rows, cols = rows_of(i), hidden_cols(plane)
        block = dot_nt(narrow_one[rows, :], inner_t[plane].reshape(768, 768))
        block = block + bias_row[0:1, cols]
        below = 0.5 + 0.5 * lax.erf(block * 0.7071067811865476)
        hidden[rows, cols] = (block * below).astype(NARROW)
        slope[rows, cols] = (below + block * jnp.exp(-0.5 * block * block) * 0.3989422804014327).astype(NARROW)

    def branch_block(turn):
        plane = nearest(z, turn)
        resid[...] += dot_nn(hidden[:, hidden_cols(plane)], branch_w[plane].reshape(768, 768))

    def attend(it):
        attend_pair(2 * it)
        attend_pair(2 * it + 1)

    bodies = {
        "adapters": (2, adapters),
        "project_key": (1, lambda i: project_key()),
        "project_query": (1, lambda i: project_query()),
        "project_value": (1, lambda i: project_value()),
        "attend": (6, attend),
        "close": (2, close_attention),
        "inner": (8, inner_block),
        "branch": (4, branch_block),
    }

    def take_step(step):
        if step[0] == "scales":
            bias_row[...] = ffn_bias[...].astype(WIDE).reshape(1, -1)
            segments(0)
            segments(1)
            scale_copy.wait()
            tokens_copy.wait()
        else:
            gather(*step)

    at = 0
    while at < len(SCHEDULE):
        name = SCHEDULE[at][0]
        if name not in bodies:
            take_step(SCHEDULE[at])
            at += 1
            continue
        count, body = bodies[name]
        between = {}
        done = 0
        while done < count - 1:
            at += 1
            if SCHEDULE[at][0] == name:
                done += 1
            else:
                between.setdefault(done + 1, []).append(SCHEDULE[at])
        at += 1
        if count == 1:
            body(0)
        else:

            @pl.loop(0, count)
            def _(i):
                steps_at(i, between)
                body(i)

    cotangent_copy.wait()

    for i in range(2):
        rows = slice(i * 256, (i + 1) * 256)
        normed, inverse = standardise(resid[rows, :])
        gain = row(norm_gains, 1)
        out_stage[rows, :] = (normed * gain + row(norm_biases, 1)).astype(NARROW)
        grad = standardise_back(normed, inverse, cotangent[rows, :].astype(WIDE) * gain)
        resid[rows, :] = grad
        narrow_one[rows, :] = grad.astype(NARROW)

    out_copy = pltpu.make_async_copy(out_stage, output, local_sems.at[0])
    out_copy.start()

    for plane in range(4):
        cols = slice(plane * 768, (plane + 1) * 768)
        for i in range(2):
            rows = slice(i * 256, (i + 1) * 256)
            grad = dot_nt(narrow_one[rows, :], branch_w[plane].reshape(768, 768)).astype(NARROW)
            hidden[rows, cols] = (slope[rows, cols].astype(WIDE) * grad.astype(WIDE)).astype(NARROW)

    for i in range(2):
        rows = slice(i * 256, (i + 1) * 256)
        grad = resid[rows, :] + dot_nn(hidden[rows, :], inner_t[...].reshape(3072, 768))
        grad = standardise_back(normed_one[rows, :], inverse_one[rows, :], grad * row(norm_gains, 0))
        resid[rows, :] = grad
        narrow_one[rows, :] = dot_nt(grad.astype(NARROW), weight(3)).astype(NARROW)

    def attend_back(it):
        seq, j = it // 6, lax.rem(it, 6)
        rows, cols = rows_of(seq), head_cols(j)
        k_pair, v_pair, grad = key[rows, cols], value[rows, cols], narrow_one[rows, cols]
        product = (grad.astype(WIDE) * context[rows, cols].astype(WIDE)).astype(NARROW)
        zero = jnp.zeros_like(grad)
        left = jnp.concatenate([jnp.where(first_half, grad, zero), jnp.where(first_half, zero, grad)])
        sums = jnp.concatenate([jnp.where(first_half, -product, zero), jnp.where(first_half, zero, -product)])
        change = dot_nt(
            jnp.concatenate([left, sums], axis=1), jnp.concatenate([v_pair, jnp.ones_like(v_pair)], axis=1)
        )
        soft = [probs[it * 2 + half] for half in range(2)]
        grad_scores = [
            (soft[half].astype(WIDE) * change[half * 256 : (half + 1) * 256]).astype(NARROW) for half in range(2)
        ]
        grad_q = dot_nn(jnp.concatenate(grad_scores), k_pair)
        grad_v = dot_tn(jnp.concatenate(soft, axis=1), grad)
        for half in range(2):
            probs[it * 2 + half] = grad_scores[half]
        narrow_one[rows, cols] = (jnp.where(first_half, grad_q[:256], grad_q[256:]) * HEAD ** (-0.5)).astype(NARROW)
        value[rows, cols] = jnp.where(first_half, grad_v[:256], grad_v[256:]).astype(NARROW)

    def key_back(it):
        rows, cols = rows_of(it // 6), head_cols(lax.rem(it, 6))
        both = jnp.concatenate([probs[it * 2], probs[it * 2 + 1]], axis=1)
        grad_k = dot_tn(both, query[rows, cols])
        key[rows, cols] = jnp.where(first_half, grad_k[:256], grad_k[256:]).astype(NARROW)

    @pl.loop(0, 2)
    def _(it):
        for k in range(6):
            attend_back(6 * it + k)

    plane_sums[spot] = jnp.zeros((4, 1024), WIDE)
    low_grad = hidden

    for i in range(2):
        rows = slice(i * 256, (i + 1) * 256)
        grad_q, grad_v = narrow_one[rows, :].astype(WIDE), value[rows, :].astype(WIDE)
        plane_sums[spot, 2:3, 0:768] += jnp.sum(extra_q[rows, :] * grad_q, axis=0, keepdims=True)
        plane_sums[spot, 3:4, 0:768] += jnp.sum(extra_v[rows, :] * grad_v, axis=0, keepdims=True)
        grad_q = (row(scale_b, 0) * grad_q).astype(NARROW)
        grad_v = (row(scale_b, 1) * grad_v).astype(NARROW)
        for h in range(2):
            half = slice(h * 512, (h + 1) * 512)
            scaled_q, scaled_v = dot_nn(grad_q, up(h)), dot_nn(grad_v, up(h))
            plane_sums[spot, 0:1, half] += jnp.sum(low[rows, half] * scaled_q, axis=0, keepdims=True)
            plane_sums[spot, 1:2, half] += jnp.sum(low[rows, half] * scaled_v, axis=0, keepdims=True)
            total = scales[h, 0:1, :].astype(WIDE) * scaled_q + scales[h, 1:2, :].astype(WIDE) * scaled_v
            low_grad[rows, half] = total.astype(NARROW)

    def plane_copy(turn, slot):
        return pltpu.make_async_remote_copy(
            plane_sums.at[slot],
            plane_sums.at[slot],
            sum_sems.at[1 + turn],
            sum_sems.at[9 + slot],
            device_id=in_plane(turn)[1],
            device_id_type=MESH_IDS,
        )

    def line_copy(turn, slot):
        return pltpu.make_async_remote_copy(
            line_sums.at[slot],
            line_sums.at[slot],
            sum_sems.at[16 + turn],
            sum_sems.at[20 + slot],
            device_id=in_line(turn)[1],
            device_id_type=MESH_IDS,
        )

    def input_rows(i):
        rows = slice(i * 256, (i + 1) * 256)
        total = resid[rows, :] + dot_nt(narrow_one[rows, :], weight(0))
        total = total + dot_nt(key[rows, :], weight(1))
        total = total + dot_nt(value[rows, :], weight(2))
        for h in range(2):
            total = total + dot_nt(low_grad[rows, h * 512 : (h + 1) * 512], down_t(h))
        grad_stage[rows, :] = total.astype(NARROW)
        return pltpu.make_async_copy(grad_stage.at[rows, :], input_grad.at[rows, :], local_sems.at[1 + i])

    for turn in range(1, PLANE):
        plane_copy(turn, spot).start()

    @pl.loop(0, 2)
    def _(it):
        for k in range(6):
            key_back(6 * it + k)

    for turn in range(1, PLANE):
        plane_copy(turn, in_plane(turn)[0]).wait_recv()
    total = plane_sums[0]
    for other in range(1, PLANE):
        total = total + plane_sums[other]
    line_sums[z] = total
    for turn in range(1, LINE):
        line_copy(turn, z).start()
    grad_copies = []
    for i in range(2):
        grad_copies.append(input_rows(i))
        grad_copies[i].start()
    for turn in range(1, LINE):
        line_copy(turn, in_line(turn)[0]).wait_recv()
    cols = pl.ds(pl.multiple_of(x * 512, 512), 512)
    total_d, total_b = line_sums[0, 0:2, cols], line_sums[0, 2:4, 0:768]
    for other in range(1, LINE):
        total_d = total_d + line_sums[other, 0:2, cols]
        total_b = total_b + line_sums[other, 2:4, 0:768]
    d_grad[...] = total_d * grad_scale
    b_grad[...] = total_b * grad_scale

    for turn in range(1, PLANE):
        plane_copy(turn, spot).wait_send()
    for turn in range(1, LINE):
        line_copy(turn, z).wait_send()
    for g in range(len(GROUPS)):
        gather("finish", g)
    out_copy.wait()
    for copy in grad_copies:
        copy.wait()


def settle_kernel(*refs):
    sources, targets, sems = refs[:4], refs[4:8], refs[8]
    copies = [pltpu.make_async_copy(sources[k], targets[k], sems.at[k]) for k in range(4)]
    for copy in copies:
        copy.start()
    for copy in copies:
        copy.wait()


def settle(results):
    anywhere = pl.BlockSpec(memory_space=pl.ANY)
    return pl.pallas_call(
        settle_kernel,
        out_shape=[jax.ShapeDtypeStruct(result.shape, result.dtype) for result in results],
        in_specs=[pl.BlockSpec(memory_space=pltpu.VMEM)] * 4,
        out_specs=[anywhere] * 4,
        scratch_shapes=[pltpu.SemaphoreType.DMA((4,))],
    )(*results)


def fused_layer(
    tokens,
    cotangent,
    seg_lengths,
    attn_weights,
    out_weight,
    ffn_in,
    ffn_out,
    lin_biases,
    ffn_bias,
    norm_gains,
    norm_biases,
    shared_down,
    shared_up,
    scale_d,
    scale_b,
):
    rows, width = tokens.shape[0] * tokens.shape[1] * tokens.shape[2], tokens.shape[3]
    devices = lax.axis_size("dp") * lax.axis_size("rank")
    in_vmem, anywhere = pl.BlockSpec(memory_space=pltpu.VMEM), pl.BlockSpec(memory_space=pl.ANY)
    in_smem = pl.BlockSpec(memory_space=pltpu.SMEM)
    shapes = [(4, 2, 2, 2) + lead + (cols,) for lead, cols, _ in GROUPS]
    flat = (rows, width)
    scratch = [pltpu.VMEM(shape, NARROW) for shape in shapes] + [
        pltpu.VMEM((2, 2, 512), NARROW),
        pltpu.VMEM((2, 256, 256), WIDE),
        pltpu.VMEM((rows, 1024), WIDE),
        pltpu.VMEM(flat, WIDE),
        pltpu.VMEM(flat, WIDE),
        pltpu.VMEM(flat, NARROW),
        pltpu.VMEM(flat, NARROW),
        pltpu.VMEM(flat, NARROW),
        pltpu.VMEM((24, 256, 256), NARROW),
        pltpu.VMEM(flat, NARROW),
        pltpu.VMEM(flat, WIDE),
        pltpu.VMEM((rows, 1), WIDE),
        pltpu.VMEM(flat, WIDE),
        pltpu.VMEM(flat, NARROW),
        pltpu.VMEM((rows, 3072), NARROW),
        pltpu.VMEM((rows, 3072), NARROW),
        pltpu.VMEM(flat, NARROW),
        pltpu.VMEM(flat, NARROW),
        pltpu.VMEM((PLANE, 4, 1024), WIDE),
        pltpu.VMEM((LINE, 4, 1024), WIDE),
        pltpu.VMEM((1, 3072), WIDE),
        pltpu.VMEM(flat, NARROW),
        pltpu.VMEM(flat, NARROW),
        pltpu.SemaphoreType.DMA((len(GROUPS), 4)),
        pltpu.SemaphoreType.DMA((2, SEND_SLOTS - 4)),
        pltpu.SemaphoreType.DMA((len(GROUPS), RECV_SLOTS)),
        pltpu.SemaphoreType.DMA((9,)),
        pltpu.SemaphoreType.DMA((24,)),
    ]
    results = pl.pallas_call(
        functools.partial(layer_kernel, 1.0 / math.sqrt(rows * devices)),
        out_shape=(
            jax.ShapeDtypeStruct(flat, NARROW),
            jax.ShapeDtypeStruct(flat, NARROW),
            jax.ShapeDtypeStruct((2, 512), WIDE),
            jax.ShapeDtypeStruct((2, 768), WIDE),
        ),
        in_specs=[anywhere, anywhere, in_smem]
        + [anywhere] * 4
        + [in_vmem] * 4
        + [anywhere] * 3
        + [in_vmem],
        out_specs=(anywhere, anywhere, in_vmem, in_vmem),
        scratch_shapes=scratch,
        compiler_params=pltpu.CompilerParams(
            collective_id=0, has_side_effects=True, vmem_limit_bytes=61 << 20
        ),
    )(
        tokens.reshape(flat),
        cotangent.reshape(flat),
        seg_lengths.reshape(-1, seg_lengths.shape[-1]),
        attn_weights,
        out_weight,
        ffn_in.T,
        ffn_out,
        lin_biases,
        ffn_bias,
        norm_gains,
        norm_biases,
        shared_down.T,
        shared_up,
        scale_d,
        scale_b,
    )
    output, input_grad, d_grad, b_grad = settle(results)
    return output.reshape(tokens.shape), input_grad.reshape(tokens.shape), d_grad, b_grad


def gather_weights(attn_weights, out_weight, ffn_in, ffn_out, shared_down, shared_up):
    down_local = lax.all_gather(shared_down, "dp", axis=1, tiled=True)
    up_local = lax.all_gather(shared_up, "dp", axis=0, tiled=True)
    return (
        lax.all_gather(attn_weights, ("dp", "rank"), axis=1, tiled=True),
        lax.all_gather(out_weight, ("dp", "rank"), axis=0, tiled=True),
        lax.all_gather(ffn_in, ("dp", "rank"), axis=1, tiled=True),
        lax.all_gather(ffn_out, ("dp", "rank"), axis=0, tiled=True),
        lax.all_gather(down_local, "rank", axis=0, tiled=True),
        lax.all_gather(up_local, "rank", axis=1, tiled=True),
    )


def per_device(
    tokens,
    cotangent,
    seg_lengths,
    attn_weights,
    out_weight,
    ffn_in,
    ffn_out,
    lin_biases,
    ffn_bias,
    norm_gains,
    norm_biases,
    shared_down,
    shared_up,
    scale_d,
    scale_b,
):
    micro_count, seq_count, length_rows, model_width = tokens.shape
    head_count = model_width // HEAD
    out_shape = tokens.shape
    seq_count = micro_count * seq_count
    row_count = seq_count * length_rows
    head_shape = (seq_count, length_rows, head_count, HEAD)
    float_wide = jnp.float32
    narrow = jnp.bfloat16
    attn_full, output_full, inner_full, branch_full, down_use, up_use = gather_weights(
        attn_weights, out_weight, ffn_in, ffn_out, shared_down, shared_up
    )
    scales_use = lax.all_gather(scale_d, "rank", axis=1, tiled=True)
    rank_cols = scales_use.shape[1]
    sum_d = jnp.zeros((2, rank_cols), float_wide)
    sum_b = jnp.zeros((2, model_width), float_wide)
    outputs = []
    input_grads = []
    for micro_step in range(1):
        token_rows = tokens.reshape(row_count, model_width)
        same_segment = segment_match(seg_lengths.reshape(seq_count, -1), length_rows)
        lowrank = jnp.einsum("rd,kd->rk", token_rows, down_use, preferred_element_type=float_wide)
        scaled = (scales_use[:, None, :] * lowrank[None]).astype(narrow)
        adapted = jnp.concatenate(
            [
                jnp.einsum("rk,dk->rd", scaled[0], up_use, preferred_element_type=float_wide),
                jnp.einsum("rk,dk->rd", scaled[1], up_use, preferred_element_type=float_wide),
            ],
            axis=1,
        )
        extra_query = adapted[:, :model_width]
        extra_value = adapted[:, model_width:]
        query_rows = (
            jnp.dot(token_rows, attn_full[0], preferred_element_type=float_wide)
            + lin_biases[0]
            + scale_b[0] * extra_query
        ).astype(narrow)
        key_rows = jnp.dot(token_rows, attn_full[1], preferred_element_type=float_wide).astype(
            narrow
        )
        value_rows = (
            jnp.dot(token_rows, attn_full[2], preferred_element_type=float_wide)
            + lin_biases[1]
            + scale_b[1] * extra_value
        ).astype(narrow)
        query_heads = query_rows.reshape(head_shape)
        key_heads = key_rows.reshape(head_shape)
        value_heads = value_rows.reshape(head_shape)
        context, log_total = attend(query_heads, key_heads, value_heads, same_segment)
        attended = (
            jnp.dot(
                context.reshape(row_count, model_width),
                output_full,
                preferred_element_type=float_wide,
            )
            + lin_biases[2]
        )
        resid_one = token_rows.astype(float_wide) + attended
        normed_one = layer_norm(resid_one, norm_gains[0], norm_biases[0])
        inner_pre = (
            jnp.dot(normed_one.astype(narrow), inner_full, preferred_element_type=float_wide)
            + ffn_bias
        )
        hidden = gelu_exact(inner_pre).astype(narrow)
        branch = jnp.dot(hidden, branch_full, preferred_element_type=float_wide) + lin_biases[3]
        resid_two = normed_one + branch
        outputs.append(
            layer_norm(resid_two, norm_gains[1], norm_biases[1])
            .astype(narrow)
            .reshape(out_shape)
        )
        grad_out = cotangent.reshape(row_count, model_width).astype(float_wide)
        grad_two = norm_back(resid_two, norm_gains[1], norm_biases[1], grad_out)
        grad_hidden = jnp.einsum(
            "rd,fd->rf", grad_two.astype(narrow), branch_full, preferred_element_type=float_wide
        ).astype(narrow)
        grad_inner = gelu_back(inner_pre, grad_hidden.astype(float_wide)).astype(narrow)
        grad_normed = grad_two + jnp.einsum(
            "rf,df->rd", grad_inner, inner_full, preferred_element_type=float_wide
        )
        grad_one = norm_back(resid_one, norm_gains[0], norm_biases[0], grad_normed)
        grad_attended = grad_one.astype(narrow)
        grad_context = jnp.einsum(
            "ro,io->ri", grad_attended, output_full, preferred_element_type=float_wide
        ).astype(narrow)
        grad_query, grad_keys, grad_values = attend_back(
            query_heads,
            key_heads,
            value_heads,
            same_segment,
            log_total,
            grad_context.reshape(head_shape),
        )
        query_grad = grad_query.reshape(row_count, model_width).astype(narrow)
        key_grad = grad_keys.reshape(row_count, model_width).astype(narrow)
        value_grad = grad_values.reshape(row_count, model_width).astype(narrow)
        grad_input = grad_one + jnp.einsum(
            "ro,io->ri", query_grad, attn_full[0], preferred_element_type=float_wide
        )
        grad_input = grad_input + jnp.einsum(
            "ro,io->ri", key_grad, attn_full[1], preferred_element_type=float_wide
        )
        grad_input = grad_input + jnp.einsum(
            "ro,io->ri", value_grad, attn_full[2], preferred_element_type=float_wide
        )
        query_grad_wide = query_grad.astype(float_wide)
        value_grad_wide = value_grad.astype(float_wide)
        sum_b = sum_b + jnp.stack(
            [
                jnp.sum(extra_query * query_grad_wide, axis=0),
                jnp.sum(extra_value * value_grad_wide, axis=0),
            ]
        )
        grad_extra = jnp.concatenate(
            [
                (scale_b[0] * query_grad_wide).astype(narrow),
                (scale_b[1] * value_grad_wide).astype(narrow),
            ],
            axis=1,
        )
        grad_scaled = jnp.concatenate(
            [
                jnp.dot(grad_extra[:, :model_width], up_use, preferred_element_type=float_wide),
                jnp.dot(grad_extra[:, model_width:], up_use, preferred_element_type=float_wide),
            ],
            axis=1,
        )
        grad_scaled_query = grad_scaled[:, :rank_cols]
        grad_scaled_value = grad_scaled[:, rank_cols:]
        sum_d = sum_d + jnp.stack(
            [
                jnp.sum(lowrank * grad_scaled_query, axis=0),
                jnp.sum(lowrank * grad_scaled_value, axis=0),
            ]
        )
        grad_lowrank = (
            scales_use[0] * grad_scaled_query + scales_use[1] * grad_scaled_value
        ).astype(narrow)
        grad_from_adapter = jnp.dot(grad_lowrank, down_use, preferred_element_type=float_wide)
        input_grads.append(
            (grad_input + grad_from_adapter)
            .astype(narrow)
            .reshape(out_shape)
        )
    grad_scale = 1.0 / math.sqrt(
        row_count * lax.axis_size("dp") * lax.axis_size("rank")
    )
    total_d, total_b = lax.psum((sum_d, sum_b), ("dp", "rank"))
    local_cols = scale_d.shape[1]
    total_d = lax.dynamic_slice_in_dim(total_d, lax.axis_index("rank") * local_cols, local_cols, 1)
    return (outputs[0], input_grads[0], total_d * grad_scale, total_b * grad_scale)


def solution(mesh):
    return jax.shard_map(
        fused_layer if (mesh.shape["dp"], mesh.shape["rank"]) == (16, 2) else per_device,
        mesh=mesh,
        in_specs=(
            P(None, ("dp", "rank"), None, None),
            P(None, ("dp", "rank"), None, None),
            P(None, ("dp", "rank"), None),
            P(None, ("dp", "rank"), None),
            P(("dp", "rank"), None),
            P(None, ("dp", "rank")),
            P(("dp", "rank"), None),
            P(),
            P(),
            P(),
            P(),
            P("rank", "dp"),
            P("dp", "rank"),
            P(None, "rank"),
            P(),
        ),
        out_specs=(
            P(None, ("dp", "rank"), None, None),
            P(None, ("dp", "rank"), None, None),
            P(None, "rank"),
            P(),
        ),
        check_vma=False,
    )
```

```python
import functools
import math

import jax
import jax.numpy as jnp
from jax import lax
from jax.experimental import pallas as pl
from jax.experimental.pallas import tpu as pltpu
from jax.sharding import PartitionSpec as P

HEAD = 64


eps_norm = 1e-05
neg_big = -1000000000.0


def layer_norm(resid, norm_gain, norm_shift):
    row_mean = jnp.mean(resid, axis=-1, keepdims=True)
    centred = resid - row_mean
    variance = jnp.mean(centred * centred, axis=-1, keepdims=True)
    return centred * lax.rsqrt(variance + eps_norm) * norm_gain + norm_shift


def norm_back(resid, norm_gain, norm_shift, grad_normed):

    def forward_norm(values_in):
        return layer_norm(values_in, norm_gain, norm_shift)

    pullback = jax.vjp(forward_norm, resid)[1]
    return pullback(grad_normed)[0]


def gelu_exact(values_in):
    return jax.nn.gelu(values_in, approximate=False)


def gelu_back(inner_pre, grad_hidden):
    pullback = jax.vjp(gelu_exact, inner_pre)[1]
    return pullback(grad_hidden)[0]


def segment_match(lengths, length_rows):
    cumulative = jnp.cumsum(lengths, axis=-1)
    places = jnp.arange(length_rows, dtype=jnp.int32)
    labels = jnp.sum((places[None, :, None] >= cumulative[:, None, :]).astype(jnp.int32), axis=-1)
    return labels[:, :, None] == labels[:, None, :]


def masked_scores(query_heads, key_heads, same_segment):
    scores = jnp.einsum(
        "sqhe,skhe->shqk", query_heads, key_heads, preferred_element_type=jnp.float32
    ) * HEAD ** (-0.5)
    return jnp.where(same_segment[:, None], scores, neg_big)


def attend(query_heads, key_heads, value_heads, same_segment):
    scores = masked_scores(query_heads, key_heads, same_segment)
    row_peak = jnp.max(scores, axis=-1, keepdims=True)
    exponent = jnp.exp(scores - row_peak)
    row_total = jnp.sum(exponent, axis=-1, keepdims=True)
    weights_soft = (exponent / row_total).astype(jnp.bfloat16)
    context = jnp.einsum(
        "shqk,skhe->sqhe", weights_soft, value_heads, preferred_element_type=jnp.float32
    )
    return (context.astype(jnp.bfloat16), row_peak + jnp.log(row_total))


def attend_back(query_heads, key_heads, value_heads, same_segment, log_total, grad_context):
    scores = masked_scores(query_heads, key_heads, same_segment)
    weights_soft = jnp.exp(scores - log_total)
    grad_values = jnp.einsum(
        "shqk,sqhe->skhe",
        weights_soft.astype(jnp.bfloat16),
        grad_context,
        preferred_element_type=jnp.float32,
    )
    grad_weights = jnp.einsum(
        "sqhe,skhe->shqk", grad_context, value_heads, preferred_element_type=jnp.float32
    )
    inner_sum = jnp.sum(grad_weights * weights_soft, axis=-1, keepdims=True)
    grad_scores = (weights_soft * (grad_weights - inner_sum)).astype(jnp.bfloat16)
    grad_query = jnp.einsum(
        "shqk,skhe->sqhe", grad_scores, key_heads, preferred_element_type=jnp.float32
    ) * HEAD ** (-0.5)
    grad_keys = jnp.einsum(
        "shqk,sqhe->skhe", grad_scores, query_heads, preferred_element_type=jnp.float32
    ) * HEAD ** (-0.5)
    return (grad_query, grad_keys, grad_values)


ALL = slice(None)
MESH_IDS = pl.DeviceIdType.MESH
WIDE = jnp.float32
NARROW = jnp.bfloat16
GROUPS = (((2, 48), 512, 256), ((4, 24), 768, 512), ((96,), 768, 384), ((96,), 768, 512))
VERA, SQUARE, INNER, BRANCH = range(4)
SCHEDULE = (
    ("own", SQUARE),
    ("own", VERA),
    ("own", INNER),
    ("line_b", SQUARE, 1),
    ("pair", VERA),
    ("pair", SQUARE),
    ("line_b", VERA, 1),
    ("cross", VERA, 0),
    ("line_a", VERA, 1),
    ("line_b", SQUARE, 2),
    ("cross", VERA, 1),
    ("pair", INNER),
    ("line_b", VERA, 2),
    ("cross", SQUARE, 0),
    ("line_a", SQUARE, 1),
    ("line_a", VERA, 2),
    ("cross", VERA, 2),
    ("line_b", INNER, 1),
    ("cross", SQUARE, 2),
    ("cross", INNER, 0),
    ("cross", SQUARE, 1),
    ("line_b", SQUARE, 3),
    ("line_b", VERA, 3),
    ("own", BRANCH),
    ("cross", VERA, 3),
    ("cross", SQUARE, 3),
    ("line_a", SQUARE, 2),
    ("hand_on", VERA, 0),
    ("cross", INNER, 1),
    ("hand_on", VERA, 2),
    ("hand_on", SQUARE, 1),
    ("line_a", VERA, 3),
    ("line_b", INNER, 2),
    ("take", SQUARE, 1),
    ("line_a", INNER, 1),
    ("line_b", BRANCH, 1),
    ("hand_on", VERA, 3),
    ("take", VERA, 0),
    ("line_a", SQUARE, 3),
    ("hand_on", VERA, 1),
    ("hand_on", SQUARE, 2),
    ("take", VERA, 3),
    ("hand_on", SQUARE, 0),
    ("line_b", INNER, 3),
    ("pair", BRANCH),
    ("hand_on", SQUARE, 3),
    ("cross", INNER, 3),
    ("take", VERA, 1),
    ("take", SQUARE, 0),
    ("take", VERA, 2),
    ("cross", INNER, 2),
    ("scales",),
    ("adapters", 0),
    ("take", SQUARE, 2),
    ("line_b", BRANCH, 2),
    ("hand_on", INNER, 0),
    ("adapters", 1),
    ("cross", BRANCH, 0),
    ("hand_on", INNER, 1),
    ("take", SQUARE, 3),
    ("project_key", 0),
    ("line_a", INNER, 2),
    ("line_a", BRANCH, 1),
    ("project_query", 0),
    ("project_value", 0),
    ("cross", BRANCH, 1),
    ("attend", 0),
    ("line_a", INNER, 3),
    ("attend", 1),
    ("attend", 2),
    ("take", INNER, 0),
    ("line_b", BRANCH, 3),
    ("cross", BRANCH, 2),
    ("hand_on", INNER, 2),
    ("close", 0),
    ("line_a", BRANCH, 2),
    ("close", 1),
    ("inner", 0),
    ("cross", BRANCH, 3),
    ("hand_on", INNER, 3),
    ("take", INNER, 1),
    ("inner", 1),
    ("inner", 2),
    ("hand_on", BRANCH, 0),
    ("inner", 3),
    ("take", INNER, 3),
    ("take", INNER, 2),
    ("hand_on", BRANCH, 1),
    ("line_a", BRANCH, 3),
    ("inner", 4),
    ("hand_on", BRANCH, 2),
    ("inner", 5),
    ("inner", 6),
    ("take", BRANCH, 1),
    ("inner", 7),
    ("take", BRANCH, 2),
    ("take", BRANCH, 0),
    ("branch", 0),
    ("hand_on", BRANCH, 3),
    ("branch", 1),
    ("branch", 2),
    ("take", BRANCH, 3),
    ("branch", 3),
)
SEND_SLOTS = 29
RECV_SLOTS = 21
LINE = 4
PLANE = 8


def nearest(z, turn):
    upper = z // 2
    inner = z * (1 - upper) + (3 - z) * upper
    plane = turn + inner * (1 - 2 * turn) * (1 - turn // 2)
    return plane * (1 - upper) + (3 - plane) * upper


class Relay:
    def __init__(self, buffers, own_sems, send_sems, recv_sems):
        self.buffers, self.own_sems, self.send_sems, self.recv_sems = buffers, own_sems, send_sems, recv_sems
        place = lax.axis_index("dp")
        self.x = lax.axis_index("rank")
        self.z, self.y, self.c = place // 4, (place // 2) % 2, place % 2

    def device(self, z, y, c, x):
        return {"dp": z * 4 + y * 2 + c, "rank": x}

    def neighbour(self, c, which):
        z, y, x = self.z, self.y, self.x
        if which == "s":
            return self.device(z, y, 1 - c, x)
        if which == "u":
            return self.device(z + 1, y, c, x)
        if which == "d":
            return self.device(z - 1, y, c, x)
        if (which == "p") == (c == 0):
            return self.device(z, y, c, 1 - x)
        return self.device(z, 1 - y, c, x)

    def view(self, g, c, plane, p, q, part):
        lead, cols, split = GROUPS[g]
        window = {"A": pl.ds(0, split), "B": pl.ds(split, cols - split), "F": pl.ds(0, cols)}[part]
        place = (plane, q, c, p) if c == 0 else (plane, p, c, q)
        return self.buffers[g].at[place + (ALL,) * len(lead) + (window,)]

    def copy(self, g, c, plane, p, q, part, to, send, recv):
        block = self.view(g, c, plane, p, q, part)
        return pltpu.make_async_remote_copy(
            block,
            block,
            self.own_sems.at[g, send] if send < 4 else self.send_sems.at[g % 2, send - 4],
            self.recv_sems.at[g, recv],
            device_id=self.neighbour(c, to),
            device_id_type=MESH_IDS,
        )


class Steps:
    def __init__(self, relay, g, c):
        self.relay, self.g, self.c = relay, g, c
        self.z = relay.z
        self.p, self.q = (relay.x, relay.y) if c == 0 else (relay.y, relay.x)
        self.closing = False

    def send(self, cond, *where):
        def act():
            copy = self.relay.copy(self.g, self.c, *where)
            if self.closing:
                copy.wait_send()
                return
            if self.g > 1 and where[-2] >= 4:
                self.relay.copy(self.g - 2, self.c, *where).wait_send()
            copy.start()

        if cond is None:
            act()
        else:
            pl.when(cond)(act)

    def finish(self):
        self.closing = True
        self.own()
        if self.g < 2:
            return
        self.pair()
        for far in (1, 2, 3):
            self.line_a(far)
            self.line_b(far)
        for turn in range(4):
            self.cross(turn)
            self.hand_on(turn)

    def got(self, *where):
        if not self.closing:
            self.relay.copy(self.g, self.c, *where).wait_recv()

    def own(self):
        z, p, q = self.z, self.p, self.q
        self.send(None, z, p, q, "A", "p", 0, 0)
        self.send(z < 3, z, p, q, "B", "u", 1, 9 + z)
        self.send(z > 0, z, p, q, "B", "d", 2, 9 + z)
        self.send(None, z, p, q, "B", "p", 3, 13 + z)

    def pair(self):
        z, p, q = self.z, self.p, self.q
        self.got(z, 1 - p, q, "A", "p", 0, 0)
        self.send(z < 3, z, ALL, q, "A", "u", 4, 1 + z)
        self.send(z > 0, z, ALL, q, "A", "d", 5, 1 + z)
        self.send(None, z, ALL, q, "A", "q", 6, 5 + z)

    def line(self, part, far):
        z, p, q = self.z, self.p, self.q
        for side in (0, 1):
            plane = z - far if side == 0 else z + far
            cond = plane >= 0 if side == 0 else plane <= 3
            more = z < 3 if side == 0 else z > 0
            to = "u" if side == 0 else "d"
            slot = {1: 7 + 3 * side, 2: 13, 3: 15}[far]
            slot_p = {1: 17 + side, 2: 19, 3: 20}[far]
            if part == "A":

                @pl.when(cond)
                def _():
                    self.got(plane, ALL, q, "A", to, 0, 1 + plane)

                if far < 3:
                    self.send(jnp.logical_and(cond, more), plane, ALL, q, "A", to, slot, 1 + plane)
                self.send(cond, plane, ALL, q, "A", "q", slot + 1, 5 + plane)
            else:

                @pl.when(cond)
                def _():
                    self.got(plane, p, q, "B", to, 0, 9 + plane)

                if far < 3:
                    self.send(jnp.logical_and(cond, more), plane, p, q, "B", to, slot + 2, 9 + plane)
                self.send(cond, plane, p, q, "B", "p", slot_p, 13 + plane)

    def line_a(self, far):
        self.line("A", far)

    def line_b(self, far):
        self.line("B", far)

    def cross(self, turn):
        plane = nearest(self.z, turn)
        self.got(plane, 1 - self.p, self.q, "B", "p", 0, 13 + plane)
        self.send(None, plane, ALL, self.q, "B", "q", 21 + turn, 5 + plane)

    def hand_on(self, turn):
        plane = nearest(self.z, turn)
        self.got(plane, ALL, 1 - self.q, "F", "q", 0, 5 + plane)
        self.send(None, plane, ALL, ALL, "F", "s", 25 + turn, 17 + plane)

    def take(self, turn):
        plane = nearest(self.z, turn)
        self.relay.copy(self.g, 1 - self.c, plane, ALL, ALL, "F", "s", 0, 17 + plane).wait_recv()


class Gather:
    def __init__(self, relay):
        self.relay = relay
        self.steps = [[Steps(relay, g, c) for g in range(len(GROUPS))] for c in (0, 1)]

    def __call__(self, name, g, *where):
        for core in (0, 1):

            @pl.when(self.relay.c == core)
            def _():
                getattr(self.steps[core][g], name)(*where)


def dot_nn(left, right):
    return jnp.dot(left, right, preferred_element_type=WIDE)


def dot_nt(left, right):
    return lax.dot_general(left, right, (((1,), (1,)), ((), ())), preferred_element_type=WIDE)


def dot_tn(left, right):
    return lax.dot_general(left, right, (((0,), (0,)), ((), ())), preferred_element_type=WIDE)


def standardise(resid):
    centred = resid - jnp.mean(resid, axis=-1, keepdims=True)
    inverse = lax.rsqrt(jnp.mean(centred * centred, axis=-1, keepdims=True) + eps_norm)
    return centred * inverse, inverse


def standardise_back(normed, inverse, grad):
    along = jnp.mean(grad * normed, axis=-1, keepdims=True)
    return inverse * (grad - jnp.mean(grad, axis=-1, keepdims=True) - normed * along)


def layer_kernel(grad_scale, *refs):
    (
        tokens_in,
        cotangent_in,
        seg_lengths,
        attn_piece,
        out_piece,
        inner_piece,
        branch_piece,
        lin_biases,
        ffn_bias,
        norm_gains,
        norm_biases,
        down_piece,
        up_piece,
        scale_d,
        scale_b,
        output,
        input_grad,
        d_grad,
        b_grad,
        vera,
        square,
        inner_t,
        branch_w,
        scales,
        same,
        low,
        extra_q,
        extra_v,
        query,
        key,
        value,
        probs,
        context,
        normed_one,
        inverse_one,
        resid,
        narrow_one,
        hidden,
        slope,
        out_stage,
        grad_stage,
        plane_sums,
        line_sums,
        bias_row,
        tokens,
        cotangent,
        own_sems,
        send_sems,
        recv_sems,
        local_sems,
        sum_sems,
    ) = refs
    relay = Relay((vera, square, inner_t, branch_w), own_sems, send_sems, recv_sems)
    gather = Gather(relay)
    z, y, c, x = relay.z, relay.y, relay.c, relay.x
    spot = c * 4 + y * 2 + x

    def in_plane(turn):
        other = lax.rem(spot + turn, PLANE)
        return other, relay.device(z, (other // 2) % 2, other // 4, other % 2)

    def in_line(turn):
        other = lax.rem(z + turn, LINE)
        return other, relay.device(other, y, c, x)

    mine = [
        pltpu.make_async_copy(up_piece, vera.at[z, y, c, x, 1], local_sems.at[0]),
        pltpu.make_async_copy(attn_piece, square.at[z, y, c, x, pl.ds(0, 3)], local_sems.at[1]),
        pltpu.make_async_copy(out_piece, square.at[z, y, c, x, 3], local_sems.at[2]),
        pltpu.make_async_copy(branch_piece, branch_w.at[z, y, c, x], local_sems.at[3]),
        pltpu.make_async_copy(scale_d, scales.at[x], local_sems.at[4]),
        pltpu.make_async_copy(inner_piece, inner_t.at[z, y, c, x], local_sems.at[5]),
        pltpu.make_async_copy(down_piece, vera.at[z, y, c, x, 0], local_sems.at[6]),
    ]
    tokens_copy = pltpu.make_async_copy(tokens_in, tokens, local_sems.at[7])
    cotangent_copy = pltpu.make_async_copy(cotangent_in, cotangent, local_sems.at[8])
    for copy in mine + [tokens_copy, cotangent_copy]:
        copy.start()
    barrier = pltpu.get_barrier_semaphore()

    def greet(device):
        pl.semaphore_signal(barrier, 1, device_id=device, device_id_type=MESH_IDS)

    greet(relay.device(z, y, 1 - c, x))
    greet(relay.device(z, y, c, 1 - x))
    greet(relay.device(z, 1 - y, c, x))

    @pl.when(z < 3)
    def _():
        greet(relay.device(z + 1, y, c, x))

    @pl.when(z > 0)
    def _():
        greet(relay.device(z - 1, y, c, x))

    for copy in mine:
        copy.wait()
    pl.semaphore_wait(barrier, 3 + jnp.where(z < 3, 1, 0) + jnp.where(z > 0, 1, 0))

    scale_copy = pltpu.make_async_remote_copy(
        scales.at[x],
        scales.at[x],
        sum_sems.at[0],
        sum_sems.at[1],
        device_id=relay.device(z, y, c, 1 - x),
        device_id_type=MESH_IDS,
    )
    scale_copy.start()

    def segments(seq):
        row_place = lax.broadcasted_iota(jnp.int32, (256, 256), 0)
        col_place = lax.broadcasted_iota(jnp.int32, (256, 256), 1)
        row_label = jnp.zeros((256, 256), jnp.int32)
        col_label = jnp.zeros((256, 256), jnp.int32)
        end = jnp.int32(0)
        for k in range(seg_lengths.shape[1]):
            end = end + seg_lengths[seq, k]
            row_label = row_label + (row_place >= end).astype(jnp.int32)
            col_label = col_label + (col_place >= end).astype(jnp.int32)
        same[seq] = jnp.where(row_label == col_label, 0.0, neg_big)

    def row(ref, k):
        return ref[k : k + 1, :].astype(WIDE)

    def rows_of(i):
        return pl.ds(pl.multiple_of(i * 256, 256), 256)

    def down_t(h):
        return vera[:, :, :, h, 0].reshape(768, 512)

    def up(h):
        return vera[:, :, :, h, 1].reshape(768, 512)

    def weight(k):
        return square[:, :, :, :, k].reshape(768, 768)

    def steps_at(i, relays):
        for k, steps in relays.items():

            @pl.when(i == k)
            def _():
                for step in steps:
                    take_step(step)

    def adapters(i):
        rows = rows_of(i)
        token_rows = tokens[rows, :]
        parts_q, parts_v = [], []
        for h in range(2):
            lowrank = dot_nn(token_rows, down_t(h))
            low[rows, h * 512 : (h + 1) * 512] = lowrank
            parts_q.append(dot_nt((scales[h, 0:1, :].astype(WIDE) * lowrank).astype(NARROW), up(h)))
            parts_v.append(dot_nt((scales[h, 1:2, :].astype(WIDE) * lowrank).astype(NARROW), up(h)))
        extra_q[rows, :] = parts_q[0] + parts_q[1]
        extra_v[rows, :] = parts_v[0] + parts_v[1]

    def project_key():
        key[...] = dot_nn(tokens[...], weight(1)).astype(NARROW)

    def project_query():
        total = dot_nn(tokens[...], weight(0)) + row(lin_biases, 0) + row(scale_b, 0) * extra_q[...]
        query[...] = (total * HEAD ** (-0.5)).astype(NARROW)

    def project_value():
        total = dot_nn(tokens[...], weight(2)) + row(lin_biases, 1) + row(scale_b, 1) * extra_v[...]
        value[...] = total.astype(NARROW)

    def head_cols(j):
        return pl.ds(pl.multiple_of(j * 128, 128), 128)

    lane = lax.broadcasted_iota(jnp.int32, (256, 128), 1)
    first_half = lane < HEAD

    def attend_pair(it):
        seq, j = it // 6, lax.rem(it, 6)
        rows, cols = rows_of(seq), head_cols(j)
        q_pair, k_pair, v_pair = query[rows, cols], key[rows, cols], value[rows, cols]
        zero = jnp.zeros_like(q_pair)
        queries = jnp.concatenate([jnp.where(first_half, q_pair, zero), jnp.where(first_half, zero, q_pair)])
        both = dot_nt(queries, k_pair)
        parts = []
        for half in range(2):
            scores = both[half * 256 : (half + 1) * 256] + same[seq]
            peak = jnp.max(scores, axis=-1, keepdims=True)
            exponent = jnp.exp(scores - peak)
            total = jnp.sum(exponent, axis=-1, keepdims=True)
            soft = (exponent * (1.0 / total)).astype(NARROW)
            probs[it * 2 + half] = soft
            parts.append(soft)
        both = dot_nn(jnp.concatenate(parts), v_pair)
        context[rows, cols] = jnp.where(first_half, both[:256], both[256:]).astype(NARROW)

    def close_attention(i):
        rows = rows_of(i)
        attended = dot_nn(context[rows, :], weight(3)) + row(lin_biases, 2)
        normed, inverse = standardise(tokens[rows, :].astype(WIDE) + attended)
        normed_one[rows, :] = normed
        inverse_one[rows, :] = inverse
        scaled = normed * row(norm_gains, 0) + row(norm_biases, 0)
        narrow_one[rows, :] = scaled.astype(NARROW)
        resid[rows, :] = scaled + row(lin_biases, 3)

    def hidden_cols(plane):
        return pl.ds(pl.multiple_of(plane * 768, 768), 768)

    def inner_block(it):
        turn, i = it // 2, lax.rem(it, 2)
        plane = nearest(z, turn)
        rows, cols = rows_of(i), hidden_cols(plane)
        block = dot_nt(narrow_one[rows, :], inner_t[plane].reshape(768, 768))
        block = block + bias_row[0:1, cols]
        below = 0.5 + 0.5 * lax.erf(block * 0.7071067811865476)
        hidden[rows, cols] = (block * below).astype(NARROW)
        slope[rows, cols] = (below + block * jnp.exp(-0.5 * block * block) * 0.3989422804014327).astype(NARROW)

    def branch_block(turn):
        plane = nearest(z, turn)
        resid[...] += dot_nn(hidden[:, hidden_cols(plane)], branch_w[plane].reshape(768, 768))

    def attend(it):
        attend_pair(2 * it)
        attend_pair(2 * it + 1)

    bodies = {
        "adapters": (2, adapters),
        "project_key": (1, lambda i: project_key()),
        "project_query": (1, lambda i: project_query()),
        "project_value": (1, lambda i: project_value()),
        "attend": (3, lambda k: (attend(2 * k), attend(2 * k + 1))),
        "close": (2, close_attention),
        "inner": (8, inner_block),
        "branch": (4, branch_block),
    }

    def take_step(step):
        if step[0] == "scales":
            bias_row[...] = ffn_bias[...].astype(WIDE).reshape(1, -1)
            segments(0)
            segments(1)
            scale_copy.wait()
            tokens_copy.wait()
        else:
            gather(*step)

    at = 0
    while at < len(SCHEDULE):
        name = SCHEDULE[at][0]
        if name not in bodies:
            take_step(SCHEDULE[at])
            at += 1
            continue
        count, body = bodies[name]
        between = {}
        done = 0
        while done < count - 1:
            at += 1
            if SCHEDULE[at][0] == name:
                done += 1
            else:
                between.setdefault(done + 1, []).append(SCHEDULE[at])
        at += 1
        if count == 1:
            body(0)
        else:

            @pl.loop(0, count)
            def _(i):
                steps_at(i, between)
                body(i)

    cotangent_copy.wait()

    for i in range(2):
        rows = slice(i * 256, (i + 1) * 256)
        normed, inverse = standardise(resid[rows, :])
        gain = row(norm_gains, 1)
        out_stage[rows, :] = (normed * gain + row(norm_biases, 1)).astype(NARROW)
        grad = standardise_back(normed, inverse, cotangent[rows, :].astype(WIDE) * gain)
        resid[rows, :] = grad
        narrow_one[rows, :] = grad.astype(NARROW)

    out_copy = pltpu.make_async_copy(out_stage, output, local_sems.at[0])
    out_copy.start()

    for plane in range(4):
        cols = slice(plane * 768, (plane + 1) * 768)
        for i in range(2):
            rows = slice(i * 256, (i + 1) * 256)
            grad = dot_nt(narrow_one[rows, :], branch_w[plane].reshape(768, 768)).astype(NARROW)
            hidden[rows, cols] = (slope[rows, cols].astype(WIDE) * grad.astype(WIDE)).astype(NARROW)

    for i in range(2):
        rows = slice(i * 256, (i + 1) * 256)
        grad = resid[rows, :] + dot_nn(hidden[rows, :], inner_t[...].reshape(3072, 768))
        grad = standardise_back(normed_one[rows, :], inverse_one[rows, :], grad * row(norm_gains, 0))
        resid[rows, :] = grad
        narrow_one[rows, :] = dot_nt(grad.astype(NARROW), weight(3)).astype(NARROW)

    def attend_back(it):
        seq, j = it // 6, lax.rem(it, 6)
        rows, cols = rows_of(seq), head_cols(j)
        k_pair, v_pair, grad = key[rows, cols], value[rows, cols], narrow_one[rows, cols]
        product = (grad.astype(WIDE) * context[rows, cols].astype(WIDE)).astype(NARROW)
        zero = jnp.zeros_like(grad)
        left = jnp.concatenate([jnp.where(first_half, grad, zero), jnp.where(first_half, zero, grad)])
        sums = jnp.concatenate([jnp.where(first_half, -product, zero), jnp.where(first_half, zero, -product)])
        change = dot_nt(
            jnp.concatenate([left, sums], axis=1), jnp.concatenate([v_pair, jnp.ones_like(v_pair)], axis=1)
        )
        soft = [probs[it * 2 + half] for half in range(2)]
        grad_scores = [
            (soft[half].astype(WIDE) * change[half * 256 : (half + 1) * 256]).astype(NARROW) for half in range(2)
        ]
        grad_q = dot_nn(jnp.concatenate(grad_scores), k_pair)
        grad_v = dot_tn(jnp.concatenate(soft, axis=1), grad)
        for half in range(2):
            probs[it * 2 + half] = grad_scores[half]
        narrow_one[rows, cols] = (jnp.where(first_half, grad_q[:256], grad_q[256:]) * HEAD ** (-0.5)).astype(NARROW)
        value[rows, cols] = jnp.where(first_half, grad_v[:256], grad_v[256:]).astype(NARROW)

    def key_back(it):
        rows, cols = rows_of(it // 6), head_cols(lax.rem(it, 6))
        both = jnp.concatenate([probs[it * 2], probs[it * 2 + 1]], axis=1)
        grad_k = dot_tn(both, query[rows, cols])
        key[rows, cols] = jnp.where(first_half, grad_k[:256], grad_k[256:]).astype(NARROW)

    @pl.loop(0, 2)
    def _(it):
        for k in range(6):
            attend_back(6 * it + k)

    plane_sums[spot] = jnp.zeros((4, 1024), WIDE)
    low_grad = hidden

    for i in range(2):
        rows = slice(i * 256, (i + 1) * 256)
        grad_q, grad_v = narrow_one[rows, :].astype(WIDE), value[rows, :].astype(WIDE)
        plane_sums[spot, 2:3, 0:768] += jnp.sum(extra_q[rows, :] * grad_q, axis=0, keepdims=True)
        plane_sums[spot, 3:4, 0:768] += jnp.sum(extra_v[rows, :] * grad_v, axis=0, keepdims=True)
        grad_q = (row(scale_b, 0) * grad_q).astype(NARROW)
        grad_v = (row(scale_b, 1) * grad_v).astype(NARROW)
        for h in range(2):
            half = slice(h * 512, (h + 1) * 512)
            scaled_q, scaled_v = dot_nn(grad_q, up(h)), dot_nn(grad_v, up(h))
            plane_sums[spot, 0:1, half] += jnp.sum(low[rows, half] * scaled_q, axis=0, keepdims=True)
            plane_sums[spot, 1:2, half] += jnp.sum(low[rows, half] * scaled_v, axis=0, keepdims=True)
            total = scales[h, 0:1, :].astype(WIDE) * scaled_q + scales[h, 1:2, :].astype(WIDE) * scaled_v
            low_grad[rows, half] = total.astype(NARROW)

    def plane_copy(turn, slot):
        return pltpu.make_async_remote_copy(
            plane_sums.at[slot],
            plane_sums.at[slot],
            sum_sems.at[1 + turn],
            sum_sems.at[9 + slot],
            device_id=in_plane(turn)[1],
            device_id_type=MESH_IDS,
        )

    def line_copy(turn, slot):
        return pltpu.make_async_remote_copy(
            line_sums.at[slot],
            line_sums.at[slot],
            sum_sems.at[16 + turn],
            sum_sems.at[20 + slot],
            device_id=in_line(turn)[1],
            device_id_type=MESH_IDS,
        )

    def input_rows(i):
        rows = slice(i * 256, (i + 1) * 256)
        total = resid[rows, :] + dot_nt(narrow_one[rows, :], weight(0))
        total = total + dot_nt(key[rows, :], weight(1))
        total = total + dot_nt(value[rows, :], weight(2))
        for h in range(2):
            total = total + dot_nt(low_grad[rows, h * 512 : (h + 1) * 512], down_t(h))
        grad_stage[rows, :] = total.astype(NARROW)
        return pltpu.make_async_copy(grad_stage.at[rows, :], input_grad.at[rows, :], local_sems.at[1 + i])

    for turn in range(1, PLANE):
        plane_copy(turn, spot).start()

    @pl.loop(0, 2)
    def _(it):
        for k in range(6):
            key_back(6 * it + k)

    for turn in range(1, PLANE):
        plane_copy(turn, in_plane(turn)[0]).wait_recv()
    total = plane_sums[0]
    for other in range(1, PLANE):
        total = total + plane_sums[other]
    line_sums[z] = total
    for turn in range(1, LINE):
        line_copy(turn, z).start()
    grad_copies = []
    for i in range(2):
        grad_copies.append(input_rows(i))
        grad_copies[i].start()
    for turn in range(1, LINE):
        line_copy(turn, in_line(turn)[0]).wait_recv()
    cols = pl.ds(pl.multiple_of(x * 512, 512), 512)
    total_d, total_b = line_sums[0, 0:2, cols], line_sums[0, 2:4, 0:768]
    for other in range(1, LINE):
        total_d = total_d + line_sums[other, 0:2, cols]
        total_b = total_b + line_sums[other, 2:4, 0:768]
    d_grad[...] = total_d * grad_scale
    b_grad[...] = total_b * grad_scale

    for turn in range(1, PLANE):
        plane_copy(turn, spot).wait_send()
    for turn in range(1, LINE):
        line_copy(turn, z).wait_send()
    for g in range(len(GROUPS)):
        gather("finish", g)
    out_copy.wait()
    for copy in grad_copies:
        copy.wait()


def settle_kernel(*refs):
    sources, targets, stages, sems = refs[:4], refs[4:8], refs[8:12], refs[12]
    halves = [(0, 0, 256), (0, 256, 256), (1, 0, 256), (1, 256, 256), (2, 0, 2), (3, 0, 2)]
    loads, stores = [], []
    for n, (k, start, size) in enumerate(halves):
        part = pl.ds(start, size)
        loads.append(pltpu.make_async_copy(sources[k].at[part], stages[k].at[part], sems.at[0, n]))
        stores.append(pltpu.make_async_copy(stages[k].at[part], targets[k].at[part], sems.at[1, n]))
    for load in loads:
        load.start()
    for load, store in zip(loads, stores):
        load.wait()
        store.start()
    for store in stores:
        store.wait()


def settle(results):
    anywhere = pl.BlockSpec(memory_space=pl.ANY)
    return pl.pallas_call(
        settle_kernel,
        out_shape=[jax.ShapeDtypeStruct(result.shape, result.dtype) for result in results],
        in_specs=[anywhere] * 4,
        out_specs=[anywhere] * 4,
        scratch_shapes=[pltpu.VMEM(result.shape, result.dtype) for result in results]
        + [pltpu.SemaphoreType.DMA((2, 6))],
    )(*results)


def fused_layer(
    tokens,
    cotangent,
    seg_lengths,
    attn_weights,
    out_weight,
    ffn_in,
    ffn_out,
    lin_biases,
    ffn_bias,
    norm_gains,
    norm_biases,
    shared_down,
    shared_up,
    scale_d,
    scale_b,
):
    rows, width = tokens.shape[0] * tokens.shape[1] * tokens.shape[2], tokens.shape[3]
    devices = lax.axis_size("dp") * lax.axis_size("rank")
    in_vmem, anywhere = pl.BlockSpec(memory_space=pltpu.VMEM), pl.BlockSpec(memory_space=pl.ANY)
    in_smem = pl.BlockSpec(memory_space=pltpu.SMEM)
    shapes = [(4, 2, 2, 2) + lead + (cols,) for lead, cols, _ in GROUPS]
    flat = (rows, width)
    scratch = [pltpu.VMEM(shape, NARROW) for shape in shapes] + [
        pltpu.VMEM((2, 2, 512), NARROW),
        pltpu.VMEM((2, 256, 256), WIDE),
        pltpu.VMEM((rows, 1024), WIDE),
        pltpu.VMEM(flat, WIDE),
        pltpu.VMEM(flat, WIDE),
        pltpu.VMEM(flat, NARROW),
        pltpu.VMEM(flat, NARROW),
        pltpu.VMEM(flat, NARROW),
        pltpu.VMEM((24, 256, 256), NARROW),
        pltpu.VMEM(flat, NARROW),
        pltpu.VMEM(flat, WIDE),
        pltpu.VMEM((rows, 1), WIDE),
        pltpu.VMEM(flat, WIDE),
        pltpu.VMEM(flat, NARROW),
        pltpu.VMEM((rows, 3072), NARROW),
        pltpu.VMEM((rows, 3072), NARROW),
        pltpu.VMEM(flat, NARROW),
        pltpu.VMEM(flat, NARROW),
        pltpu.VMEM((PLANE, 4, 1024), WIDE),
        pltpu.VMEM((LINE, 4, 1024), WIDE),
        pltpu.VMEM((1, 3072), WIDE),
        pltpu.VMEM(flat, NARROW),
        pltpu.VMEM(flat, NARROW),
        pltpu.SemaphoreType.DMA((len(GROUPS), 4)),
        pltpu.SemaphoreType.DMA((2, SEND_SLOTS - 4)),
        pltpu.SemaphoreType.DMA((len(GROUPS), RECV_SLOTS)),
        pltpu.SemaphoreType.DMA((9,)),
        pltpu.SemaphoreType.DMA((24,)),
    ]
    results = pl.pallas_call(
        functools.partial(layer_kernel, 1.0 / math.sqrt(rows * devices)),
        out_shape=(
            jax.ShapeDtypeStruct(flat, NARROW),
            jax.ShapeDtypeStruct(flat, NARROW),
            jax.ShapeDtypeStruct((2, 512), WIDE),
            jax.ShapeDtypeStruct((2, 768), WIDE),
        ),
        in_specs=[anywhere, anywhere, in_smem]
        + [anywhere] * 4
        + [in_vmem] * 4
        + [anywhere] * 3
        + [in_vmem],
        out_specs=(anywhere, anywhere, in_vmem, in_vmem),
        scratch_shapes=scratch,
        compiler_params=pltpu.CompilerParams(
            collective_id=0, has_side_effects=True, vmem_limit_bytes=61 << 20
        ),
    )(
        tokens.reshape(flat),
        cotangent.reshape(flat),
        seg_lengths.reshape(-1, seg_lengths.shape[-1]),
        attn_weights,
        out_weight,
        ffn_in.T,
        ffn_out,
        lin_biases,
        ffn_bias,
        norm_gains,
        norm_biases,
        shared_down.T,
        shared_up,
        scale_d,
        scale_b,
    )
    output, input_grad, d_grad, b_grad = settle(results)
    return output.reshape(tokens.shape), input_grad.reshape(tokens.shape), d_grad, b_grad


def gather_weights(attn_weights, out_weight, ffn_in, ffn_out, shared_down, shared_up):
    down_local = lax.all_gather(shared_down, "dp", axis=1, tiled=True)
    up_local = lax.all_gather(shared_up, "dp", axis=0, tiled=True)
    return (
        lax.all_gather(attn_weights, ("dp", "rank"), axis=1, tiled=True),
        lax.all_gather(out_weight, ("dp", "rank"), axis=0, tiled=True),
        lax.all_gather(ffn_in, ("dp", "rank"), axis=1, tiled=True),
        lax.all_gather(ffn_out, ("dp", "rank"), axis=0, tiled=True),
        lax.all_gather(down_local, "rank", axis=0, tiled=True),
        lax.all_gather(up_local, "rank", axis=1, tiled=True),
    )


def per_device(
    tokens,
    cotangent,
    seg_lengths,
    attn_weights,
    out_weight,
    ffn_in,
    ffn_out,
    lin_biases,
    ffn_bias,
    norm_gains,
    norm_biases,
    shared_down,
    shared_up,
    scale_d,
    scale_b,
):
    micro_count, seq_count, length_rows, model_width = tokens.shape
    head_count = model_width // HEAD
    out_shape = tokens.shape
    seq_count = micro_count * seq_count
    row_count = seq_count * length_rows
    head_shape = (seq_count, length_rows, head_count, HEAD)
    float_wide = jnp.float32
    narrow = jnp.bfloat16
    attn_full, output_full, inner_full, branch_full, down_use, up_use = gather_weights(
        attn_weights, out_weight, ffn_in, ffn_out, shared_down, shared_up
    )
    scales_use = lax.all_gather(scale_d, "rank", axis=1, tiled=True)
    rank_cols = scales_use.shape[1]
    sum_d = jnp.zeros((2, rank_cols), float_wide)
    sum_b = jnp.zeros((2, model_width), float_wide)
    outputs = []
    input_grads = []
    for micro_step in range(1):
        token_rows = tokens.reshape(row_count, model_width)
        same_segment = segment_match(seg_lengths.reshape(seq_count, -1), length_rows)
        lowrank = jnp.einsum("rd,kd->rk", token_rows, down_use, preferred_element_type=float_wide)
        scaled = (scales_use[:, None, :] * lowrank[None]).astype(narrow)
        adapted = jnp.concatenate(
            [
                jnp.einsum("rk,dk->rd", scaled[0], up_use, preferred_element_type=float_wide),
                jnp.einsum("rk,dk->rd", scaled[1], up_use, preferred_element_type=float_wide),
            ],
            axis=1,
        )
        extra_query = adapted[:, :model_width]
        extra_value = adapted[:, model_width:]
        query_rows = (
            jnp.dot(token_rows, attn_full[0], preferred_element_type=float_wide)
            + lin_biases[0]
            + scale_b[0] * extra_query
        ).astype(narrow)
        key_rows = jnp.dot(token_rows, attn_full[1], preferred_element_type=float_wide).astype(
            narrow
        )
        value_rows = (
            jnp.dot(token_rows, attn_full[2], preferred_element_type=float_wide)
            + lin_biases[1]
            + scale_b[1] * extra_value
        ).astype(narrow)
        query_heads = query_rows.reshape(head_shape)
        key_heads = key_rows.reshape(head_shape)
        value_heads = value_rows.reshape(head_shape)
        context, log_total = attend(query_heads, key_heads, value_heads, same_segment)
        attended = (
            jnp.dot(
                context.reshape(row_count, model_width),
                output_full,
                preferred_element_type=float_wide,
            )
            + lin_biases[2]
        )
        resid_one = token_rows.astype(float_wide) + attended
        normed_one = layer_norm(resid_one, norm_gains[0], norm_biases[0])
        inner_pre = (
            jnp.dot(normed_one.astype(narrow), inner_full, preferred_element_type=float_wide)
            + ffn_bias
        )
        hidden = gelu_exact(inner_pre).astype(narrow)
        branch = jnp.dot(hidden, branch_full, preferred_element_type=float_wide) + lin_biases[3]
        resid_two = normed_one + branch
        outputs.append(
            layer_norm(resid_two, norm_gains[1], norm_biases[1])
            .astype(narrow)
            .reshape(out_shape)
        )
        grad_out = cotangent.reshape(row_count, model_width).astype(float_wide)
        grad_two = norm_back(resid_two, norm_gains[1], norm_biases[1], grad_out)
        grad_hidden = jnp.einsum(
            "rd,fd->rf", grad_two.astype(narrow), branch_full, preferred_element_type=float_wide
        ).astype(narrow)
        grad_inner = gelu_back(inner_pre, grad_hidden.astype(float_wide)).astype(narrow)
        grad_normed = grad_two + jnp.einsum(
            "rf,df->rd", grad_inner, inner_full, preferred_element_type=float_wide
        )
        grad_one = norm_back(resid_one, norm_gains[0], norm_biases[0], grad_normed)
        grad_attended = grad_one.astype(narrow)
        grad_context = jnp.einsum(
            "ro,io->ri", grad_attended, output_full, preferred_element_type=float_wide
        ).astype(narrow)
        grad_query, grad_keys, grad_values = attend_back(
            query_heads,
            key_heads,
            value_heads,
            same_segment,
            log_total,
            grad_context.reshape(head_shape),
        )
        query_grad = grad_query.reshape(row_count, model_width).astype(narrow)
        key_grad = grad_keys.reshape(row_count, model_width).astype(narrow)
        value_grad = grad_values.reshape(row_count, model_width).astype(narrow)
        grad_input = grad_one + jnp.einsum(
            "ro,io->ri", query_grad, attn_full[0], preferred_element_type=float_wide
        )
        grad_input = grad_input + jnp.einsum(
            "ro,io->ri", key_grad, attn_full[1], preferred_element_type=float_wide
        )
        grad_input = grad_input + jnp.einsum(
            "ro,io->ri", value_grad, attn_full[2], preferred_element_type=float_wide
        )
        query_grad_wide = query_grad.astype(float_wide)
        value_grad_wide = value_grad.astype(float_wide)
        sum_b = sum_b + jnp.stack(
            [
                jnp.sum(extra_query * query_grad_wide, axis=0),
                jnp.sum(extra_value * value_grad_wide, axis=0),
            ]
        )
        grad_extra = jnp.concatenate(
            [
                (scale_b[0] * query_grad_wide).astype(narrow),
                (scale_b[1] * value_grad_wide).astype(narrow),
            ],
            axis=1,
        )
        grad_scaled = jnp.concatenate(
            [
                jnp.dot(grad_extra[:, :model_width], up_use, preferred_element_type=float_wide),
                jnp.dot(grad_extra[:, model_width:], up_use, preferred_element_type=float_wide),
            ],
            axis=1,
        )
        grad_scaled_query = grad_scaled[:, :rank_cols]
        grad_scaled_value = grad_scaled[:, rank_cols:]
        sum_d = sum_d + jnp.stack(
            [
                jnp.sum(lowrank * grad_scaled_query, axis=0),
                jnp.sum(lowrank * grad_scaled_value, axis=0),
            ]
        )
        grad_lowrank = (
            scales_use[0] * grad_scaled_query + scales_use[1] * grad_scaled_value
        ).astype(narrow)
        grad_from_adapter = jnp.dot(grad_lowrank, down_use, preferred_element_type=float_wide)
        input_grads.append(
            (grad_input + grad_from_adapter)
            .astype(narrow)
            .reshape(out_shape)
        )
    grad_scale = 1.0 / math.sqrt(
        row_count * lax.axis_size("dp") * lax.axis_size("rank")
    )
    total_d, total_b = lax.psum((sum_d, sum_b), ("dp", "rank"))
    local_cols = scale_d.shape[1]
    total_d = lax.dynamic_slice_in_dim(total_d, lax.axis_index("rank") * local_cols, local_cols, 1)
    return (outputs[0], input_grads[0], total_d * grad_scale, total_b * grad_scale)


def solution(mesh):
    return jax.shard_map(
        fused_layer if (mesh.shape["dp"], mesh.shape["rank"]) == (16, 2) else per_device,
        mesh=mesh,
        in_specs=(
            P(None, ("dp", "rank"), None, None),
            P(None, ("dp", "rank"), None, None),
            P(None, ("dp", "rank"), None),
            P(None, ("dp", "rank"), None),
            P(("dp", "rank"), None),
            P(None, ("dp", "rank")),
            P(("dp", "rank"), None),
            P(),
            P(),
            P(),
            P(),
            P("rank", "dp"),
            P("dp", "rank"),
            P(None, "rank"),
            P(),
        ),
        out_specs=(
            P(None, ("dp", "rank"), None, None),
            P(None, ("dp", "rank"), None, None),
            P(None, "rank"),
            P(),
        ),
        check_vma=False,
    )
```

```python
import functools
import math

import jax
import jax.numpy as jnp
from jax import lax
from jax.experimental import pallas as pl
from jax.experimental.pallas import tpu as pltpu
from jax.sharding import PartitionSpec as P

HEAD = 64


eps_norm = 1e-05
neg_big = -1000000000.0


def layer_norm(resid, norm_gain, norm_shift):
    row_mean = jnp.mean(resid, axis=-1, keepdims=True)
    centred = resid - row_mean
    variance = jnp.mean(centred * centred, axis=-1, keepdims=True)
    return centred * lax.rsqrt(variance + eps_norm) * norm_gain + norm_shift


def norm_back(resid, norm_gain, norm_shift, grad_normed):

    def forward_norm(values_in):
        return layer_norm(values_in, norm_gain, norm_shift)

    pullback = jax.vjp(forward_norm, resid)[1]
    return pullback(grad_normed)[0]


def gelu_exact(values_in):
    return jax.nn.gelu(values_in, approximate=False)


def gelu_back(inner_pre, grad_hidden):
    pullback = jax.vjp(gelu_exact, inner_pre)[1]
    return pullback(grad_hidden)[0]


def segment_match(lengths, length_rows):
    cumulative = jnp.cumsum(lengths, axis=-1)
    places = jnp.arange(length_rows, dtype=jnp.int32)
    labels = jnp.sum((places[None, :, None] >= cumulative[:, None, :]).astype(jnp.int32), axis=-1)
    return labels[:, :, None] == labels[:, None, :]


def masked_scores(query_heads, key_heads, same_segment):
    scores = jnp.einsum(
        "sqhe,skhe->shqk", query_heads, key_heads, preferred_element_type=jnp.float32
    ) * HEAD ** (-0.5)
    return jnp.where(same_segment[:, None], scores, neg_big)


def attend(query_heads, key_heads, value_heads, same_segment):
    scores = masked_scores(query_heads, key_heads, same_segment)
    row_peak = jnp.max(scores, axis=-1, keepdims=True)
    exponent = jnp.exp(scores - row_peak)
    row_total = jnp.sum(exponent, axis=-1, keepdims=True)
    weights_soft = (exponent / row_total).astype(jnp.bfloat16)
    context = jnp.einsum(
        "shqk,skhe->sqhe", weights_soft, value_heads, preferred_element_type=jnp.float32
    )
    return (context.astype(jnp.bfloat16), row_peak + jnp.log(row_total))


def attend_back(query_heads, key_heads, value_heads, same_segment, log_total, grad_context):
    scores = masked_scores(query_heads, key_heads, same_segment)
    weights_soft = jnp.exp(scores - log_total)
    grad_values = jnp.einsum(
        "shqk,sqhe->skhe",
        weights_soft.astype(jnp.bfloat16),
        grad_context,
        preferred_element_type=jnp.float32,
    )
    grad_weights = jnp.einsum(
        "sqhe,skhe->shqk", grad_context, value_heads, preferred_element_type=jnp.float32
    )
    inner_sum = jnp.sum(grad_weights * weights_soft, axis=-1, keepdims=True)
    grad_scores = (weights_soft * (grad_weights - inner_sum)).astype(jnp.bfloat16)
    grad_query = jnp.einsum(
        "shqk,skhe->sqhe", grad_scores, key_heads, preferred_element_type=jnp.float32
    ) * HEAD ** (-0.5)
    grad_keys = jnp.einsum(
        "shqk,sqhe->skhe", grad_scores, query_heads, preferred_element_type=jnp.float32
    ) * HEAD ** (-0.5)
    return (grad_query, grad_keys, grad_values)


ALL = slice(None)
MESH_IDS = pl.DeviceIdType.MESH
WIDE = jnp.float32
NARROW = jnp.bfloat16
GROUPS = (((2, 48), 512, 256), ((4, 24), 768, 512), ((96,), 768, 384), ((96,), 768, 512))
VERA, SQUARE, INNER, BRANCH = range(4)
SCHEDULE = (
    ("own", SQUARE),
    ("own", VERA),
    ("own", INNER),
    ("line_b", SQUARE, 1),
    ("pair", VERA),
    ("pair", SQUARE),
    ("line_b", VERA, 1),
    ("cross", VERA, 0),
    ("line_a", VERA, 1),
    ("line_b", SQUARE, 2),
    ("cross", VERA, 1),
    ("pair", INNER),
    ("line_b", VERA, 2),
    ("cross", SQUARE, 0),
    ("line_a", SQUARE, 1),
    ("line_a", VERA, 2),
    ("cross", VERA, 2),
    ("line_b", INNER, 1),
    ("cross", SQUARE, 2),
    ("cross", INNER, 0),
    ("cross", SQUARE, 1),
    ("line_b", SQUARE, 3),
    ("line_b", VERA, 3),
    ("own", BRANCH),
    ("cross", VERA, 3),
    ("cross", SQUARE, 3),
    ("line_a", SQUARE, 2),
    ("hand_on", VERA, 0),
    ("cross", INNER, 1),
    ("hand_on", VERA, 2),
    ("hand_on", SQUARE, 1),
    ("line_a", VERA, 3),
    ("line_b", INNER, 2),
    ("take", SQUARE, 1),
    ("line_a", INNER, 1),
    ("line_b", BRANCH, 1),
    ("hand_on", VERA, 3),
    ("take", VERA, 0),
    ("line_a", SQUARE, 3),
    ("hand_on", VERA, 1),
    ("hand_on", SQUARE, 2),
    ("take", VERA, 3),
    ("hand_on", SQUARE, 0),
    ("line_b", INNER, 3),
    ("pair", BRANCH),
    ("hand_on", SQUARE, 3),
    ("cross", INNER, 3),
    ("take", VERA, 1),
    ("take", SQUARE, 0),
    ("take", VERA, 2),
    ("cross", INNER, 2),
    ("scales",),
    ("adapters", 0),
    ("take", SQUARE, 2),
    ("line_b", BRANCH, 2),
    ("hand_on", INNER, 0),
    ("adapters", 1),
    ("cross", BRANCH, 0),
    ("hand_on", INNER, 1),
    ("take", SQUARE, 3),
    ("project_key", 0),
    ("line_a", INNER, 2),
    ("line_a", BRANCH, 1),
    ("project_query", 0),
    ("project_value", 0),
    ("cross", BRANCH, 1),
    ("attend", 0),
    ("line_a", INNER, 3),
    ("attend", 1),
    ("attend", 2),
    ("take", INNER, 0),
    ("line_b", BRANCH, 3),
    ("cross", BRANCH, 2),
    ("hand_on", INNER, 2),
    ("close", 0),
    ("line_a", BRANCH, 2),
    ("close", 1),
    ("inner", 0),
    ("cross", BRANCH, 3),
    ("hand_on", INNER, 3),
    ("take", INNER, 1),
    ("inner", 1),
    ("inner", 2),
    ("hand_on", BRANCH, 0),
    ("inner", 3),
    ("take", INNER, 3),
    ("take", INNER, 2),
    ("hand_on", BRANCH, 1),
    ("line_a", BRANCH, 3),
    ("inner", 4),
    ("hand_on", BRANCH, 2),
    ("inner", 5),
    ("inner", 6),
    ("take", BRANCH, 1),
    ("inner", 7),
    ("take", BRANCH, 2),
    ("take", BRANCH, 0),
    ("branch", 0),
    ("hand_on", BRANCH, 3),
    ("branch", 1),
    ("branch", 2),
    ("take", BRANCH, 3),
    ("branch", 3),
)
SEND_SLOTS = 29
RECV_SLOTS = 21
LINE = 4
PLANE = 8


def nearest(z, turn):
    upper = z // 2
    inner = z * (1 - upper) + (3 - z) * upper
    plane = turn + inner * (1 - 2 * turn) * (1 - turn // 2)
    return plane * (1 - upper) + (3 - plane) * upper


class Relay:
    def __init__(self, buffers, own_sems, send_sems, recv_sems):
        self.buffers, self.own_sems, self.send_sems, self.recv_sems = buffers, own_sems, send_sems, recv_sems
        place = lax.axis_index("dp")
        self.x = lax.axis_index("rank")
        self.z, self.y, self.c = place // 4, (place // 2) % 2, place % 2

    def device(self, z, y, c, x):
        return {"dp": z * 4 + y * 2 + c, "rank": x}

    def neighbour(self, c, which):
        z, y, x = self.z, self.y, self.x
        if which == "s":
            return self.device(z, y, 1 - c, x)
        if which == "u":
            return self.device(z + 1, y, c, x)
        if which == "d":
            return self.device(z - 1, y, c, x)
        if (which == "p") == (c == 0):
            return self.device(z, y, c, 1 - x)
        return self.device(z, 1 - y, c, x)

    def view(self, g, c, plane, p, q, part):
        lead, cols, split = GROUPS[g]
        window = {"A": pl.ds(0, split), "B": pl.ds(split, cols - split), "F": pl.ds(0, cols)}[part]
        place = (plane, q, c, p) if c == 0 else (plane, p, c, q)
        return self.buffers[g].at[place + (ALL,) * len(lead) + (window,)]

    def copy(self, g, c, plane, p, q, part, to, send, recv):
        block = self.view(g, c, plane, p, q, part)
        return pltpu.make_async_remote_copy(
            block,
            block,
            self.own_sems.at[g, send] if send < 4 else self.send_sems.at[g % 2, send - 4],
            self.recv_sems.at[g, recv],
            device_id=self.neighbour(c, to),
            device_id_type=MESH_IDS,
        )


class Steps:
    def __init__(self, relay, g, c):
        self.relay, self.g, self.c = relay, g, c
        self.z = relay.z
        self.p, self.q = (relay.x, relay.y) if c == 0 else (relay.y, relay.x)
        self.closing = False

    def send(self, cond, *where):
        def act():
            copy = self.relay.copy(self.g, self.c, *where)
            if self.closing:
                copy.wait_send()
                return
            if self.g > 1 and where[-2] >= 4:
                self.relay.copy(self.g - 2, self.c, *where).wait_send()
            copy.start()

        if cond is None:
            act()
        else:
            pl.when(cond)(act)

    def finish(self):
        self.closing = True
        self.own()
        if self.g < 2:
            return
        self.pair()
        for far in (1, 2, 3):
            self.line_a(far)
            self.line_b(far)
        for turn in range(4):
            self.cross(turn)
            self.hand_on(turn)

    def got(self, *where):
        if not self.closing:
            self.relay.copy(self.g, self.c, *where).wait_recv()

    def own(self):
        z, p, q = self.z, self.p, self.q
        self.send(None, z, p, q, "A", "p", 0, 0)
        self.send(z < 3, z, p, q, "B", "u", 1, 9 + z)
        self.send(z > 0, z, p, q, "B", "d", 2, 9 + z)
        self.send(None, z, p, q, "B", "p", 3, 13 + z)

    def pair(self):
        z, p, q = self.z, self.p, self.q
        self.got(z, 1 - p, q, "A", "p", 0, 0)
        self.send(z < 3, z, ALL, q, "A", "u", 4, 1 + z)
        self.send(z > 0, z, ALL, q, "A", "d", 5, 1 + z)
        self.send(None, z, ALL, q, "A", "q", 6, 5 + z)

    def line(self, part, far):
        z, p, q = self.z, self.p, self.q
        for side in (0, 1):
            plane = z - far if side == 0 else z + far
            cond = plane >= 0 if side == 0 else plane <= 3
            more = z < 3 if side == 0 else z > 0
            to = "u" if side == 0 else "d"
            slot = {1: 7 + 3 * side, 2: 13, 3: 15}[far]
            slot_p = {1: 17 + side, 2: 19, 3: 20}[far]
            if part == "A":

                @pl.when(cond)
                def _():
                    self.got(plane, ALL, q, "A", to, 0, 1 + plane)

                if far < 3:
                    self.send(jnp.logical_and(cond, more), plane, ALL, q, "A", to, slot, 1 + plane)
                self.send(cond, plane, ALL, q, "A", "q", slot + 1, 5 + plane)
            else:

                @pl.when(cond)
                def _():
                    self.got(plane, p, q, "B", to, 0, 9 + plane)

                if far < 3:
                    self.send(jnp.logical_and(cond, more), plane, p, q, "B", to, slot + 2, 9 + plane)
                self.send(cond, plane, p, q, "B", "p", slot_p, 13 + plane)

    def line_a(self, far):
        self.line("A", far)

    def line_b(self, far):
        self.line("B", far)

    def cross(self, turn):
        plane = nearest(self.z, turn)
        self.got(plane, 1 - self.p, self.q, "B", "p", 0, 13 + plane)
        self.send(None, plane, ALL, self.q, "B", "q", 21 + turn, 5 + plane)

    def hand_on(self, turn):
        plane = nearest(self.z, turn)
        self.got(plane, ALL, 1 - self.q, "F", "q", 0, 5 + plane)
        self.send(None, plane, ALL, ALL, "F", "s", 25 + turn, 17 + plane)

    def take(self, turn):
        plane = nearest(self.z, turn)
        self.relay.copy(self.g, 1 - self.c, plane, ALL, ALL, "F", "s", 0, 17 + plane).wait_recv()


class Gather:
    def __init__(self, relay):
        self.relay = relay
        self.steps = [[Steps(relay, g, c) for g in range(len(GROUPS))] for c in (0, 1)]

    def __call__(self, name, g, *where):
        for core in (0, 1):

            @pl.when(self.relay.c == core)
            def _():
                getattr(self.steps[core][g], name)(*where)


def dot_nn(left, right):
    return jnp.dot(left, right, preferred_element_type=WIDE)


def dot_nt(left, right):
    return lax.dot_general(left, right, (((1,), (1,)), ((), ())), preferred_element_type=WIDE)


def dot_tn(left, right):
    return lax.dot_general(left, right, (((0,), (0,)), ((), ())), preferred_element_type=WIDE)


def standardise(resid):
    centred = resid - jnp.mean(resid, axis=-1, keepdims=True)
    inverse = lax.rsqrt(jnp.mean(centred * centred, axis=-1, keepdims=True) + eps_norm)
    return centred * inverse, inverse


def standardise_back(normed, inverse, grad):
    along = jnp.mean(grad * normed, axis=-1, keepdims=True)
    return inverse * (grad - jnp.mean(grad, axis=-1, keepdims=True) - normed * along)


def layer_kernel(grad_scale, *refs):
    (
        tokens_in,
        cotangent_in,
        seg_lengths,
        attn_piece,
        out_piece,
        inner_piece,
        branch_piece,
        lin_biases,
        ffn_bias,
        norm_gains,
        norm_biases,
        down_piece,
        up_piece,
        scale_d,
        scale_b,
        output,
        input_grad,
        d_grad,
        b_grad,
        vera,
        square,
        inner_t,
        branch_w,
        scales,
        same,
        low,
        extra_q,
        extra_v,
        query,
        key,
        value,
        probs,
        context,
        normed_one,
        inverse_one,
        resid,
        narrow_one,
        hidden,
        slope,
        out_stage,
        grad_stage,
        plane_sums,
        line_sums,
        bias_row,
        tokens,
        cotangent,
        own_sems,
        send_sems,
        recv_sems,
        local_sems,
        sum_sems,
    ) = refs
    relay = Relay((vera, square, inner_t, branch_w), own_sems, send_sems, recv_sems)
    gather = Gather(relay)
    z, y, c, x = relay.z, relay.y, relay.c, relay.x
    spot = c * 4 + y * 2 + x

    def in_plane(turn):
        other = lax.rem(spot + turn, PLANE)
        return other, relay.device(z, (other // 2) % 2, other // 4, other % 2)

    def in_line(turn):
        other = lax.rem(z + turn, LINE)
        return other, relay.device(other, y, c, x)

    mine = [
        pltpu.make_async_copy(up_piece, vera.at[z, y, c, x, 1], local_sems.at[0]),
        pltpu.make_async_copy(attn_piece, square.at[z, y, c, x, pl.ds(0, 3)], local_sems.at[1]),
        pltpu.make_async_copy(out_piece, square.at[z, y, c, x, 3], local_sems.at[2]),
        pltpu.make_async_copy(branch_piece, branch_w.at[z, y, c, x], local_sems.at[3]),
        pltpu.make_async_copy(scale_d, scales.at[x], local_sems.at[4]),
        pltpu.make_async_copy(inner_piece, inner_t.at[z, y, c, x], local_sems.at[5]),
        pltpu.make_async_copy(down_piece, vera.at[z, y, c, x, 0], local_sems.at[6]),
    ]
    tokens_copy = pltpu.make_async_copy(tokens_in, tokens, local_sems.at[7])
    cotangent_copy = pltpu.make_async_copy(cotangent_in, cotangent, local_sems.at[8])
    for copy in mine + [tokens_copy, cotangent_copy]:
        copy.start()
    barrier = pltpu.get_barrier_semaphore()

    def greet(device):
        pl.semaphore_signal(barrier, 1, device_id=device, device_id_type=MESH_IDS)

    greet(relay.device(z, y, 1 - c, x))
    greet(relay.device(z, y, c, 1 - x))
    greet(relay.device(z, 1 - y, c, x))

    @pl.when(z < 3)
    def _():
        greet(relay.device(z + 1, y, c, x))

    @pl.when(z > 0)
    def _():
        greet(relay.device(z - 1, y, c, x))

    for copy in mine:
        copy.wait()
    pl.semaphore_wait(barrier, 3 + jnp.where(z < 3, 1, 0) + jnp.where(z > 0, 1, 0))

    scale_copy = pltpu.make_async_remote_copy(
        scales.at[x],
        scales.at[x],
        sum_sems.at[0],
        sum_sems.at[1],
        device_id=relay.device(z, y, c, 1 - x),
        device_id_type=MESH_IDS,
    )
    scale_copy.start()

    def segments(seq):
        row_place = lax.broadcasted_iota(jnp.int32, (256, 256), 0)
        col_place = lax.broadcasted_iota(jnp.int32, (256, 256), 1)
        row_label = jnp.zeros((256, 256), jnp.int32)
        col_label = jnp.zeros((256, 256), jnp.int32)
        end = jnp.int32(0)
        for k in range(seg_lengths.shape[1]):
            end = end + seg_lengths[seq, k]
            row_label = row_label + (row_place >= end).astype(jnp.int32)
            col_label = col_label + (col_place >= end).astype(jnp.int32)
        same[seq] = jnp.where(row_label == col_label, 0.0, neg_big)

    def row(ref, k):
        return ref[k : k + 1, :].astype(WIDE)

    def rows_of(i):
        return pl.ds(pl.multiple_of(i * 256, 256), 256)

    def down_t(h):
        return vera[:, :, :, h, 0].reshape(768, 512)

    def up(h):
        return vera[:, :, :, h, 1].reshape(768, 512)

    def weight(k):
        return square[:, :, :, :, k].reshape(768, 768)

    def steps_at(i, relays):
        for k, steps in relays.items():

            @pl.when(i == k)
            def _():
                for step in steps:
                    take_step(step)

    def adapters(i):
        rows = rows_of(i)
        token_rows = tokens[rows, :]
        parts_q, parts_v = [], []
        for h in range(2):
            lowrank = dot_nn(token_rows, down_t(h))
            low[rows, h * 512 : (h + 1) * 512] = lowrank
            parts_q.append(dot_nt((scales[h, 0:1, :].astype(WIDE) * lowrank).astype(NARROW), up(h)))
            parts_v.append(dot_nt((scales[h, 1:2, :].astype(WIDE) * lowrank).astype(NARROW), up(h)))
        extra_q[rows, :] = parts_q[0] + parts_q[1]
        extra_v[rows, :] = parts_v[0] + parts_v[1]

    def project_key():
        key[...] = dot_nn(tokens[...], weight(1)).astype(NARROW)

    def project_query():
        total = dot_nn(tokens[...], weight(0)) + row(lin_biases, 0) + row(scale_b, 0) * extra_q[...]
        query[...] = (total * HEAD ** (-0.5)).astype(NARROW)

    def project_value():
        total = dot_nn(tokens[...], weight(2)) + row(lin_biases, 1) + row(scale_b, 1) * extra_v[...]
        value[...] = total.astype(NARROW)

    def head_cols(j):
        return pl.ds(pl.multiple_of(j * 128, 128), 128)

    lane = lax.broadcasted_iota(jnp.int32, (256, 128), 1)
    first_half = lane < HEAD

    def attend_pair(it):
        seq, j = it // 6, lax.rem(it, 6)
        rows, cols = rows_of(seq), head_cols(j)
        q_pair, k_pair, v_pair = query[rows, cols], key[rows, cols], value[rows, cols]
        zero = jnp.zeros_like(q_pair)
        queries = jnp.concatenate([jnp.where(first_half, q_pair, zero), jnp.where(first_half, zero, q_pair)])
        both = dot_nt(queries, k_pair)
        parts = []
        for half in range(2):
            scores = both[half * 256 : (half + 1) * 256] + same[seq]
            peak = jnp.max(scores, axis=-1, keepdims=True)
            exponent = jnp.exp(scores - peak)
            total = jnp.sum(exponent, axis=-1, keepdims=True)
            soft = (exponent * (1.0 / total)).astype(NARROW)
            probs[it * 2 + half] = soft
            parts.append(soft)
        both = dot_nn(jnp.concatenate(parts), v_pair)
        context[rows, cols] = jnp.where(first_half, both[:256], both[256:]).astype(NARROW)

    def close_attention(i):
        rows = rows_of(i)
        attended = dot_nn(context[rows, :], weight(3)) + row(lin_biases, 2)
        normed, inverse = standardise(tokens[rows, :].astype(WIDE) + attended)
        normed_one[rows, :] = normed
        inverse_one[rows, :] = inverse
        scaled = normed * row(norm_gains, 0) + row(norm_biases, 0)
        narrow_one[rows, :] = scaled.astype(NARROW)
        resid[rows, :] = scaled + row(lin_biases, 3)

    def hidden_cols(plane):
        return pl.ds(pl.multiple_of(plane * 768, 768), 768)

    def inner_block(it):
        turn, i = it // 2, lax.rem(it, 2)
        plane = nearest(z, turn)
        rows, cols = rows_of(i), hidden_cols(plane)
        block = dot_nt(narrow_one[rows, :], inner_t[plane].reshape(768, 768))
        block = block + bias_row[0:1, cols]
        below = 0.5 + 0.5 * lax.erf(block * 0.7071067811865476)
        hidden[rows, cols] = (block * below).astype(NARROW)
        slope[rows, cols] = (below + block * jnp.exp(-0.5 * block * block) * 0.3989422804014327).astype(NARROW)

    def branch_block(turn):
        plane = nearest(z, turn)
        resid[...] += dot_nn(hidden[:, hidden_cols(plane)], branch_w[plane].reshape(768, 768))

    def attend(it):
        attend_pair(2 * it)
        attend_pair(2 * it + 1)

    bodies = {
        "adapters": (2, adapters),
        "project_key": (1, lambda i: project_key()),
        "project_query": (1, lambda i: project_query()),
        "project_value": (1, lambda i: project_value()),
        "attend": (3, lambda k: (attend(2 * k), attend(2 * k + 1))),
        "close": (2, close_attention),
        "inner": (8, inner_block),
        "branch": (4, branch_block),
    }

    def take_step(step):
        if step[0] == "scales":
            bias_row[...] = ffn_bias[...].astype(WIDE).reshape(1, -1)
            segments(0)
            segments(1)
            scale_copy.wait()
            tokens_copy.wait()
        else:
            gather(*step)

    at = 0
    while at < len(SCHEDULE):
        name = SCHEDULE[at][0]
        if name not in bodies:
            take_step(SCHEDULE[at])
            at += 1
            continue
        count, body = bodies[name]
        between = {}
        done = 0
        while done < count - 1:
            at += 1
            if SCHEDULE[at][0] == name:
                done += 1
            else:
                between.setdefault(done + 1, []).append(SCHEDULE[at])
        at += 1
        if count == 1:
            body(0)
        else:

            @pl.loop(0, count)
            def _(i):
                steps_at(i, between)
                body(i)

    cotangent_copy.wait()

    for i in range(2):
        rows = slice(i * 256, (i + 1) * 256)
        normed, inverse = standardise(resid[rows, :])
        gain = row(norm_gains, 1)
        out_stage[rows, :] = (normed * gain + row(norm_biases, 1)).astype(NARROW)
        grad = standardise_back(normed, inverse, cotangent[rows, :].astype(WIDE) * gain)
        resid[rows, :] = grad
        narrow_one[rows, :] = grad.astype(NARROW)

    out_copy = pltpu.make_async_copy(out_stage, output, local_sems.at[0])
    out_copy.start()

    for plane in range(4):
        cols = slice(plane * 768, (plane + 1) * 768)
        for i in range(2):
            rows = slice(i * 256, (i + 1) * 256)
            grad = dot_nt(narrow_one[rows, :], branch_w[plane].reshape(768, 768)).astype(NARROW)
            hidden[rows, cols] = (slope[rows, cols].astype(WIDE) * grad.astype(WIDE)).astype(NARROW)

    for i in range(2):
        rows = slice(i * 256, (i + 1) * 256)
        grad = resid[rows, :] + dot_nn(hidden[rows, :], inner_t[...].reshape(3072, 768))
        grad = standardise_back(normed_one[rows, :], inverse_one[rows, :], grad * row(norm_gains, 0))
        resid[rows, :] = grad
        narrow_one[rows, :] = dot_nt(grad.astype(NARROW), weight(3)).astype(NARROW)

    def attend_back(it):
        seq, j = it // 6, lax.rem(it, 6)
        rows, cols = rows_of(seq), head_cols(j)
        k_pair, v_pair, grad = key[rows, cols], value[rows, cols], narrow_one[rows, cols]
        product = (grad.astype(WIDE) * context[rows, cols].astype(WIDE)).astype(NARROW)
        zero = jnp.zeros_like(grad)
        left = jnp.concatenate([jnp.where(first_half, grad, zero), jnp.where(first_half, zero, grad)])
        sums = jnp.concatenate([jnp.where(first_half, -product, zero), jnp.where(first_half, zero, -product)])
        change = dot_nt(
            jnp.concatenate([left, sums], axis=1), jnp.concatenate([v_pair, jnp.ones_like(v_pair)], axis=1)
        )
        soft = [probs[it * 2 + half] for half in range(2)]
        grad_scores = [
            (soft[half].astype(WIDE) * change[half * 256 : (half + 1) * 256]).astype(NARROW) for half in range(2)
        ]
        grad_q = dot_nn(jnp.concatenate(grad_scores), k_pair)
        grad_v = dot_tn(jnp.concatenate(soft, axis=1), grad)
        for half in range(2):
            probs[it * 2 + half] = grad_scores[half]
        narrow_one[rows, cols] = (jnp.where(first_half, grad_q[:256], grad_q[256:]) * HEAD ** (-0.5)).astype(NARROW)
        value[rows, cols] = jnp.where(first_half, grad_v[:256], grad_v[256:]).astype(NARROW)

    def key_back(it):
        rows, cols = rows_of(it // 6), head_cols(lax.rem(it, 6))
        both = jnp.concatenate([probs[it * 2], probs[it * 2 + 1]], axis=1)
        grad_k = dot_tn(both, query[rows, cols])
        key[rows, cols] = jnp.where(first_half, grad_k[:256], grad_k[256:]).astype(NARROW)

    @pl.loop(0, 2)
    def _(it):
        for k in range(6):
            attend_back(6 * it + k)

    plane_sums[spot] = jnp.zeros((4, 1024), WIDE)
    low_grad = hidden

    for i in range(2):
        rows = slice(i * 256, (i + 1) * 256)
        grad_q, grad_v = narrow_one[rows, :].astype(WIDE), value[rows, :].astype(WIDE)
        plane_sums[spot, 2:3, 0:768] += jnp.sum(extra_q[rows, :] * grad_q, axis=0, keepdims=True)
        plane_sums[spot, 3:4, 0:768] += jnp.sum(extra_v[rows, :] * grad_v, axis=0, keepdims=True)
        grad_q = (row(scale_b, 0) * grad_q).astype(NARROW)
        grad_v = (row(scale_b, 1) * grad_v).astype(NARROW)
        for h in range(2):
            half = slice(h * 512, (h + 1) * 512)
            scaled_q, scaled_v = dot_nn(grad_q, up(h)), dot_nn(grad_v, up(h))
            plane_sums[spot, 0:1, half] += jnp.sum(low[rows, half] * scaled_q, axis=0, keepdims=True)
            plane_sums[spot, 1:2, half] += jnp.sum(low[rows, half] * scaled_v, axis=0, keepdims=True)
            total = scales[h, 0:1, :].astype(WIDE) * scaled_q + scales[h, 1:2, :].astype(WIDE) * scaled_v
            low_grad[rows, half] = total.astype(NARROW)

    def plane_copy(turn, slot):
        return pltpu.make_async_remote_copy(
            plane_sums.at[slot],
            plane_sums.at[slot],
            sum_sems.at[1 + turn],
            sum_sems.at[9 + slot],
            device_id=in_plane(turn)[1],
            device_id_type=MESH_IDS,
        )

    def line_copy(turn, slot):
        return pltpu.make_async_remote_copy(
            line_sums.at[slot],
            line_sums.at[slot],
            sum_sems.at[16 + turn],
            sum_sems.at[20 + slot],
            device_id=in_line(turn)[1],
            device_id_type=MESH_IDS,
        )

    def input_rows(i):
        rows = slice(i * 256, (i + 1) * 256)
        total = resid[rows, :] + dot_nt(narrow_one[rows, :], weight(0))
        total = total + dot_nt(key[rows, :], weight(1))
        total = total + dot_nt(value[rows, :], weight(2))
        for h in range(2):
            total = total + dot_nt(low_grad[rows, h * 512 : (h + 1) * 512], down_t(h))
        grad_stage[rows, :] = total.astype(NARROW)
        return pltpu.make_async_copy(grad_stage.at[rows, :], input_grad.at[rows, :], local_sems.at[1 + i])

    for turn in range(1, PLANE):
        plane_copy(turn, spot).start()

    for k in range(6):
        key_back(k)
    grad_copies = [input_rows(0)]
    grad_copies[0].start()
    for turn in range(1, PLANE):
        plane_copy(turn, in_plane(turn)[0]).wait_recv()
    total = plane_sums[0]
    for other in range(1, PLANE):
        total = total + plane_sums[other]
    line_sums[z] = total
    for turn in range(1, LINE):
        line_copy(turn, z).start()
    for k in range(6, 12):
        key_back(k)
    grad_copies.append(input_rows(1))
    grad_copies[1].start()
    for turn in range(1, LINE):
        line_copy(turn, in_line(turn)[0]).wait_recv()
    cols = pl.ds(pl.multiple_of(x * 512, 512), 512)
    total_d, total_b = line_sums[0, 0:2, cols], line_sums[0, 2:4, 0:768]
    for other in range(1, LINE):
        total_d = total_d + line_sums[other, 0:2, cols]
        total_b = total_b + line_sums[other, 2:4, 0:768]
    d_grad[...] = total_d * grad_scale
    b_grad[...] = total_b * grad_scale

    for turn in range(1, PLANE):
        plane_copy(turn, spot).wait_send()
    for turn in range(1, LINE):
        line_copy(turn, z).wait_send()
    for g in range(len(GROUPS)):
        gather("finish", g)
    out_copy.wait()
    for copy in grad_copies:
        copy.wait()


def settle_kernel(*refs):
    sources, targets, stages, sems = refs[:4], refs[4:8], refs[8:12], refs[12]
    halves = [(0, 0, 256), (0, 256, 256), (1, 0, 256), (1, 256, 256), (2, 0, 2), (3, 0, 2)]
    loads, stores = [], []
    for n, (k, start, size) in enumerate(halves):
        part = pl.ds(start, size)
        loads.append(pltpu.make_async_copy(sources[k].at[part], stages[k].at[part], sems.at[0, n]))
        stores.append(pltpu.make_async_copy(stages[k].at[part], targets[k].at[part], sems.at[1, n]))
    for load in loads:
        load.start()
    for load, store in zip(loads, stores):
        load.wait()
        store.start()
    for store in stores:
        store.wait()


def settle(results):
    anywhere = pl.BlockSpec(memory_space=pl.ANY)
    return pl.pallas_call(
        settle_kernel,
        out_shape=[jax.ShapeDtypeStruct(result.shape, result.dtype) for result in results],
        in_specs=[anywhere] * 4,
        out_specs=[anywhere] * 4,
        scratch_shapes=[pltpu.VMEM(result.shape, result.dtype) for result in results]
        + [pltpu.SemaphoreType.DMA((2, 6))],
    )(*results)


def fused_layer(
    tokens,
    cotangent,
    seg_lengths,
    attn_weights,
    out_weight,
    ffn_in,
    ffn_out,
    lin_biases,
    ffn_bias,
    norm_gains,
    norm_biases,
    shared_down,
    shared_up,
    scale_d,
    scale_b,
):
    rows, width = tokens.shape[0] * tokens.shape[1] * tokens.shape[2], tokens.shape[3]
    devices = lax.axis_size("dp") * lax.axis_size("rank")
    in_vmem, anywhere = pl.BlockSpec(memory_space=pltpu.VMEM), pl.BlockSpec(memory_space=pl.ANY)
    in_smem = pl.BlockSpec(memory_space=pltpu.SMEM)
    shapes = [(4, 2, 2, 2) + lead + (cols,) for lead, cols, _ in GROUPS]
    flat = (rows, width)
    scratch = [pltpu.VMEM(shape, NARROW) for shape in shapes] + [
        pltpu.VMEM((2, 2, 512), NARROW),
        pltpu.VMEM((2, 256, 256), WIDE),
        pltpu.VMEM((rows, 1024), WIDE),
        pltpu.VMEM(flat, WIDE),
        pltpu.VMEM(flat, WIDE),
        pltpu.VMEM(flat, NARROW),
        pltpu.VMEM(flat, NARROW),
        pltpu.VMEM(flat, NARROW),
        pltpu.VMEM((24, 256, 256), NARROW),
        pltpu.VMEM(flat, NARROW),
        pltpu.VMEM(flat, WIDE),
        pltpu.VMEM((rows, 1), WIDE),
        pltpu.VMEM(flat, WIDE),
        pltpu.VMEM(flat, NARROW),
        pltpu.VMEM((rows, 3072), NARROW),
        pltpu.VMEM((rows, 3072), NARROW),
        pltpu.VMEM(flat, NARROW),
        pltpu.VMEM(flat, NARROW),
        pltpu.VMEM((PLANE, 4, 1024), WIDE),
        pltpu.VMEM((LINE, 4, 1024), WIDE),
        pltpu.VMEM((1, 3072), WIDE),
        pltpu.VMEM(flat, NARROW),
        pltpu.VMEM(flat, NARROW),
        pltpu.SemaphoreType.DMA((len(GROUPS), 4)),
        pltpu.SemaphoreType.DMA((2, SEND_SLOTS - 4)),
        pltpu.SemaphoreType.DMA((len(GROUPS), RECV_SLOTS)),
        pltpu.SemaphoreType.DMA((9,)),
        pltpu.SemaphoreType.DMA((24,)),
    ]
    results = pl.pallas_call(
        functools.partial(layer_kernel, 1.0 / math.sqrt(rows * devices)),
        out_shape=(
            jax.ShapeDtypeStruct(flat, NARROW),
            jax.ShapeDtypeStruct(flat, NARROW),
            jax.ShapeDtypeStruct((2, 512), WIDE),
            jax.ShapeDtypeStruct((2, 768), WIDE),
        ),
        in_specs=[anywhere, anywhere, in_smem]
        + [anywhere] * 4
        + [in_vmem] * 4
        + [anywhere] * 3
        + [in_vmem],
        out_specs=(anywhere, anywhere, in_vmem, in_vmem),
        scratch_shapes=scratch,
        compiler_params=pltpu.CompilerParams(
            collective_id=0, has_side_effects=True, vmem_limit_bytes=61 << 20
        ),
    )(
        tokens.reshape(flat),
        cotangent.reshape(flat),
        seg_lengths.reshape(-1, seg_lengths.shape[-1]),
        attn_weights,
        out_weight,
        ffn_in.T,
        ffn_out,
        lin_biases,
        ffn_bias,
        norm_gains,
        norm_biases,
        shared_down.T,
        shared_up,
        scale_d,
        scale_b,
    )
    output, input_grad, d_grad, b_grad = settle(results)
    return output.reshape(tokens.shape), input_grad.reshape(tokens.shape), d_grad, b_grad


def gather_weights(attn_weights, out_weight, ffn_in, ffn_out, shared_down, shared_up):
    down_local = lax.all_gather(shared_down, "dp", axis=1, tiled=True)
    up_local = lax.all_gather(shared_up, "dp", axis=0, tiled=True)
    return (
        lax.all_gather(attn_weights, ("dp", "rank"), axis=1, tiled=True),
        lax.all_gather(out_weight, ("dp", "rank"), axis=0, tiled=True),
        lax.all_gather(ffn_in, ("dp", "rank"), axis=1, tiled=True),
        lax.all_gather(ffn_out, ("dp", "rank"), axis=0, tiled=True),
        lax.all_gather(down_local, "rank", axis=0, tiled=True),
        lax.all_gather(up_local, "rank", axis=1, tiled=True),
    )


def per_device(
    tokens,
    cotangent,
    seg_lengths,
    attn_weights,
    out_weight,
    ffn_in,
    ffn_out,
    lin_biases,
    ffn_bias,
    norm_gains,
    norm_biases,
    shared_down,
    shared_up,
    scale_d,
    scale_b,
):
    micro_count, seq_count, length_rows, model_width = tokens.shape
    head_count = model_width // HEAD
    out_shape = tokens.shape
    seq_count = micro_count * seq_count
    row_count = seq_count * length_rows
    head_shape = (seq_count, length_rows, head_count, HEAD)
    float_wide = jnp.float32
    narrow = jnp.bfloat16
    attn_full, output_full, inner_full, branch_full, down_use, up_use = gather_weights(
        attn_weights, out_weight, ffn_in, ffn_out, shared_down, shared_up
    )
    scales_use = lax.all_gather(scale_d, "rank", axis=1, tiled=True)
    rank_cols = scales_use.shape[1]
    sum_d = jnp.zeros((2, rank_cols), float_wide)
    sum_b = jnp.zeros((2, model_width), float_wide)
    outputs = []
    input_grads = []
    for micro_step in range(1):
        token_rows = tokens.reshape(row_count, model_width)
        same_segment = segment_match(seg_lengths.reshape(seq_count, -1), length_rows)
        lowrank = jnp.einsum("rd,kd->rk", token_rows, down_use, preferred_element_type=float_wide)
        scaled = (scales_use[:, None, :] * lowrank[None]).astype(narrow)
        adapted = jnp.concatenate(
            [
                jnp.einsum("rk,dk->rd", scaled[0], up_use, preferred_element_type=float_wide),
                jnp.einsum("rk,dk->rd", scaled[1], up_use, preferred_element_type=float_wide),
            ],
            axis=1,
        )
        extra_query = adapted[:, :model_width]
        extra_value = adapted[:, model_width:]
        query_rows = (
            jnp.dot(token_rows, attn_full[0], preferred_element_type=float_wide)
            + lin_biases[0]
            + scale_b[0] * extra_query
        ).astype(narrow)
        key_rows = jnp.dot(token_rows, attn_full[1], preferred_element_type=float_wide).astype(
            narrow
        )
        value_rows = (
            jnp.dot(token_rows, attn_full[2], preferred_element_type=float_wide)
            + lin_biases[1]
            + scale_b[1] * extra_value
        ).astype(narrow)
        query_heads = query_rows.reshape(head_shape)
        key_heads = key_rows.reshape(head_shape)
        value_heads = value_rows.reshape(head_shape)
        context, log_total = attend(query_heads, key_heads, value_heads, same_segment)
        attended = (
            jnp.dot(
                context.reshape(row_count, model_width),
                output_full,
                preferred_element_type=float_wide,
            )
            + lin_biases[2]
        )
        resid_one = token_rows.astype(float_wide) + attended
        normed_one = layer_norm(resid_one, norm_gains[0], norm_biases[0])
        inner_pre = (
            jnp.dot(normed_one.astype(narrow), inner_full, preferred_element_type=float_wide)
            + ffn_bias
        )
        hidden = gelu_exact(inner_pre).astype(narrow)
        branch = jnp.dot(hidden, branch_full, preferred_element_type=float_wide) + lin_biases[3]
        resid_two = normed_one + branch
        outputs.append(
            layer_norm(resid_two, norm_gains[1], norm_biases[1])
            .astype(narrow)
            .reshape(out_shape)
        )
        grad_out = cotangent.reshape(row_count, model_width).astype(float_wide)
        grad_two = norm_back(resid_two, norm_gains[1], norm_biases[1], grad_out)
        grad_hidden = jnp.einsum(
            "rd,fd->rf", grad_two.astype(narrow), branch_full, preferred_element_type=float_wide
        ).astype(narrow)
        grad_inner = gelu_back(inner_pre, grad_hidden.astype(float_wide)).astype(narrow)
        grad_normed = grad_two + jnp.einsum(
            "rf,df->rd", grad_inner, inner_full, preferred_element_type=float_wide
        )
        grad_one = norm_back(resid_one, norm_gains[0], norm_biases[0], grad_normed)
        grad_attended = grad_one.astype(narrow)
        grad_context = jnp.einsum(
            "ro,io->ri", grad_attended, output_full, preferred_element_type=float_wide
        ).astype(narrow)
        grad_query, grad_keys, grad_values = attend_back(
            query_heads,
            key_heads,
            value_heads,
            same_segment,
            log_total,
            grad_context.reshape(head_shape),
        )
        query_grad = grad_query.reshape(row_count, model_width).astype(narrow)
        key_grad = grad_keys.reshape(row_count, model_width).astype(narrow)
        value_grad = grad_values.reshape(row_count, model_width).astype(narrow)
        grad_input = grad_one + jnp.einsum(
            "ro,io->ri", query_grad, attn_full[0], preferred_element_type=float_wide
        )
        grad_input = grad_input + jnp.einsum(
            "ro,io->ri", key_grad, attn_full[1], preferred_element_type=float_wide
        )
        grad_input = grad_input + jnp.einsum(
            "ro,io->ri", value_grad, attn_full[2], preferred_element_type=float_wide
        )
        query_grad_wide = query_grad.astype(float_wide)
        value_grad_wide = value_grad.astype(float_wide)
        sum_b = sum_b + jnp.stack(
            [
                jnp.sum(extra_query * query_grad_wide, axis=0),
                jnp.sum(extra_value * value_grad_wide, axis=0),
            ]
        )
        grad_extra = jnp.concatenate(
            [
                (scale_b[0] * query_grad_wide).astype(narrow),
                (scale_b[1] * value_grad_wide).astype(narrow),
            ],
            axis=1,
        )
        grad_scaled = jnp.concatenate(
            [
                jnp.dot(grad_extra[:, :model_width], up_use, preferred_element_type=float_wide),
                jnp.dot(grad_extra[:, model_width:], up_use, preferred_element_type=float_wide),
            ],
            axis=1,
        )
        grad_scaled_query = grad_scaled[:, :rank_cols]
        grad_scaled_value = grad_scaled[:, rank_cols:]
        sum_d = sum_d + jnp.stack(
            [
                jnp.sum(lowrank * grad_scaled_query, axis=0),
                jnp.sum(lowrank * grad_scaled_value, axis=0),
            ]
        )
        grad_lowrank = (
            scales_use[0] * grad_scaled_query + scales_use[1] * grad_scaled_value
        ).astype(narrow)
        grad_from_adapter = jnp.dot(grad_lowrank, down_use, preferred_element_type=float_wide)
        input_grads.append(
            (grad_input + grad_from_adapter)
            .astype(narrow)
            .reshape(out_shape)
        )
    grad_scale = 1.0 / math.sqrt(
        row_count * lax.axis_size("dp") * lax.axis_size("rank")
    )
    total_d, total_b = lax.psum((sum_d, sum_b), ("dp", "rank"))
    local_cols = scale_d.shape[1]
    total_d = lax.dynamic_slice_in_dim(total_d, lax.axis_index("rank") * local_cols, local_cols, 1)
    return (outputs[0], input_grads[0], total_d * grad_scale, total_b * grad_scale)


def solution(mesh):
    return jax.shard_map(
        fused_layer if (mesh.shape["dp"], mesh.shape["rank"]) == (16, 2) else per_device,
        mesh=mesh,
        in_specs=(
            P(None, ("dp", "rank"), None, None),
            P(None, ("dp", "rank"), None, None),
            P(None, ("dp", "rank"), None),
            P(None, ("dp", "rank"), None),
            P(("dp", "rank"), None),
            P(None, ("dp", "rank")),
            P(("dp", "rank"), None),
            P(),
            P(),
            P(),
            P(),
            P("rank", "dp"),
            P("dp", "rank"),
            P(None, "rank"),
            P(),
        ),
        out_specs=(
            P(None, ("dp", "rank"), None, None),
            P(None, ("dp", "rank"), None, None),
            P(None, "rank"),
            P(),
        ),
        check_vma=False,
    )
```
